256 devices in a mesh: ctx: 16 (over z, core), dp: 16 (over y, x).
Axes of the slice: x: 4, y: 4, z: 8, core: 2. Of those that a mesh axis runs over, the one named last changes fastest.
Arguments:
- queries: bfloat16 [16, 2048, 4096], P('dp', 'ctx'), may hold values from -48 to 48
- grad_out: bfloat16 [16, 2048, 4096], P('dp', 'ctx'), may hold values from -48 to 48
- neighbour_keys: bfloat16 [64, 128, 4096], P('dp', None, 'ctx'), may hold values from -6 to 6
- neighbour_values: bfloat16 [64, 128, 4096], P('dp', None, 'ctx'), may hold values from -6 to 6
- distinct_ids: int32 [16, 16], replicated, may hold values from 0 to 63, as said below
- group_refs: int32 [16, 32, 2], replicated, may hold values from 0 to 15, as said below
Outputs:
- grad_queries: bfloat16 [16, 2048, 4096], P('dp', 'ctx')
- grad_keys: bfloat16 [64, 128, 4096], P('dp', None, 'ctx')
- grad_values: bfloat16 [64, 128, 4096], P('dp', None, 'ctx')
The draws below stay inside these ranges and needn't reach their ends.
Inputs may be any that keep to these rules, and one draw needn't show every extreme that they name: `distinct_ids`: each row lists 16 different neighbours. Neighbour n is owned by data replica n // 4. No owner holds more than 2 of one row's neighbours, and one owner, the same for every row, holds exactly 2 in every row. `group_refs`: every position of a replica's row of distinct_ids occurs in that replica's entries.
All inputs are finite; a program needn't handle non-finite values.
Results may differ from the reference program's by a relative error of at most 0.0075.
Values may be sent and summed in bfloat16 or wider, within the bound.
No kernel may reach another device: no remote copies, remote signals or barrier semaphores. Data moves between devices by JAX's collectives and lax.ppermute only.
A program may use at most 128 MiB of HBM per device.

```python
import math
import jax
import jax.numpy as jnp
from jax import lax

H = 32
DH = 128
GROUP = 64
NBR_LEN = 128
NEIGHBOURS = 2
GROUPS = 32
SEQ = 2048
SLOTS = 64
DIST = 16
CAP = 2
NB_OWN = 4
NB_POOL = 64
REPLICAS = 16
HD = 4096


def draw_queries(key, part):
    gaussian = jax.random.truncated_normal(jax.random.fold_in(key, 11), -6.0, 6.0, (REPLICAS, SEQ, HD), jnp.float32)
    return gaussian.astype(jnp.bfloat16)


def draw_neighbour_keys(key, part):
    gaussian = jax.random.truncated_normal(jax.random.fold_in(key, 13), -6.0, 6.0, (NB_POOL, NBR_LEN, HD), jnp.float32)
    return gaussian.astype(jnp.bfloat16)


def replica_lists(key):
    base_key = jax.random.fold_in(key, 401)
    hottest = jax.random.randint(jax.random.fold_in(base_key, 1), (), 0, REPLICAS)

    def single_replica(replica):
        replica_key = jax.random.fold_in(base_key, replica + 2)
        subkeys = jax.random.split(replica_key, 5)
        others = (hottest + 1 + jnp.arange((REPLICAS - 1) * CAP) // CAP) % REPLICAS
        picked = jax.random.permutation(subkeys[0], others)[:DIST - CAP]
        owners = jnp.concatenate([jnp.full((CAP,), hottest, jnp.int32), picked.astype(jnp.int32)])
        owners = jax.random.permutation(subkeys[1], owners)
        marked = (owners[:, None] == jnp.arange(REPLICAS)[None, :]).astype(jnp.int32)
        ranking = jnp.sum(jnp.cumsum(marked, axis=0) * marked, axis=1) - 1
        orders = jax.vmap(lambda subkey: jax.random.permutation(subkey, NB_OWN))(jax.random.split(subkeys[2], REPLICAS))
        local_index = orders[owners, ranking]
        neighbour_list = owners * NB_OWN + local_index
        extras = jax.random.randint(subkeys[3], (SLOTS - DIST,), 0, DIST)
        slot_refs = jax.random.permutation(subkeys[4], jnp.concatenate([jnp.arange(DIST), extras]))
        return (neighbour_list.astype(jnp.int32), slot_refs.reshape(GROUPS, NEIGHBOURS).astype(jnp.int32))
    return jax.vmap(single_replica)(jnp.arange(REPLICAS))


def draw_distinct_ids(key, part):
    return replica_lists(key)[0]


def draw_group_refs(key, part):
    return replica_lists(key)[1]


def shard_levels(own_key, extent, shards, least, high):
    loudness, own = 1.0, jax.random.fold_in(own_key, 6)
    for dim, blocks in shards:
        draws = jnp.exp(jax.random.uniform(jax.random.fold_in(own, dim), (blocks,), jnp.float32, least / len(shards), high / len(shards)))
        loudness = loudness * jnp.repeat(draws, extent[dim] // blocks).reshape([-1 if axis == dim else 1 for axis in range(len(extent))])
    return loudness


def scatter_about(own_key, extent, spread, bound, cuts=(), held_as=jnp.bfloat16):
    array = spread * jax.random.normal(own_key, extent, jnp.float32)
    if cuts:
        array = array * shard_levels(own_key, extent, cuts, -0.22, 0.18)
    return jnp.clip(array, -bound, bound).astype(held_as)


def setup_inputs(seed: int = 0) -> dict:
    arg_keys = jax.random.split(jax.random.key(seed), 7)
    queries = draw_queries(jax.random.fold_in(arg_keys[6], 71), 0)
    grad_out = scatter_about(arg_keys[1], (REPLICAS, SEQ, HD), 8.0, 48.0, ((0, 16), (1, 16)))
    neighbour_keys = draw_neighbour_keys(jax.random.fold_in(arg_keys[6], 71), 0)
    neighbour_values = scatter_about(arg_keys[3], (NB_POOL, NBR_LEN, HD), 1.0, 6.0, ((0, 16), (2, 16)))
    distinct_ids = draw_distinct_ids(jax.random.fold_in(arg_keys[6], 71), 0)
    group_refs = draw_group_refs(jax.random.fold_in(arg_keys[6], 71), 0)
    return {"queries": queries, "grad_out": grad_out, "neighbour_keys": neighbour_keys, "neighbour_values": neighbour_values, "distinct_ids": distinct_ids, "group_refs": group_refs}


def shifted_blocks(token_rows):
    padding = jnp.zeros((GROUP - 1, token_rows.shape[1]), token_rows.dtype)
    joined = jnp.concatenate([token_rows[GROUP - 1:], padding], axis=0)
    return joined.reshape(GROUPS, GROUP, H, DH)

def rounded(values):
    return lax.optimization_barrier(values.astype(jnp.bfloat16)).astype(jnp.float32)

def reference(queries, grad_out, neighbour_keys, neighbour_values, distinct_ids, group_refs):
    score_scale = 1.0 / math.sqrt(DH)
    start_keys = jnp.zeros((NB_POOL, NBR_LEN, HD), jnp.float32)
    start_values = jnp.zeros((NB_POOL, NBR_LEN, HD), jnp.float32)

    def replica_step(running, inputs):
        total_keys, total_values = running
        query_rows, grad_rows, neighbour_list, slot_refs = inputs
        flat_refs = slot_refs.reshape(-1).astype(jnp.int32)
        slot_ids = neighbour_list[flat_refs].astype(jnp.int32)
        keys_all = neighbour_keys[slot_ids].astype(jnp.float32).reshape(GROUPS, NEIGHBOURS * NBR_LEN, H, DH)
        values_all = neighbour_values[slot_ids].astype(jnp.float32).reshape(GROUPS, NEIGHBOURS * NBR_LEN, H, DH)
        query_blocks = shifted_blocks(query_rows).astype(jnp.float32)
        grad_blocks = shifted_blocks(grad_rows).astype(jnp.float32)
        scores = jnp.einsum('cqhd,ckhd->chqk', query_blocks, keys_all) * score_scale
        totals = jax.nn.logsumexp(scores, axis=-1, keepdims=True)
        attention = jnp.exp(scores - totals)
        grad_attention = jnp.einsum('cqhd,ckhd->chqk', grad_blocks, values_all)
        row_dots = lax.optimization_barrier(jnp.sum(attention * grad_attention, axis=-1, keepdims=True))
        grad_scores = attention * (grad_attention - row_dots)
        attention_low = rounded(attention)
        grad_low = rounded(grad_scores)
        grad_query_blocks = jnp.einsum('chqk,ckhd->cqhd', grad_low, keys_all) * score_scale
        key_slots = jnp.einsum('chqk,cqhd->ckhd', grad_low, query_blocks) * score_scale
        value_slots = jnp.einsum('chqk,cqhd->ckhd', attention_low, grad_blocks)
        flat_query = grad_query_blocks.reshape(SEQ, HD)
        grad_tokens = jnp.concatenate([jnp.zeros((GROUP - 1, HD), jnp.float32), flat_query[:SEQ - GROUP + 1]], axis=0).astype(jnp.bfloat16)
        selector = (flat_refs[None, :] == jnp.arange(DIST, dtype=jnp.int32)[:, None]).astype(jnp.float32)
        key_terms = jnp.dot(selector, key_slots.reshape(SLOTS, NBR_LEN * HD), precision=lax.Precision.HIGHEST)
        value_terms = jnp.dot(selector, value_slots.reshape(SLOTS, NBR_LEN * HD), precision=lax.Precision.HIGHEST)
        key_terms = rounded(key_terms).reshape(DIST, NBR_LEN, HD)
        value_terms = rounded(value_terms).reshape(DIST, NBR_LEN, HD)
        total_keys = total_keys.at[neighbour_list.astype(jnp.int32)].add(key_terms)
        total_values = total_values.at[neighbour_list.astype(jnp.int32)].add(value_terms)
        return ((total_keys, total_values), grad_tokens)
    (total_keys, total_values), grad_queries = lax.scan(replica_step, (start_keys, start_values), (queries, grad_out, distinct_ids, group_refs))
    return (grad_queries, total_keys.astype(jnp.bfloat16), total_values.astype(jnp.bfloat16))
```

```python
import functools
import math

import jax
import jax.numpy as jnp
from jax import lax
from jax.experimental import pallas as pl
from jax.experimental.pallas import tpu as pltpu
from jax.sharding import PartitionSpec as P

DH = 128
GROUP = 64
BF16 = jnp.bfloat16
F32 = jnp.float32
HBM = pl.BlockSpec(memory_space=pl.ANY)
VMEM = pl.BlockSpec(memory_space=pltpu.VMEM)
SMEM = pl.BlockSpec(memory_space=pltpu.SMEM)


def owner_tables(distinct_ids, owned_count, capacity, replicas):
    owners = distinct_ids // owned_count
    local_index = distinct_ids % owned_count
    marked = (owners[:, :, None] == jnp.arange(replicas)[None, None, :]).astype(jnp.int32)
    ranking = jnp.sum(jnp.cumsum(marked, axis=1) * marked, axis=2) - 1
    return (owners, local_index, ranking)


def pack_heads_body(parts, width, q_ref, g_ref, out_ref, sems):
    copies = []
    for j in range(parts):
        for i, ref in enumerate((q_ref, g_ref)):
            copy = pltpu.make_async_copy(
                ref.at[:, pl.ds(j * width, width)], out_ref.at[j, i], sems.at[j, i]
            )
            copy.start()
            copies.append(copy)
    for copy in copies:
        copy.wait()


def pack_heads(queries, grad_out, parts):
    tokens, features = queries.shape
    width = features // parts
    return pl.pallas_call(
        functools.partial(pack_heads_body, parts, width),
        out_shape=jax.ShapeDtypeStruct((parts, 2, tokens, width), BF16),
        in_specs=[HBM, HBM],
        out_specs=HBM,
        scratch_shapes=[pltpu.SemaphoreType.DMA((parts, 2))],
    )(queries, grad_out)


def join_heads_body(parts, width, in_ref, out_ref, sems):
    copies = []
    for j in range(parts):
        copy = pltpu.make_async_copy(
            in_ref.at[j], out_ref.at[:, pl.ds(j * width, width)], sems.at[j]
        )
        copy.start()
        copies.append(copy)
    for copy in copies:
        copy.wait()


def join_heads(blocks):
    parts, tokens, width = blocks.shape
    return pl.pallas_call(
        functools.partial(join_heads_body, parts, width),
        out_shape=jax.ShapeDtypeStruct((tokens, parts * width), BF16),
        in_specs=[HBM],
        out_specs=HBM,
        scratch_shapes=[pltpu.SemaphoreType.DMA((parts,))],
    )(blocks)


def matmul(a, b, contract):
    return lax.dot_general(a, b, ((contract[:1], contract[1:]), ((), ())), preferred_element_type=F32)


def block_diagonal(rows):
    zero = jnp.zeros((rows.shape[0], DH), BF16)
    return jnp.concatenate(
        [
            jnp.concatenate([rows[:, :DH], zero], axis=1),
            jnp.concatenate([zero, rows[:, DH:]], axis=1),
        ],
        axis=0,
    )


def attend_body(
    groups, distinct, unroll, refs_ref, rows_ref, tokens_ref, pool_ref, gq_ref, send_ref,
    keys, values, key_sum, value_sum, query_last, grad_last, held, sems,
):
    scale = 1.0 / math.sqrt(DH)
    owned = pool_ref.shape[0] // (tokens_ref.shape[0] * 2)
    copies = []
    for j in range(distinct):
        for i, ref in enumerate((keys, values)):
            copies.append(
                pltpu.make_async_copy(pool_ref.at[rows_ref[0, j] + i * owned], ref.at[j], sems.at[j, i])
            )
    for copy in copies:
        copy.start()
    key_sum[...] = jnp.zeros_like(key_sum)
    value_sum[...] = jnp.zeros_like(value_sum)
    send_ref[...] = jnp.zeros_like(send_ref)
    width = gq_ref.shape[2]
    row = lax.broadcasted_iota(jnp.int32, (GROUP, width), 0)

    def rolled(kind, block):
        part = tokens_ref[block // 2, kind, pl.ds((block % 2) * GROUP, GROUP), :]
        return pltpu.roll(part.astype(F32), 1, 0)

    held[...] = jnp.zeros_like(held)
    query_last[...] = rolled(0, 0)
    grad_last[...] = rolled(1, 0)
    for copy in copies:
        copy.wait()

    def shifted(kind, group, last):
        following = rolled(kind, jnp.minimum(group + 1, groups - 1))
        following = jnp.where(group + 1 < groups, following, 0.0)
        block = jnp.where(row == 0, last[...], following)
        last[...] = following
        return block_diagonal(block.astype(BF16))

    def step(group):
        query = shifted(0, group, query_last)
        grad = shifted(1, group, grad_last)
        pair = (refs_ref[0, 2 * group], refs_ref[0, 2 * group + 1])
        block_keys = [keys[j] for j in pair]
        scores = [matmul(k, query, (1, 1)) for k in block_keys]
        grads = [matmul(values[j], grad, (1, 1)) for j in pair]
        top = jnp.maximum(*[jnp.max(s, axis=0, keepdims=True) for s in scores])
        weights = [jnp.exp((s - top) * scale) for s in scores]
        total = sum(jnp.sum(w, axis=0, keepdims=True) for w in weights)
        inverse = 1.0 / total
        weights = [w * inverse for w in weights]
        dots = sum(jnp.sum(w * g, axis=0, keepdims=True) for w, g in zip(weights, grads))
        grad_low = [(w * (g - dots)).astype(BF16) for w, g in zip(weights, grads)]
        weights_low = [w.astype(BF16) for w in weights]
        for j, w, g in zip(pair, weights_low, grad_low):
            value_sum[j] += matmul(w, grad, (1, 0))
            key_sum[j] += matmul(g, query, (1, 0))
        both = sum(matmul(g, k, (0, 0)) for g, k in zip(grad_low, block_keys)) * scale
        back = jnp.concatenate([both[:GROUP, :DH], both[GROUP:, DH:]], axis=1)
        back = pltpu.roll(back, GROUP - 1, 0)
        gq_ref[group // 2, pl.ds((group % 2) * GROUP, GROUP), :] = jnp.where(
            row == GROUP - 1, back, held[...]
        ).astype(BF16)
        held[...] = back

    def steps(index, carry):
        for u in range(unroll):
            step(index * unroll + u)
        return carry

    lax.fori_loop(0, groups // unroll, steps, 0)
    for j in range(distinct):
        send_ref[rows_ref[1, j]] = (key_sum[j] * scale).astype(BF16)
        send_ref[rows_ref[1, j] + rows_ref[2, 0]] = value_sum[j].astype(BF16)


def attend(slots, rows, tokens, pool, groups, distinct, send_rows):
    parts, _, part_tokens, width = tokens.shape
    nbr = pool.shape[1]
    return pl.pallas_call(
        functools.partial(attend_body, groups, distinct, 2),
        out_shape=(
            jax.ShapeDtypeStruct((parts, part_tokens, width), BF16),
            jax.ShapeDtypeStruct((send_rows, nbr, width), BF16),
        ),
        in_specs=[SMEM, SMEM, VMEM, HBM],
        out_specs=(VMEM, VMEM),
        scratch_shapes=[
            pltpu.VMEM((distinct, nbr, width), BF16),
            pltpu.VMEM((distinct, nbr, width), BF16),
            pltpu.VMEM((distinct, nbr, width), F32),
            pltpu.VMEM((distinct, nbr, width), F32),
            pltpu.VMEM((GROUP, width), F32),
            pltpu.VMEM((GROUP, width), F32),
            pltpu.VMEM((GROUP, width), F32),
            pltpu.SemaphoreType.DMA((distinct, 2)),
        ],
        compiler_params=pltpu.CompilerParams(vmem_limit_bytes=48 * 1024 * 1024),
    )(slots, rows, tokens, pool)


def collect_body(senders, capacity, local_ref, valid_ref, in_ref, keys_ref, values_ref, sums):
    sums[...] = jnp.zeros_like(sums)

    def step(r, carry):
        for k in range(capacity):
            slot = r * capacity + k

            @pl.when(valid_ref[0, slot] > 0)
            def _():
                n = local_ref[0, slot]
                sums[0, n] += in_ref[r, k].astype(F32)
                sums[1, n] += in_ref[r, capacity + k].astype(F32)

        return carry

    lax.fori_loop(0, senders, step, 0)
    keys_ref[...] = sums[0].astype(BF16)
    values_ref[...] = sums[1].astype(BF16)


def collect(local, valid, arrived, owned):
    senders, twice, nbr, width = arrived.shape
    out = jax.ShapeDtypeStruct((owned, nbr, width), BF16)
    return pl.pallas_call(
        functools.partial(collect_body, senders, twice // 2),
        out_shape=(out, out),
        in_specs=[SMEM, SMEM, VMEM],
        out_specs=(VMEM, VMEM),
        scratch_shapes=[pltpu.VMEM((2, owned, nbr, width), F32)],
        compiler_params=pltpu.CompilerParams(vmem_limit_bytes=32 * 1024 * 1024),
    )(local[None], valid[None], arrived)


def on_device(queries, grad_out, neighbour_keys, neighbour_values, distinct_ids, group_refs):
    replicas = lax.axis_size("dp")
    parts = lax.axis_size("ctx")
    me = lax.axis_index("dp")
    owned, nbr, width = neighbour_keys.shape
    capacity = owned // 2
    distinct = distinct_ids.shape[1]
    groups = group_refs.shape[1]
    owners, local_index, ranking = owner_tables(distinct_ids, owned, capacity, replicas)
    pick = lambda table: lax.dynamic_index_in_dim(table, me, 0, keepdims=False)
    slots = pick(group_refs).reshape(1, -1)
    pool_row = pick(owners) * 2 * owned + pick(local_index)
    send_row = pick(owners) * 2 * capacity + pick(ranking)
    rows = jnp.stack([pool_row, send_row, jnp.full_like(send_row, capacity)])
    matches = (
        (owners[:, :, None] == me)
        & (ranking[:, :, None] == jnp.arange(capacity)[None, None, :])
    ).astype(jnp.int32)
    arrive_local = jnp.sum(matches * local_index[:, :, None], axis=1).reshape(-1)
    arrive_valid = jnp.sum(matches, axis=1).reshape(-1)

    pool = lax.all_gather(
        jnp.concatenate([neighbour_keys, neighbour_values], axis=0), "dp", axis=0, tiled=True
    )
    packed = pack_heads(queries[0], grad_out[0], parts)
    tokens = lax.all_to_all(packed, "ctx", split_axis=0, concat_axis=0, tiled=True)
    back, send = attend(slots, rows, tokens, pool, groups, distinct, replicas * 2 * capacity)
    back = lax.all_to_all(back, "ctx", split_axis=0, concat_axis=0, tiled=True)
    arrived = lax.all_to_all(
        send.reshape(replicas, 2 * capacity, nbr, width), "dp", split_axis=0, concat_axis=0, tiled=True
    )
    grad_keys, grad_values = collect(arrive_local, arrive_valid, arrived, owned)
    return (join_heads(back)[None], grad_keys, grad_values)


def solution(mesh):
    return jax.shard_map(
        on_device,
        mesh=mesh,
        in_specs=(
            P("dp", "ctx", None),
            P("dp", "ctx", None),
            P("dp", None, "ctx"),
            P("dp", None, "ctx"),
            P(),
            P(),
        ),
        out_specs=(P("dp", "ctx", None), P("dp", None, "ctx"), P("dp", None, "ctx")),
        check_vma=False,
    )
```

```python
import functools
import math

import jax
import jax.numpy as jnp
from jax import lax
from jax.experimental import pallas as pl
from jax.experimental.pallas import tpu as pltpu
from jax.sharding import PartitionSpec as P

DH = 128
GROUP = 64
BF16 = jnp.bfloat16
F32 = jnp.float32
HBM = pl.BlockSpec(memory_space=pl.ANY)
VMEM = pl.BlockSpec(memory_space=pltpu.VMEM)
SMEM = pl.BlockSpec(memory_space=pltpu.SMEM)


def owner_tables(distinct_ids, owned_count, capacity, replicas):
    owners = distinct_ids // owned_count
    local_index = distinct_ids % owned_count
    marked = (owners[:, :, None] == jnp.arange(replicas)[None, None, :]).astype(jnp.int32)
    ranking = jnp.sum(jnp.cumsum(marked, axis=1) * marked, axis=2) - 1
    return (owners, local_index, ranking)


def pack_heads_body(width, q_ref, g_ref, out_ref):
    for j in range(out_ref.shape[0]):
        out_ref[j, 0] = q_ref[:, j * width : (j + 1) * width]
        out_ref[j, 1] = g_ref[:, j * width : (j + 1) * width]


def pack_heads(queries, grad_out, parts):
    tokens, features = queries.shape
    width = features // parts
    steps = 4
    per_step = parts // steps
    block = pl.BlockSpec((tokens, per_step * width), lambda i: (0, i))
    return pl.pallas_call(
        functools.partial(pack_heads_body, width),
        grid=(steps,),
        out_shape=jax.ShapeDtypeStruct((parts, 2, tokens, width), BF16),
        in_specs=[block, block],
        out_specs=pl.BlockSpec((per_step, 2, tokens, width), lambda i: (i, 0, 0, 0)),
    )(queries, grad_out)


def join_heads_body(width, in_ref, out_ref):
    for j in range(in_ref.shape[0]):
        out_ref[:, j * width : (j + 1) * width] = in_ref[j]


def join_heads(blocks):
    parts, tokens, width = blocks.shape
    steps = 4
    per_step = parts // steps
    return pl.pallas_call(
        functools.partial(join_heads_body, width),
        grid=(steps,),
        out_shape=jax.ShapeDtypeStruct((tokens, parts * width), BF16),
        in_specs=[pl.BlockSpec((per_step, tokens, width), lambda i: (i, 0, 0))],
        out_specs=pl.BlockSpec((tokens, per_step * width), lambda i: (0, i)),
    )(blocks)


def matmul(a, b, contract):
    return lax.dot_general(a, b, ((contract[:1], contract[1:]), ((), ())), preferred_element_type=F32)


def block_diagonal(rows):
    zero = jnp.zeros((rows.shape[0], DH), BF16)
    return jnp.concatenate(
        [
            jnp.concatenate([rows[:, :DH], zero], axis=1),
            jnp.concatenate([zero, rows[:, DH:]], axis=1),
        ],
        axis=0,
    )


def attend_body(
    groups, distinct, unroll, refs_ref, rows_ref, tokens_ref, pool_ref, gq_ref, send_ref,
    keys, values, key_sum, value_sum, query_last, grad_last, held, sems,
):
    scale = 1.0 / math.sqrt(DH)
    owned = pool_ref.shape[0] // (tokens_ref.shape[0] * 2)
    copies = []
    for j in range(distinct):
        for i, ref in enumerate((keys, values)):
            copies.append(
                pltpu.make_async_copy(pool_ref.at[rows_ref[0, j] + i * owned], ref.at[j], sems.at[j, i])
            )
    for copy in copies:
        copy.start()
    key_sum[...] = jnp.zeros_like(key_sum)
    value_sum[...] = jnp.zeros_like(value_sum)
    send_ref[...] = jnp.zeros_like(send_ref)
    width = gq_ref.shape[2]
    row = lax.broadcasted_iota(jnp.int32, (GROUP, width), 0)

    def rolled(kind, block):
        part = tokens_ref[block // 2, kind, pl.ds((block % 2) * GROUP, GROUP), :]
        return pltpu.roll(part.astype(F32), 1, 0)

    held[...] = jnp.zeros_like(held)
    query_last[...] = rolled(0, 0)
    grad_last[...] = rolled(1, 0)
    for copy in copies:
        copy.wait()

    def shifted(kind, group, last):
        following = rolled(kind, jnp.minimum(group + 1, groups - 1))
        following = jnp.where(group + 1 < groups, following, 0.0)
        block = jnp.where(row == 0, last[...], following)
        last[...] = following
        return block_diagonal(block.astype(BF16))

    def step(group):
        query = shifted(0, group, query_last)
        grad = shifted(1, group, grad_last)
        pair = (refs_ref[0, 2 * group], refs_ref[0, 2 * group + 1])
        block_keys = [keys[j] for j in pair]
        scores = [matmul(k, query, (1, 1)) for k in block_keys]
        grads = [matmul(values[j], grad, (1, 1)) for j in pair]
        top = jnp.maximum(*[jnp.max(s, axis=0, keepdims=True) for s in scores])
        weights = [jnp.exp((s - top) * scale) for s in scores]
        total = sum(jnp.sum(w, axis=0, keepdims=True) for w in weights)
        inverse = 1.0 / total
        weights = [w * inverse for w in weights]
        dots = sum(jnp.sum(w * g, axis=0, keepdims=True) for w, g in zip(weights, grads))
        grad_low = [(w * (g - dots)).astype(BF16) for w, g in zip(weights, grads)]
        weights_low = [w.astype(BF16) for w in weights]
        for j, w, g in zip(pair, weights_low, grad_low):
            value_sum[j] += matmul(w, grad, (1, 0))
            key_sum[j] += matmul(g, query, (1, 0))
        both = sum(matmul(g, k, (0, 0)) for g, k in zip(grad_low, block_keys)) * scale
        back = jnp.concatenate([both[:GROUP, :DH], both[GROUP:, DH:]], axis=1)
        back = pltpu.roll(back, GROUP - 1, 0)
        gq_ref[group // 2, pl.ds((group % 2) * GROUP, GROUP), :] = jnp.where(
            row == GROUP - 1, back, held[...]
        ).astype(BF16)
        held[...] = back

    def steps(index, carry):
        for u in range(unroll):
            step(index * unroll + u)
        return carry

    lax.fori_loop(0, groups // unroll, steps, 0)
    for j in range(distinct):
        send_ref[rows_ref[1, j]] = (key_sum[j] * scale).astype(BF16)
        send_ref[rows_ref[1, j] + rows_ref[2, 0]] = value_sum[j].astype(BF16)


def attend(slots, rows, tokens, pool, groups, distinct, send_rows):
    parts, _, part_tokens, width = tokens.shape
    nbr = pool.shape[1]
    return pl.pallas_call(
        functools.partial(attend_body, groups, distinct, 2),
        out_shape=(
            jax.ShapeDtypeStruct((parts, part_tokens, width), BF16),
            jax.ShapeDtypeStruct((send_rows, nbr, width), BF16),
        ),
        in_specs=[SMEM, SMEM, VMEM, HBM],
        out_specs=(VMEM, VMEM),
        scratch_shapes=[
            pltpu.VMEM((distinct, nbr, width), BF16),
            pltpu.VMEM((distinct, nbr, width), BF16),
            pltpu.VMEM((distinct, nbr, width), F32),
            pltpu.VMEM((distinct, nbr, width), F32),
            pltpu.VMEM((GROUP, width), F32),
            pltpu.VMEM((GROUP, width), F32),
            pltpu.VMEM((GROUP, width), F32),
            pltpu.SemaphoreType.DMA((distinct, 2)),
        ],
        compiler_params=pltpu.CompilerParams(vmem_limit_bytes=48 * 1024 * 1024),
    )(slots, rows, tokens, pool)


def collect_body(senders, capacity, local_ref, valid_ref, in_ref, keys_ref, values_ref, sums):
    sums[...] = jnp.zeros_like(sums)

    def step(r, carry):
        for k in range(capacity):
            slot = r * capacity + k

            @pl.when(valid_ref[0, slot] > 0)
            def _():
                n = local_ref[0, slot]
                sums[0, n] += in_ref[r, k].astype(F32)
                sums[1, n] += in_ref[r, capacity + k].astype(F32)

        return carry

    lax.fori_loop(0, senders, step, 0)
    keys_ref[...] = sums[0].astype(BF16)
    values_ref[...] = sums[1].astype(BF16)


def collect(local, valid, arrived, owned):
    senders, twice, nbr, width = arrived.shape
    out = jax.ShapeDtypeStruct((owned, nbr, width), BF16)
    return pl.pallas_call(
        functools.partial(collect_body, senders, twice // 2),
        out_shape=(out, out),
        in_specs=[SMEM, SMEM, VMEM],
        out_specs=(VMEM, VMEM),
        scratch_shapes=[pltpu.VMEM((2, owned, nbr, width), F32)],
        compiler_params=pltpu.CompilerParams(vmem_limit_bytes=32 * 1024 * 1024),
    )(local[None], valid[None], arrived)


def on_device(queries, grad_out, neighbour_keys, neighbour_values, distinct_ids, group_refs):
    replicas = lax.axis_size("dp")
    parts = lax.axis_size("ctx")
    me = lax.axis_index("dp")
    owned, nbr, width = neighbour_keys.shape
    capacity = owned // 2
    distinct = distinct_ids.shape[1]
    groups = group_refs.shape[1]
    owners, local_index, ranking = owner_tables(distinct_ids, owned, capacity, replicas)
    pick = lambda table: lax.dynamic_index_in_dim(table, me, 0, keepdims=False)
    slots = pick(group_refs).reshape(1, -1)
    pool_row = pick(owners) * 2 * owned + pick(local_index)
    send_row = pick(owners) * 2 * capacity + pick(ranking)
    rows = jnp.stack([pool_row, send_row, jnp.full_like(send_row, capacity)])
    matches = (
        (owners[:, :, None] == me)
        & (ranking[:, :, None] == jnp.arange(capacity)[None, None, :])
    ).astype(jnp.int32)
    arrive_local = jnp.sum(matches * local_index[:, :, None], axis=1).reshape(-1)
    arrive_valid = jnp.sum(matches, axis=1).reshape(-1)

    pool = lax.all_gather(
        jnp.concatenate([neighbour_keys, neighbour_values], axis=0), "dp", axis=0, tiled=True
    )
    packed = pack_heads(queries[0], grad_out[0], parts)
    tokens = lax.all_to_all(packed, "ctx", split_axis=0, concat_axis=0, tiled=True)
    back, send = attend(slots, rows, tokens, pool, groups, distinct, replicas * 2 * capacity)
    back = lax.all_to_all(back, "ctx", split_axis=0, concat_axis=0, tiled=True)
    arrived = lax.all_to_all(
        send.reshape(replicas, 2 * capacity, nbr, width), "dp", split_axis=0, concat_axis=0, tiled=True
    )
    grad_keys, grad_values = collect(arrive_local, arrive_valid, arrived, owned)
    return (join_heads(back)[None], grad_keys, grad_values)


def solution(mesh):
    return jax.shard_map(
        on_device,
        mesh=mesh,
        in_specs=(
            P("dp", "ctx", None),
            P("dp", "ctx", None),
            P("dp", None, "ctx"),
            P("dp", None, "ctx"),
            P(),
            P(),
        ),
        out_specs=(P("dp", "ctx", None), P("dp", None, "ctx"), P("dp", None, "ctx")),
        check_vma=False,
    )
```

```python
import functools
import math

import jax
import jax.numpy as jnp
from jax import lax
from jax.experimental import pallas as pl
from jax.experimental.pallas import tpu as pltpu
from jax.sharding import PartitionSpec as P

DH = 128
GROUP = 64
BF16 = jnp.bfloat16
F32 = jnp.float32
HBM = pl.BlockSpec(memory_space=pl.ANY)
VMEM = pl.BlockSpec(memory_space=pltpu.VMEM)
SMEM = pl.BlockSpec(memory_space=pltpu.SMEM)


SIDE = 4


def place(n, owned):
    owner = n // owned
    return (owner // SIDE, owner % SIDE, n % owned)


def shift(value, axis, amount):
    pairs = []
    for y in range(SIDE):
        for x in range(SIDE):
            to = (y, (x + amount) % SIDE) if axis == "x" else ((y + amount) % SIDE, x)
            pairs.append((y * SIDE + x, to[0] * SIDE + to[1]))
    return lax.ppermute(value, "dp", pairs)


def gather_line(own, axis):
    half = own.shape[0] // 2
    before = shift(own, axis, 1)
    after = shift(own, axis, -1)
    far = (shift(before[:half], axis, 1), shift(after[half:], axis, -1))
    return (own, after, far[0], far[1], before)


def exchange_line(chunks, axis, sign):
    one, low, high, three = chunks
    low = shift(low, axis, 1)
    high = shift(high, axis, -1)
    one = shift(one, axis, sign)
    three = shift(three, axis, -sign)
    return (one, shift(low, axis, 1), shift(high, axis, -1), three)


def pack_heads_body(width, q_ref, g_ref, out_ref):
    for j in range(out_ref.shape[0]):
        out_ref[j, 0] = q_ref[:, j * width : (j + 1) * width]
        out_ref[j, 1] = g_ref[:, j * width : (j + 1) * width]


def pack_heads(queries, grad_out, parts):
    tokens, features = queries.shape
    width = features // parts
    steps = 4
    per_step = parts // steps
    block = pl.BlockSpec((tokens, per_step * width), lambda i: (0, i))
    return pl.pallas_call(
        functools.partial(pack_heads_body, width),
        grid=(steps,),
        out_shape=jax.ShapeDtypeStruct((parts, 2, tokens, width), BF16),
        in_specs=[block, block],
        out_specs=pl.BlockSpec((per_step, 2, tokens, width), lambda i: (i, 0, 0, 0)),
    )(queries, grad_out)


def join_heads_body(width, in_ref, out_ref):
    for j in range(in_ref.shape[0]):
        out_ref[:, j * width : (j + 1) * width] = in_ref[j]


def join_heads(blocks):
    parts, tokens, width = blocks.shape
    steps = 4
    per_step = parts // steps
    return pl.pallas_call(
        functools.partial(join_heads_body, width),
        grid=(steps,),
        out_shape=jax.ShapeDtypeStruct((tokens, parts * width), BF16),
        in_specs=[pl.BlockSpec((per_step, tokens, width), lambda i: (i, 0, 0))],
        out_specs=pl.BlockSpec((tokens, per_step * width), lambda i: (0, i)),
    )(blocks)


def matmul(a, b, contract):
    return lax.dot_general(a, b, ((contract[:1], contract[1:]), ((), ())), preferred_element_type=F32)


def block_diagonal(rows):
    zero = jnp.zeros((rows.shape[0], DH), BF16)
    return jnp.concatenate(
        [
            jnp.concatenate([rows[:, :DH], zero], axis=1),
            jnp.concatenate([zero, rows[:, DH:]], axis=1),
        ],
        axis=0,
    )


def select_body(axis, owned, ids_ref, own_ref, after_ref, low_ref, high_ref, before_ref,
                zero_ref, one_ref, two_low_ref, two_high_ref, three_ref, line, picked):
    me = lax.axis_index("dp")
    mine = (me // SIDE, me % SIDE)
    half = owned // 2
    line[0:owned] = own_ref[...]
    line[owned : 2 * owned] = after_ref[...]
    line[2 * owned : 2 * owned + half] = low_ref[...]
    line[2 * owned + half : 3 * owned] = high_ref[...]
    line[3 * owned :] = before_ref[...]
    most = zero_ref.shape[0]
    distinct = ids_ref.shape[1]
    across = 0 if axis == "x" else 1
    for k in range(SIDE):
        other = (mine[across] + k) % SIDE
        replica = other * SIDE + mine[1] if across == 0 else mine[0] * SIDE + other

        def step(j, count):
            where = place(ids_ref[replica, j], owned)
            found = where[across] == mine[across]

            @pl.when(found)
            def _():
                distance = (where[1 - across] - mine[1 - across] + SIDE) % SIDE
                picked[k * most + count] = line[distance * owned + where[2]]

            return count + found.astype(jnp.int32)

        lax.fori_loop(0, distinct, step, jnp.int32(0))
    middle = 2 * most + most // 2
    zero_ref[...] = picked[0:most]
    one_ref[...] = picked[most : 2 * most]
    two_low_ref[...] = picked[2 * most : middle]
    two_high_ref[...] = picked[middle : 3 * most]
    three_ref[...] = picked[3 * most :]


def chunk_shapes(most, nbr, width):
    return tuple(
        jax.ShapeDtypeStruct((n, nbr, width), BF16) for n in (most, most, most // 2, most // 2, most)
    )


def select(ids, line, axis, most):
    owned, nbr, width = line[0].shape
    return pl.pallas_call(
        functools.partial(select_body, axis, owned),
        out_shape=chunk_shapes(most, nbr, width),
        in_specs=[SMEM] + [VMEM] * 5,
        out_specs=(VMEM,) * 5,
        scratch_shapes=[
            pltpu.VMEM((SIDE * owned, nbr, width), BF16),
            pltpu.VMEM((SIDE * most, nbr, width), BF16),
        ],
        compiler_params=pltpu.CompilerParams(vmem_limit_bytes=24 * 1024 * 1024),
    )(ids, *line)


def spread_body(axis, owned, ids_ref, zero_ref, one_ref, two_low_ref, two_high_ref, three_ref,
                own_ref, after_ref, low_ref, high_ref, before_ref, sums):
    me = lax.axis_index("dp")
    mine = (me // SIDE, me % SIDE)
    half = owned // 2
    half_most = two_low_ref.shape[0]
    distinct = ids_ref.shape[1]
    across = 0 if axis == "x" else 1
    sums[...] = jnp.zeros_like(sums)
    for k, chunk in enumerate((zero_ref, one_ref, (two_low_ref, two_high_ref), three_ref)):
        other = (mine[across] + k) % SIDE
        replica = other * SIDE + mine[1] if across == 0 else mine[0] * SIDE + other

        def step(j, count):
            where = place(ids_ref[replica, j], owned)
            found = where[across] == mine[across]
            distance = (where[1 - across] - mine[1 - across] + SIDE) % SIDE
            row = distance * owned + where[2]
            if k != 2:

                @pl.when(found)
                def _():
                    sums[row] += chunk[count].astype(F32)

            else:

                @pl.when(found & (count < half_most))
                def _():
                    sums[row] += chunk[0][jnp.minimum(count, half_most - 1)].astype(F32)

                @pl.when(found & (count >= half_most))
                def _():
                    sums[row] += chunk[1][jnp.maximum(count - half_most, 0)].astype(F32)

            return count + found.astype(jnp.int32)

        lax.fori_loop(0, distinct, step, jnp.int32(0))
    middle = 2 * owned + half
    own_ref[...] = sums[0:owned]
    after_ref[...] = sums[owned : 2 * owned].astype(BF16)
    low_ref[...] = sums[2 * owned : middle].astype(BF16)
    high_ref[...] = sums[middle : 3 * owned].astype(BF16)
    before_ref[...] = sums[3 * owned :].astype(BF16)


def spread(ids, chunks, axis, owned):
    most, nbr, width = chunks[0].shape
    shape = lambda n, kind: jax.ShapeDtypeStruct((n, nbr, width), kind)
    return pl.pallas_call(
        functools.partial(spread_body, axis, owned),
        out_shape=(
            shape(owned, F32),
            shape(owned, BF16),
            shape(owned // 2, BF16),
            shape(owned // 2, BF16),
            shape(owned, BF16),
        ),
        in_specs=[SMEM] + [VMEM] * 5,
        out_specs=(VMEM,) * 5,
        scratch_shapes=[pltpu.VMEM((SIDE * owned, nbr, width), F32)],
        compiler_params=pltpu.CompilerParams(vmem_limit_bytes=24 * 1024 * 1024),
    )(ids, *chunks)


def attend_body(
    groups, distinct, owned, most, unroll, ids_ref, refs_ref, tokens_ref, *refs
):
    key_parts, value_parts = refs[:5], refs[5:10]
    gq_ref = refs[10]
    key_out, value_out = refs[11:16], refs[16:21]
    (keys, values, key_sum, value_sum, key_send, value_send,
     query_last, grad_last, held, key_rows, value_rows, counts, sems) = refs[21:]
    scale = 1.0 / math.sqrt(DH)
    starts = (0, most, 2 * most, 2 * most + most // 2, 3 * most)
    copies = []
    for i, (parts, pool) in enumerate(((key_parts, keys), (value_parts, values))):
        for n, (part, start) in enumerate(zip(parts, starts)):
            copies.append(
                pltpu.make_async_copy(part, pool.at[pl.ds(start, part.shape[0])], sems.at[0, i, n])
            )
    for copy in copies:
        copy.start()
    key_sum[...] = jnp.zeros_like(key_sum)
    value_sum[...] = jnp.zeros_like(value_sum)
    width = gq_ref.shape[2]
    row = lax.broadcasted_iota(jnp.int32, (GROUP, width), 0)
    me = lax.axis_index("dp")
    mine = (me // SIDE, me % SIDE)
    for i in range(2 * SIDE):
        counts[i] = 0

    def rank(j, carry):
        where = place(ids_ref[me, j], owned)
        for i, table in enumerate((key_rows, value_rows)):
            distance = (mine[i] - where[i] + SIDE) % SIDE
            count = counts[i * SIDE + distance]
            table[j] = distance * most + count
            counts[i * SIDE + distance] = count + 1
        return carry

    lax.fori_loop(0, distinct, rank, 0)

    def rolled(kind, block):
        part = tokens_ref[block // 2, kind, pl.ds((block % 2) * GROUP, GROUP), :]
        return pltpu.roll(part.astype(F32), 1, 0)

    held[...] = jnp.zeros_like(held)
    query_last[...] = rolled(0, 0)
    grad_last[...] = rolled(1, 0)
    for copy in copies:
        copy.wait()

    def shifted(kind, group, last):
        following = rolled(kind, jnp.minimum(group + 1, groups - 1))
        following = jnp.where(group + 1 < groups, following, 0.0)
        block = jnp.where(row == 0, last[...], following)
        last[...] = following
        return block_diagonal(block.astype(BF16))

    def step(group):
        query = shifted(0, group, query_last)
        grad = shifted(1, group, grad_last)
        pair = (refs_ref[me, 2 * group], refs_ref[me, 2 * group + 1])
        block_keys = [keys[key_rows[j]] for j in pair]
        scores = [matmul(k, query, (1, 1)) for k in block_keys]
        grads = [matmul(values[value_rows[j]], grad, (1, 1)) for j in pair]
        top = jnp.maximum(*[jnp.max(s, axis=0, keepdims=True) for s in scores])
        weights = [jnp.exp((s - top) * scale) for s in scores]
        total = sum(jnp.sum(w, axis=0, keepdims=True) for w in weights)
        inverse = 1.0 / total
        weights = [w * inverse for w in weights]
        dots = sum(jnp.sum(w * g, axis=0, keepdims=True) for w, g in zip(weights, grads))
        grad_low = [(w * (g - dots)).astype(BF16) for w, g in zip(weights, grads)]
        weights_low = [w.astype(BF16) for w in weights]
        for j, w, g in zip(pair, weights_low, grad_low):
            value_sum[j] += matmul(w, grad, (1, 0))
            key_sum[j] += matmul(g, query, (1, 0))
        both = sum(matmul(g, k, (0, 0)) for g, k in zip(grad_low, block_keys)) * scale
        back = jnp.concatenate([both[:GROUP, :DH], both[GROUP:, DH:]], axis=1)
        back = pltpu.roll(back, GROUP - 1, 0)
        gq_ref[group // 2, pl.ds((group % 2) * GROUP, GROUP), :] = jnp.where(
            row == GROUP - 1, back, held[...]
        ).astype(BF16)
        held[...] = back

    def steps(index, carry):
        for u in range(unroll):
            step(index * unroll + u)
        return carry

    lax.fori_loop(0, groups // unroll, steps, 0)
    copies = []
    for i, (send, parts) in enumerate(((key_send, key_out), (value_send, value_out))):
        for j in range(distinct):
            if i == 0:
                send[key_rows[j]] = (key_sum[j] * scale).astype(BF16)
            else:
                send[value_rows[j]] = value_sum[j].astype(BF16)
        for n, (part, start) in enumerate(zip(parts, starts)):
            copy = pltpu.make_async_copy(send.at[pl.ds(start, part.shape[0])], part, sems.at[1, i, n])
            copy.start()
            copies.append(copy)
    for copy in copies:
        copy.wait()


def attend(ids, refs, tokens, keys, values, owned, most):
    parts, _, part_tokens, width = tokens.shape
    nbr = keys[0].shape[1]
    distinct = ids.shape[1]
    groups = refs.shape[1]
    flat = refs.reshape(refs.shape[0], -1)
    chunks = chunk_shapes(most, nbr, width)
    pool = pltpu.VMEM((SIDE * most, nbr, width), BF16)
    total = pltpu.VMEM((distinct, nbr, width), F32)
    rows = pltpu.VMEM((GROUP, width), F32)
    out = pl.pallas_call(
        functools.partial(attend_body, groups, distinct, owned, most, 2),
        out_shape=(jax.ShapeDtypeStruct((parts, part_tokens, width), BF16),) + chunks + chunks,
        in_specs=[SMEM, SMEM, VMEM] + [HBM] * 10,
        out_specs=(VMEM,) + (HBM,) * 10,
        scratch_shapes=[pool, pool, total, total, pool, pool, rows, rows, rows,
                        pltpu.SMEM((distinct,), jnp.int32), pltpu.SMEM((distinct,), jnp.int32),
                        pltpu.SMEM((2 * SIDE,), jnp.int32), pltpu.SemaphoreType.DMA((2, 2, 5))],
        compiler_params=pltpu.CompilerParams(vmem_limit_bytes=48 * 1024 * 1024),
    )(ids, flat, tokens, *keys, *values)
    return (out[0], out[1:6], out[6:])


def collect_body(*refs):
    half = refs[2].shape[0]
    for parts, out in ((refs[:5], refs[10]), (refs[5:10], refs[11])):
        own, after, low, high, before = parts
        near = own[...] + after[...].astype(F32) + before[...].astype(F32)
        out[:half] = (near[:half] + low[...].astype(F32)).astype(BF16)
        out[half:] = (near[half:] + high[...].astype(F32)).astype(BF16)


def collect(keys, values):
    out = jax.ShapeDtypeStruct(keys[0].shape, BF16)
    return pl.pallas_call(
        collect_body,
        out_shape=(out, out),
        in_specs=[VMEM] * 10,
        out_specs=(VMEM, VMEM),
        compiler_params=pltpu.CompilerParams(vmem_limit_bytes=24 * 1024 * 1024),
    )(*keys, *values)


def on_device(queries, grad_out, neighbour_keys, neighbour_values, distinct_ids, group_refs):
    parts = lax.axis_size("ctx")
    owned = neighbour_keys.shape[0]
    most = SIDE * (owned // 2)
    packed = pack_heads(queries[0], grad_out[0], parts)
    tokens = lax.all_to_all(packed, "ctx", split_axis=0, concat_axis=0, tiled=True)
    keys = select(distinct_ids, gather_line(neighbour_keys, "x"), "x", most)
    values = select(distinct_ids, gather_line(neighbour_values, "y"), "y", most)
    keys = keys[:1] + exchange_line(keys[1:], "y", 1)
    values = values[:1] + exchange_line(values[1:], "x", 1)
    back, keys, values = attend(
        distinct_ids, group_refs, tokens, keys, values, owned, most
    )
    back = lax.all_to_all(back, "ctx", split_axis=0, concat_axis=0, tiled=True)
    keys = spread(distinct_ids, keys[:1] + exchange_line(keys[1:], "y", -1), "x", owned)
    values = spread(distinct_ids, values[:1] + exchange_line(values[1:], "x", -1), "y", owned)
    keys = keys[:1] + exchange_line(keys[1:], "x", 1)
    values = values[:1] + exchange_line(values[1:], "y", 1)
    grad_keys, grad_values = collect(keys, values)
    return (join_heads(back)[None], grad_keys, grad_values)


def solution(mesh):
    return jax.shard_map(
        on_device,
        mesh=mesh,
        in_specs=(
            P("dp", "ctx", None),
            P("dp", "ctx", None),
            P("dp", None, "ctx"),
            P("dp", None, "ctx"),
            P(),
            P(),
        ),
        out_specs=(P("dp", "ctx", None), P("dp", None, "ctx"), P("dp", None, "ctx")),
        check_vma=False,
    )
```

```python
import functools
import math

import jax
import jax.numpy as jnp
from jax import lax
from jax.experimental import pallas as pl
from jax.experimental.pallas import tpu as pltpu
from jax.sharding import PartitionSpec as P

DH = 128
GROUP = 64
BF16 = jnp.bfloat16
F32 = jnp.float32
HBM = pl.BlockSpec(memory_space=pl.ANY)
VMEM = pl.BlockSpec(memory_space=pltpu.VMEM)
SMEM = pl.BlockSpec(memory_space=pltpu.SMEM)


SIDE = 4


def place(n, owned):
    owner = n // owned
    return (owner // SIDE, owner % SIDE, n % owned)


def shift(value, axis, amount):
    pairs = []
    for y in range(SIDE):
        for x in range(SIDE):
            to = (y, (x + amount) % SIDE) if axis == "x" else ((y + amount) % SIDE, x)
            pairs.append((y * SIDE + x, to[0] * SIDE + to[1]))
    return lax.ppermute(value, "dp", pairs)


def gather_line(own, axis):
    half = own.shape[0] // 2
    before = shift(own, axis, 1)
    after = shift(own, axis, -1)
    low = shift(before[:half], axis, 1)
    high = shift(after[half:], axis, -1)
    return (own, after, low, high, before)


def exchange_line(sent, axis, sign):
    own, plus, minus = sent
    most = plus.shape[0] * 2 // 3
    plus = shift(plus, axis, sign)
    minus = shift(minus, axis, -sign)
    low = shift(plus[most:], axis, sign)
    high = shift(minus[most:], axis, -sign)
    return (own, plus, low, minus, high)


def sent_row(distance, count, most):
    base = jnp.where(distance == 1, most, jnp.where(distance == 3, most * 5 // 2, 0))
    far = 2 * most + jnp.where(count < most // 2, 0, most)
    return jnp.where(distance == 2, far, base) + count


def put(refs, row, value):
    own, plus, minus = refs
    first, second = own.shape[0], own.shape[0] + plus.shape[0]

    @pl.when(row < first)
    def _():
        own[jnp.minimum(row, first - 1)] = value.astype(own.dtype)

    @pl.when((row >= first) & (row < second))
    def _():
        plus[jnp.clip(row - first, 0, plus.shape[0] - 1)] = value.astype(plus.dtype)

    @pl.when(row >= second)
    def _():
        minus[jnp.clip(row - second, 0, minus.shape[0] - 1)] = value.astype(minus.dtype)


def sent_shapes(most, nbr, width, own_type=BF16):
    return (
        jax.ShapeDtypeStruct((most, nbr, width), own_type),
        jax.ShapeDtypeStruct((most * 3 // 2, nbr, width), BF16),
        jax.ShapeDtypeStruct((most * 3 // 2, nbr, width), BF16),
    )


def pack_heads_body(width, q_ref, g_ref, out_ref):
    for j in range(out_ref.shape[0]):
        out_ref[j, 0] = q_ref[:, j * width : (j + 1) * width]
        out_ref[j, 1] = g_ref[:, j * width : (j + 1) * width]


def pack_heads(queries, grad_out, parts):
    tokens, features = queries.shape
    width = features // parts
    steps = 4
    per_step = parts // steps
    block = pl.BlockSpec((tokens, per_step * width), lambda i: (0, i))
    return pl.pallas_call(
        functools.partial(pack_heads_body, width),
        grid=(steps,),
        out_shape=jax.ShapeDtypeStruct((parts, 2, tokens, width), BF16),
        in_specs=[block, block],
        out_specs=pl.BlockSpec((per_step, 2, tokens, width), lambda i: (i, 0, 0, 0)),
    )(queries, grad_out)


def join_heads_body(width, in_ref, out_ref):
    for j in range(in_ref.shape[0]):
        out_ref[:, j * width : (j + 1) * width] = in_ref[j]


def join_heads(blocks):
    parts, tokens, width = blocks.shape
    steps = 4
    per_step = parts // steps
    return pl.pallas_call(
        functools.partial(join_heads_body, width),
        grid=(steps,),
        out_shape=jax.ShapeDtypeStruct((tokens, parts * width), BF16),
        in_specs=[pl.BlockSpec((per_step, tokens, width), lambda i: (i, 0, 0))],
        out_specs=pl.BlockSpec((tokens, per_step * width), lambda i: (0, i)),
    )(blocks)


def matmul(a, b, contract):
    return lax.dot_general(a, b, ((contract[:1], contract[1:]), ((), ())), preferred_element_type=F32)


def block_diagonal(rows):
    zero = jnp.zeros((rows.shape[0], DH), BF16)
    return jnp.concatenate(
        [
            jnp.concatenate([rows[:, :DH], zero], axis=1),
            jnp.concatenate([zero, rows[:, DH:]], axis=1),
        ],
        axis=0,
    )


def select_body(owned, ids_ref, *refs):
    me = lax.axis_index("dp")
    mine = (me // SIDE, me % SIDE)
    distinct = ids_ref.shape[1]
    line = refs[16]
    for across in range(2):
        start = 0
        for part in refs[5 * across : 5 * across + 5]:
            size = part.shape[0]
            for n in range(size):
                line[start + n] = part[n]
            start += size
        out = refs[10 + 3 * across : 13 + 3 * across]
        most = out[0].shape[0]

        def chunk(k, carry):
            other = (mine[across] + k) % SIDE
            replica = other * SIDE + mine[1] if across == 0 else mine[0] * SIDE + other

            def step(j, count):
                where = place(ids_ref[replica, j], owned)
                found = where[across] == mine[across]

                @pl.when(found)
                def _():
                    distance = (where[1 - across] - mine[1 - across] + SIDE) % SIDE
                    put(out, sent_row(k, count, most), line[distance * owned + where[2]])

                return count + found.astype(jnp.int32)

            lax.fori_loop(0, distinct, step, jnp.int32(0))
            return carry

        lax.fori_loop(0, SIDE, chunk, 0)


def select(ids, keys, values, most):
    owned, nbr, width = keys[0].shape
    out = pl.pallas_call(
        functools.partial(select_body, owned),
        out_shape=sent_shapes(most, nbr, width) * 2,
        in_specs=[SMEM] + [VMEM] * 10,
        out_specs=(VMEM,) * 6,
        scratch_shapes=[pltpu.VMEM((SIDE * owned, nbr, width), BF16)],
        compiler_params=pltpu.CompilerParams(vmem_limit_bytes=24 * 1024 * 1024),
    )(ids, *keys, *values)
    return (out[:3], out[3:])


def spread_body(owned, ids_ref, *refs):
    me = lax.axis_index("dp")
    mine = (me // SIDE, me % SIDE)
    distinct = ids_ref.shape[1]
    sums = refs[16]
    zero = jnp.zeros(sums.shape[1:], F32)
    for across in range(2):
        own, plus, low, minus, high = refs[5 * across : 5 * across + 5]
        most, half = own.shape[0], low.shape[0]
        out = refs[10 + 3 * across : 13 + 3 * across]

        def clear(n, carry):
            sums[n] = zero
            return carry

        lax.fori_loop(0, SIDE * owned, clear, 0)
        for k, chunk in enumerate((own, plus, None, minus)):
            other = (mine[across] + k) % SIDE
            replica = other * SIDE + mine[1] if across == 0 else mine[0] * SIDE + other

            def step(j, count):
                where = place(ids_ref[replica, j], owned)
                found = where[across] == mine[across]
                distance = (where[1 - across] - mine[1 - across] + SIDE) % SIDE
                row = distance * owned + where[2]
                if chunk is not None:

                    @pl.when(found)
                    def _():
                        sums[row] += chunk[jnp.minimum(count, most - 1)].astype(F32)

                else:

                    @pl.when(found & (count < half))
                    def _():
                        sums[row] += low[jnp.minimum(count, half - 1)].astype(F32)

                    @pl.when(found & (count >= half))
                    def _():
                        sums[row] += high[jnp.clip(count - half, 0, half - 1)].astype(F32)

                return count + found.astype(jnp.int32)

            lax.fori_loop(0, distinct, step, jnp.int32(0))

        def store(n, carry):
            put(out, sent_row(n // owned, n % owned, owned), sums[n])
            return carry

        lax.fori_loop(0, SIDE * owned, store, 0)


def spread(ids, keys, values, owned):
    _, nbr, width = keys[0].shape
    out = pl.pallas_call(
        functools.partial(spread_body, owned),
        out_shape=sent_shapes(owned, nbr, width, F32) * 2,
        in_specs=[SMEM] + [VMEM] * 10,
        out_specs=(VMEM,) * 6,
        scratch_shapes=[pltpu.VMEM((SIDE * owned, nbr, width), F32)],
        compiler_params=pltpu.CompilerParams(vmem_limit_bytes=32 * 1024 * 1024),
    )(ids, *keys, *values)
    return (out[:3], out[3:])


def attend_body(
    groups, distinct, owned, most, unroll, ids_ref, refs_ref, tokens_ref, *refs
):
    key_parts, value_parts = refs[:5], refs[5:10]
    gq_ref = refs[10]
    key_out, value_out = refs[11:14], refs[14:17]
    (keys, values, key_sum, value_sum, query_last, grad_last, held, key_rows, value_rows, counts,
     sems) = refs[17:]
    scale = 1.0 / math.sqrt(DH)
    copies = []
    for i, (parts, pool) in enumerate(((key_parts, keys), (value_parts, values))):
        start = 0
        for n, (part, size) in enumerate(zip(parts, (most, most, most // 2, most, most // 2))):
            copies.append(
                pltpu.make_async_copy(
                    part.at[pl.ds(0, size)], pool.at[pl.ds(start, size)], sems.at[i, n]
                )
            )
            start += size
    for copy in copies:
        copy.start()

    def clear(j, carry):
        key_sum[j] = jnp.zeros(key_sum.shape[1:], F32)
        value_sum[j] = jnp.zeros(value_sum.shape[1:], F32)
        return carry

    lax.fori_loop(0, distinct, clear, 0)
    width = gq_ref.shape[2]
    row = lax.broadcasted_iota(jnp.int32, (GROUP, width), 0)
    me = lax.axis_index("dp")
    mine = (me // SIDE, me % SIDE)
    for i in range(2 * SIDE):
        counts[i] = 0

    def rank(j, carry):
        where = place(ids_ref[me, j], owned)
        for i, table in enumerate((key_rows, value_rows)):
            distance = (mine[i] - where[i] + SIDE) % SIDE
            count = counts[i * SIDE + distance]
            table[j] = sent_row(distance, count, most)
            counts[i * SIDE + distance] = count + 1
        return carry

    lax.fori_loop(0, distinct, rank, 0)

    def rolled(kind, block):
        part = tokens_ref[block // 2, kind, pl.ds((block % 2) * GROUP, GROUP), :]
        return pltpu.roll(part.astype(F32), 1, 0)

    held[...] = jnp.zeros_like(held)
    query_last[...] = rolled(0, 0)
    grad_last[...] = rolled(1, 0)
    for copy in copies:
        copy.wait()

    def shifted(kind, group, last):
        following = rolled(kind, jnp.minimum(group + 1, groups - 1))
        following = jnp.where(group + 1 < groups, following, 0.0)
        block = jnp.where(row == 0, last[...], following)
        last[...] = following
        return block_diagonal(block.astype(BF16))

    def step(group):
        query = shifted(0, group, query_last)
        grad = shifted(1, group, grad_last)
        pair = (refs_ref[me, 2 * group], refs_ref[me, 2 * group + 1])
        block_keys = [keys[key_rows[j]] for j in pair]
        scores = [matmul(k, query, (1, 1)) for k in block_keys]
        grads = [matmul(values[value_rows[j]], grad, (1, 1)) for j in pair]
        top = jnp.maximum(*[jnp.max(s, axis=0, keepdims=True) for s in scores])
        weights = [jnp.exp((s - top) * scale) for s in scores]
        total = sum(jnp.sum(w, axis=0, keepdims=True) for w in weights)
        inverse = 1.0 / total
        weights = [w * inverse for w in weights]
        dots = sum(jnp.sum(w * g, axis=0, keepdims=True) for w, g in zip(weights, grads))
        grad_low = [(w * (g - dots)).astype(BF16) for w, g in zip(weights, grads)]
        weights_low = [w.astype(BF16) for w in weights]
        for j, w, g in zip(pair, weights_low, grad_low):
            value_sum[j] += matmul(w, grad, (1, 0))
            key_sum[j] += matmul(g, query, (1, 0))
        both = sum(matmul(g, k, (0, 0)) for g, k in zip(grad_low, block_keys)) * scale
        back = jnp.concatenate([both[:GROUP, :DH], both[GROUP:, DH:]], axis=1)
        back = pltpu.roll(back, GROUP - 1, 0)
        gq_ref[group // 2, pl.ds((group % 2) * GROUP, GROUP), :] = jnp.where(
            row == GROUP - 1, back, held[...]
        ).astype(BF16)
        held[...] = back

    def steps(index, carry):
        for u in range(unroll):
            step(index * unroll + u)
        return carry

    lax.fori_loop(0, groups // unroll, steps, 0)

    def give(j, carry):
        put(key_out, key_rows[j], key_sum[j] * scale)
        put(value_out, value_rows[j], value_sum[j])
        return carry

    lax.fori_loop(0, distinct, give, 0)


def attend(ids, refs, tokens, keys, values, owned, most):
    parts, _, part_tokens, width = tokens.shape
    nbr = keys[0].shape[1]
    distinct = ids.shape[1]
    groups = refs.shape[1]
    flat = refs.reshape(refs.shape[0], -1)
    pool = pltpu.VMEM((SIDE * most, nbr, width), BF16)
    total = pltpu.VMEM((distinct, nbr, width), F32)
    rows = pltpu.VMEM((GROUP, width), F32)
    out = pl.pallas_call(
        functools.partial(attend_body, groups, distinct, owned, most, 2),
        out_shape=(jax.ShapeDtypeStruct((parts, part_tokens, width), BF16),)
        + sent_shapes(most, nbr, width) * 2,
        in_specs=[SMEM, SMEM, VMEM] + [HBM] * 10,
        out_specs=(VMEM,) * 7,
        scratch_shapes=[pool, pool, total, total, rows, rows, rows,
                        pltpu.SMEM((distinct,), jnp.int32), pltpu.SMEM((distinct,), jnp.int32),
                        pltpu.SMEM((2 * SIDE,), jnp.int32), pltpu.SemaphoreType.DMA((2, 5))],
        compiler_params=pltpu.CompilerParams(vmem_limit_bytes=36 * 1024 * 1024),
    )(ids, flat, tokens, *keys, *values)
    return (out[0], out[1:4], out[4:])


def collect_body(*refs):
    for i, out in enumerate(refs[10:]):
        own, plus, low, minus, high = refs[5 * i : 5 * i + 5]
        half = low.shape[0]
        for n in range(own.shape[0]):
            far = low[n] if n < half else high[n - half]
            out[n] = (
                own[n] + plus[n].astype(F32) + minus[n].astype(F32) + far.astype(F32)
            ).astype(BF16)


def collect(keys, values):
    out = jax.ShapeDtypeStruct(keys[0].shape, BF16)
    return pl.pallas_call(
        collect_body,
        out_shape=(out, out),
        in_specs=[VMEM] * 10,
        out_specs=(VMEM, VMEM),
        compiler_params=pltpu.CompilerParams(vmem_limit_bytes=24 * 1024 * 1024),
    )(*keys, *values)


def on_device(queries, grad_out, neighbour_keys, neighbour_values, distinct_ids, group_refs):
    parts = lax.axis_size("ctx")
    owned = neighbour_keys.shape[0]
    most = SIDE * (owned // 2)
    packed = pack_heads(queries[0], grad_out[0], parts)
    tokens = lax.all_to_all(packed, "ctx", split_axis=0, concat_axis=0, tiled=True)
    keys, values = select(
        distinct_ids, gather_line(neighbour_keys, "x"), gather_line(neighbour_values, "y"), most
    )
    back, keys, values = attend(
        distinct_ids,
        group_refs,
        tokens,
        exchange_line(keys, "y", 1),
        exchange_line(values, "x", 1),
        owned,
        most,
    )
    back = lax.all_to_all(back, "ctx", split_axis=0, concat_axis=0, tiled=True)
    keys, values = spread(
        distinct_ids, exchange_line(keys, "y", -1), exchange_line(values, "x", -1), owned
    )
    grad_keys, grad_values = collect(exchange_line(keys, "x", 1), exchange_line(values, "y", 1))
    return (join_heads(back)[None], grad_keys, grad_values)


def solution(mesh):
    return jax.shard_map(
        on_device,
        mesh=mesh,
        in_specs=(
            P("dp", "ctx", None),
            P("dp", "ctx", None),
            P("dp", None, "ctx"),
            P("dp", None, "ctx"),
            P(),
            P(),
        ),
        out_specs=(P("dp", "ctx", None), P("dp", None, "ctx"), P("dp", None, "ctx")),
        check_vma=False,
    )
```

```python
import functools
import math

import jax
import jax.numpy as jnp
from jax import lax
from jax.experimental import pallas as pl
from jax.experimental.pallas import tpu as pltpu
from jax.sharding import PartitionSpec as P

DH = 128
GROUP = 64
BF16 = jnp.bfloat16
F32 = jnp.float32
HBM = pl.BlockSpec(memory_space=pltpu.MemorySpace.HBM)
VMEM = pl.BlockSpec(memory_space=pltpu.VMEM)
SMEM = pl.BlockSpec(memory_space=pltpu.SMEM)
SELECT_VMEM = 10 * 1024 * 1024
SPREAD_VMEM = 8 * 1024 * 1024
ATTEND_VMEM = 20 * 1024 * 1024
COLLECT_VMEM = 8 * 1024 * 1024


SIDE = 4


def place(n, owned):
    owner = lax.div(n, owned)
    return (lax.div(owner, SIDE), lax.rem(owner, SIDE), lax.rem(n, owned))


def shift(value, axis, amount):
    pairs = []
    for y in range(SIDE):
        for x in range(SIDE):
            to = (y, (x + amount) % SIDE) if axis == "x" else ((y + amount) % SIDE, x)
            pairs.append((y * SIDE + x, to[0] * SIDE + to[1]))
    return lax.ppermute(value, "dp", pairs)


DISTANCES = (2, 1, 3)


def gather_lines(lines):
    parts = [[own, None, None, None] for own, _ in lines]
    for distance in DISTANCES:
        for part, (own, axis) in zip(parts, lines):
            part[distance] = shift(own, axis, -distance)
    return parts


def exchange_lines(lines):
    parts = [list(chunks) for chunks, _, _ in lines]
    for distance in DISTANCES:
        for part, (chunks, axis, sign) in zip(parts, lines):
            part[distance] = shift(chunks[distance], axis, sign * distance)
    return parts


def chunk_shapes(most, nbr, width, own_type=BF16):
    return tuple(
        jax.ShapeDtypeStruct((most, nbr, width), own_type if k == 0 else BF16) for k in range(SIDE)
    )


def pack_heads_body(parts, width, q_ref, g_ref, out_ref, sems):
    copies = []
    for i, ref in enumerate((q_ref, g_ref)):
        for j in range(parts):
            copies.append(
                pltpu.make_async_copy(
                    ref.at[:, pl.ds(j * width, width)], out_ref.at[j, i], sems.at[i, j]
                )
            )
    for copy in copies:
        copy.start()
    for copy in copies:
        copy.wait()


def pack_heads(queries, grad_out, parts):
    tokens, features = queries.shape
    width = features // parts
    return pl.pallas_call(
        functools.partial(pack_heads_body, parts, width),
        out_shape=jax.ShapeDtypeStruct((parts, 2, tokens, width), BF16),
        in_specs=[HBM, HBM],
        out_specs=VMEM,
        scratch_shapes=[pltpu.SemaphoreType.DMA((2, parts))],
    )(queries, grad_out)


def join_heads_body(parts, width, in_ref, out_ref, sems):
    copies = [
        pltpu.make_async_copy(in_ref.at[j], out_ref.at[:, pl.ds(j * width, width)], sems.at[j])
        for j in range(parts)
    ]
    for copy in copies:
        copy.start()
    for copy in copies:
        copy.wait()


def join_heads(blocks):
    parts, tokens, width = blocks.shape
    return pl.pallas_call(
        functools.partial(join_heads_body, parts, width),
        out_shape=jax.ShapeDtypeStruct((tokens, parts * width), BF16),
        in_specs=[VMEM],
        out_specs=HBM,
        scratch_shapes=[pltpu.SemaphoreType.DMA((parts,))],
    )(blocks)


def matmul(a, b, contract):
    return lax.dot_general(a, b, ((contract[:1], contract[1:]), ((), ())), preferred_element_type=F32)


def block_diagonal(rows):
    zero = jnp.zeros((rows.shape[0], DH), BF16)
    return jnp.concatenate(
        [
            jnp.concatenate([rows[:, :DH], zero], axis=1),
            jnp.concatenate([zero, rows[:, DH:]], axis=1),
        ],
        axis=0,
    )


def tables_body(owned, most, ids_ref, take_ref, add_ref):
    me = lax.axis_index("dp")
    mine = (lax.div(me, SIDE), lax.rem(me, SIDE))
    distinct = ids_ref.shape[1]
    for across in range(2):
        for n in range(SIDE * most):
            take_ref[across, n] = 0
        for n in range(SIDE * owned * SIDE):
            add_ref[across, n] = -1
        for k in range(SIDE):
            other = lax.rem(mine[across] + k, SIDE)
            replica = other * SIDE + mine[1] if across == 0 else mine[0] * SIDE + other

            def step(j, count):
                where = place(ids_ref[replica, j], owned)
                found = where[across] == mine[across]

                @pl.when(found)
                def _():
                    distance = lax.rem(where[1 - across] - mine[1 - across] + SIDE, SIDE)
                    row = distance * owned + where[2]
                    take_ref[across, k * most + count] = row
                    add_ref[across, row * SIDE + k] = count

                return count + found.astype(jnp.int32)

            lax.fori_loop(0, distinct, step, jnp.int32(0))


def tables(ids, owned, most):
    return pl.pallas_call(
        functools.partial(tables_body, owned, most),
        out_shape=(
            jax.ShapeDtypeStruct((2, SIDE * most), jnp.int32),
            jax.ShapeDtypeStruct((2, SIDE * owned * SIDE), jnp.int32),
        ),
        in_specs=[SMEM],
        out_specs=(SMEM, SMEM),
    )(ids)


def select_body(take_ref, *refs):
    lines, kept, sems = refs[16:18], refs[18:20], refs[20]
    copies = []
    for across in range(2):
        parts = refs[4 * across : 4 * across + 4]
        line = lines[across]
        owned = parts[0].shape[0]
        for k, part in enumerate(parts):
            for n in range(owned):
                line[k * owned + n] = part[n]
        own, *sent = refs[8 + 4 * across : 12 + 4 * across]
        most = own.shape[0]

        def pick(n, carry):
            kept[across][n] = line[take_ref[across, n]]
            for k, out in enumerate(sent):
                out[n] = line[take_ref[across, (k + 1) * most + n]]
            return carry

        lax.fori_loop(0, most, pick, 0, unroll=2)
        copies.append(pltpu.make_async_copy(kept[across], own, sems.at[across]))
        copies[-1].start()
    for copy in copies:
        copy.wait()


def select(take, keys, values, most):
    owned, nbr, width = keys[0].shape
    line = pltpu.VMEM((SIDE * owned, nbr, width), BF16)
    kept = pltpu.VMEM((most, nbr, width), BF16)
    shapes = chunk_shapes(most, nbr, width)
    out = pl.pallas_call(
        select_body,
        out_shape=((pltpu.HBM(shapes[0].shape, BF16),) + shapes[1:]) * 2,
        in_specs=[SMEM] + [VMEM] * 8,
        out_specs=((HBM,) + (VMEM,) * 3) * 2,
        scratch_shapes=[line, line, kept, kept, pltpu.SemaphoreType.DMA((2,))],
        compiler_params=pltpu.CompilerParams(vmem_limit_bytes=SELECT_VMEM),
    )(take, *keys, *values)
    return (out[:4], out[4:])


def spread_body(add_ref, *refs):
    for across in range(2):
        chunks = refs[4 * across : 4 * across + 4]
        outs = refs[8 + 4 * across : 12 + 4 * across]
        most, owned = chunks[0].shape[0], outs[0].shape[0]

        def add(n, carry):
            for distance, out in enumerate(outs):
                value = jnp.zeros(out.shape[1:], F32)
                for k, chunk in enumerate(chunks):
                    index = add_ref[across, (distance * owned + n) * SIDE + k]
                    term = chunk[jnp.clip(index, 0, most - 1)].astype(F32)
                    value += jnp.where(index >= 0, term, 0.0)
                out[n] = value.astype(out.dtype)
            return carry

        lax.fori_loop(0, owned, add, 0)


def spread(add, keys, values, owned):
    _, nbr, width = keys[0].shape
    out = pl.pallas_call(
        spread_body,
        out_shape=chunk_shapes(owned, nbr, width, F32) * 2,
        in_specs=[SMEM] + [VMEM] * 8,
        out_specs=(VMEM,) * 8,
        compiler_params=pltpu.CompilerParams(vmem_limit_bytes=SPREAD_VMEM),
    )(add, *keys, *values)
    return (out[:4], out[4:])


def attend_body(
    groups, distinct, owned, most, unroll, ids_ref, refs_ref, tokens_ref, *refs
):
    key_parts, value_parts = refs[:4], refs[4:8]
    gq_out, key_out, value_out = refs[8], refs[9:13], refs[13:17]
    (keys, values, key_sum, value_sum, gq_ref, key_send, value_send, query_last, grad_last, held,
     key_rows, value_rows, counts, in_sems, out_sems, gq_sem) = refs[17:]
    scale = 1.0 / math.sqrt(DH)
    copies = [
        pltpu.make_async_copy(part, pool.at[pl.ds(k * most, most)], in_sems.at[i, k])
        for i, (parts, pool) in enumerate(((key_parts, keys), (value_parts, values)))
        for k, part in enumerate(parts)
    ]
    for copy in copies:
        copy.start()

    def clear(j, carry):
        key_sum[j] = jnp.zeros(key_sum.shape[1:], F32)
        value_sum[j] = jnp.zeros(value_sum.shape[1:], F32)
        return carry

    lax.fori_loop(0, distinct, clear, 0)
    width = gq_ref.shape[2]
    row = lax.broadcasted_iota(jnp.int32, (GROUP, width), 0)
    me = lax.axis_index("dp")
    mine = (me // SIDE, me % SIDE)
    for i in range(2 * SIDE):
        counts[i] = 0

    def rank(j, carry):
        where = place(ids_ref[me, j], owned)
        for i, table in enumerate((key_rows, value_rows)):
            distance = (mine[i] - where[i] + SIDE) % SIDE
            count = counts[i * SIDE + distance]
            table[j] = distance * most + count
            counts[i * SIDE + distance] = count + 1
        return carry

    lax.fori_loop(0, distinct, rank, 0)

    def rolled(kind, block):
        part = tokens_ref[block // 2, kind, pl.ds((block % 2) * GROUP, GROUP), :]
        return pltpu.roll(part.astype(F32), 1, 0)

    held[...] = jnp.zeros_like(held)
    query_last[...] = rolled(0, 0)
    grad_last[...] = rolled(1, 0)
    for copy in copies:
        copy.wait()

    def shifted(kind, group, last):
        following = rolled(kind, jnp.minimum(group + 1, groups - 1))
        following = jnp.where(group + 1 < groups, following, 0.0)
        block = jnp.where(row == 0, last[...], following)
        last[...] = following
        return block_diagonal(block.astype(BF16))

    def step(group):
        query = shifted(0, group, query_last)
        grad = shifted(1, group, grad_last)
        pair = (refs_ref[me, 2 * group], refs_ref[me, 2 * group + 1])
        block_keys = [keys[key_rows[j]] for j in pair]
        scores = [matmul(k, query, (1, 1)) for k in block_keys]
        grads = [matmul(values[value_rows[j]], grad, (1, 1)) for j in pair]
        top = jnp.maximum(*[jnp.max(s, axis=0, keepdims=True) for s in scores])
        weights = [jnp.exp((s - top) * scale) for s in scores]
        total = sum(jnp.sum(w, axis=0, keepdims=True) for w in weights)
        inverse = 1.0 / total
        weights = [w * inverse for w in weights]
        dots = sum(jnp.sum(w * g, axis=0, keepdims=True) for w, g in zip(weights, grads))
        grad_low = [(w * (g - dots)).astype(BF16) for w, g in zip(weights, grads)]
        weights_low = [w.astype(BF16) for w in weights]
        for j, w, g in zip(pair, weights_low, grad_low):
            value_sum[j] += matmul(w, grad, (1, 0))
            key_sum[j] += matmul(g, query, (1, 0))
        both = sum(matmul(g, k, (0, 0)) for g, k in zip(grad_low, block_keys)) * scale
        back = jnp.concatenate([both[:GROUP, :DH], both[GROUP:, DH:]], axis=1)
        back = pltpu.roll(back, GROUP - 1, 0)
        gq_ref[group // 2, pl.ds((group % 2) * GROUP, GROUP), :] = jnp.where(
            row == GROUP - 1, back, held[...]
        ).astype(BF16)
        held[...] = back

    def steps(index, carry):
        for u in range(unroll):
            step(index * unroll + u)
        return carry

    lax.fori_loop(0, groups // unroll, steps, 0)

    copies = [pltpu.make_async_copy(gq_ref, gq_out, gq_sem)]
    copies[0].start()

    def give(j, carry):
        key_send[key_rows[j]] = (key_sum[j] * scale).astype(BF16)
        value_send[value_rows[j]] = value_sum[j].astype(BF16)
        return carry

    lax.fori_loop(0, distinct, give, 0, unroll=2)
    for i, (send, parts) in enumerate(((key_send, key_out), (value_send, value_out))):
        for k, part in enumerate(parts):
            copy = pltpu.make_async_copy(send.at[pl.ds(k * most, most)], part, out_sems.at[i, k])
            copy.start()
            copies.append(copy)
    for copy in copies:
        copy.wait()


def attend(ids, refs, tokens, keys, values, owned, most):
    parts, _, part_tokens, width = tokens.shape
    nbr = keys[0].shape[1]
    distinct = ids.shape[1]
    groups = refs.shape[1]
    flat = refs.reshape(refs.shape[0], -1)
    pool = pltpu.VMEM((SIDE * most, nbr, width), BF16)
    total = pltpu.VMEM((distinct, nbr, width), F32)
    rows = pltpu.VMEM((GROUP, width), F32)
    table = pltpu.SMEM((distinct,), jnp.int32)
    shapes = (jax.ShapeDtypeStruct((parts, part_tokens, width), BF16),) + chunk_shapes(
        most, nbr, width
    ) * 2
    constrain = lambda value: pltpu.with_memory_space_constraint(value, pltpu.MemorySpace.HBM)
    keys, values = jax.tree.map(constrain, (list(keys), list(values)))
    out = pl.pallas_call(
        functools.partial(attend_body, groups, distinct, owned, most, 2),
        out_shape=tuple(pltpu.HBM(shape.shape, shape.dtype) for shape in shapes),
        in_specs=[SMEM, SMEM, VMEM] + [HBM] * 8,
        out_specs=(HBM,) * 9,
        scratch_shapes=[pool, pool, total, total, pltpu.VMEM((parts, part_tokens, width), BF16),
                        pool, pool, rows, rows, rows, table, table,
                        pltpu.SMEM((2 * SIDE,), jnp.int32),
                        pltpu.SemaphoreType.DMA((2, SIDE)), pltpu.SemaphoreType.DMA((2, SIDE)),
                        pltpu.SemaphoreType.DMA],
        compiler_params=pltpu.CompilerParams(vmem_limit_bytes=ATTEND_VMEM),
    )(ids, flat, tokens, *keys, *values)
    return (out[0], out[1:5], out[5:])


def collect_body(*refs):
    for i, out in enumerate(refs[8:]):
        own, *others = refs[4 * i : 4 * i + 4]
        for n in range(own.shape[0]):
            value = own[n]
            for other in others:
                value += other[n].astype(F32)
            out[n] = value.astype(BF16)


def collect(keys, values):
    out = jax.ShapeDtypeStruct(keys[0].shape, BF16)
    return pl.pallas_call(
        collect_body,
        out_shape=(out, out),
        in_specs=[VMEM] * 8,
        out_specs=(VMEM, VMEM),
        compiler_params=pltpu.CompilerParams(vmem_limit_bytes=COLLECT_VMEM),
    )(*keys, *values)


def on_device(queries, grad_out, neighbour_keys, neighbour_values, distinct_ids, group_refs):
    parts = lax.axis_size("ctx")
    owned = neighbour_keys.shape[0]
    most = SIDE * (owned // 2)
    take, add = tables(distinct_ids, owned, most)
    lines = gather_lines(((neighbour_keys, "x"), (neighbour_values, "y")))
    packed = pack_heads(queries[0], grad_out[0], parts)
    tokens = lax.all_to_all(packed, "ctx", split_axis=0, concat_axis=0, tiled=True)
    keys, values = select(take, *lines, most)
    keys, values = exchange_lines(((keys, "y", 1), (values, "x", 1)))
    back, keys, values = attend(distinct_ids, group_refs, tokens, keys, values, owned, most)
    keys, values = exchange_lines(((keys, "y", -1), (values, "x", -1)))
    back = lax.all_to_all(back, "ctx", split_axis=0, concat_axis=0, tiled=True)
    keys, values = spread(add, keys, values, owned)
    keys, values = exchange_lines(((keys, "x", 1), (values, "y", 1)))
    grad_queries = join_heads(back)[None]
    grad_queries, keys, values = lax.optimization_barrier((grad_queries, keys, values))
    grad_keys, grad_values = collect(keys, values)
    return (grad_queries, grad_keys, grad_values)


def solution(mesh):
    return jax.shard_map(
        on_device,
        mesh=mesh,
        in_specs=(
            P("dp", "ctx", None),
            P("dp", "ctx", None),
            P("dp", None, "ctx"),
            P("dp", None, "ctx"),
            P(),
            P(),
        ),
        out_specs=(P("dp", "ctx", None), P("dp", None, "ctx"), P("dp", None, "ctx")),
        check_vma=False,
    )
```

```python
import functools
import math

import jax
import jax.numpy as jnp
from jax import lax
from jax.experimental import pallas as pl
from jax.experimental.pallas import tpu as pltpu
from jax.sharding import PartitionSpec as P

DH = 128
GROUP = 64
BF16 = jnp.bfloat16
F32 = jnp.float32
HBM = pl.BlockSpec(memory_space=pltpu.MemorySpace.HBM)
VMEM = pl.BlockSpec(memory_space=pltpu.VMEM)
SMEM = pl.BlockSpec(memory_space=pltpu.SMEM)
SELECT_VMEM = 10 * 1024 * 1024
SPREAD_VMEM = 8 * 1024 * 1024
ATTEND_VMEM = 20 * 1024 * 1024
COLLECT_VMEM = 8 * 1024 * 1024


SIDE = 4


def place(n, owned):
    owner = lax.div(n, owned)
    return (lax.div(owner, SIDE), lax.rem(owner, SIDE), lax.rem(n, owned))


def shift(value, axis, amount):
    pairs = []
    for y in range(SIDE):
        for x in range(SIDE):
            to = (y, (x + amount) % SIDE) if axis == "x" else ((y + amount) % SIDE, x)
            pairs.append((y * SIDE + x, to[0] * SIDE + to[1]))
    return lax.ppermute(value, "dp", pairs)


DISTANCES = (2, 1, 3)


def gather_lines(lines):
    parts = [[own, None, None, None] for own, _ in lines]
    for distance in DISTANCES:
        for part, (own, axis) in zip(parts, lines):
            part[distance] = shift(own, axis, -distance)
    return parts


def exchange_lines(lines):
    parts = [list(chunks) for chunks, _, _ in lines]
    for distance in DISTANCES:
        for part, (chunks, axis, sign) in zip(parts, lines):
            part[distance] = shift(chunks[distance], axis, sign * distance)
    return parts


def chunk_shapes(most, nbr, width, own_type=BF16):
    return tuple(
        jax.ShapeDtypeStruct((most, nbr, width), own_type if k == 0 else BF16) for k in range(SIDE)
    )


def pack_heads_body(parts, width, q_ref, g_ref, out_ref, sems):
    copies = []
    for i, ref in enumerate((q_ref, g_ref)):
        for j in range(parts):
            copies.append(
                pltpu.make_async_copy(
                    ref.at[:, pl.ds(j * width, width)], out_ref.at[j, i], sems.at[i, j]
                )
            )
    for copy in copies:
        copy.start()
    for copy in copies:
        copy.wait()


def pack_heads(queries, grad_out, parts):
    tokens, features = queries.shape
    width = features // parts
    return pl.pallas_call(
        functools.partial(pack_heads_body, parts, width),
        out_shape=jax.ShapeDtypeStruct((parts, 2, tokens, width), BF16),
        in_specs=[HBM, HBM],
        out_specs=VMEM,
        scratch_shapes=[pltpu.SemaphoreType.DMA((2, parts))],
    )(queries, grad_out)


def join_heads_body(parts, width, in_ref, out_ref, sems):
    copies = [
        pltpu.make_async_copy(in_ref.at[j], out_ref.at[:, pl.ds(j * width, width)], sems.at[j])
        for j in range(parts)
    ]
    for copy in copies:
        copy.start()
    for copy in copies:
        copy.wait()


def join_heads(blocks):
    parts, tokens, width = blocks.shape
    return pl.pallas_call(
        functools.partial(join_heads_body, parts, width),
        out_shape=jax.ShapeDtypeStruct((tokens, parts * width), BF16),
        in_specs=[VMEM],
        out_specs=HBM,
        scratch_shapes=[pltpu.SemaphoreType.DMA((parts,))],
    )(blocks)


def matmul(a, b, contract):
    return lax.dot_general(a, b, ((contract[:1], contract[1:]), ((), ())), preferred_element_type=F32)


def block_diagonal(rows):
    zero = jnp.zeros((rows.shape[0], DH), BF16)
    return jnp.concatenate(
        [
            jnp.concatenate([rows[:, :DH], zero], axis=1),
            jnp.concatenate([zero, rows[:, DH:]], axis=1),
        ],
        axis=0,
    )


def tables_body(owned, most, ids_ref, take_ref, add_ref):
    me = lax.axis_index("dp")
    mine = (lax.div(me, SIDE), lax.rem(me, SIDE))
    distinct = ids_ref.shape[1]
    for across in range(2):
        for n in range(SIDE * most):
            take_ref[across, n] = 0
        for n in range(SIDE * owned * SIDE):
            add_ref[across, n] = -1
        for k in range(SIDE):
            other = lax.rem(mine[across] + k, SIDE)
            replica = other * SIDE + mine[1] if across == 0 else mine[0] * SIDE + other

            def step(j, count):
                where = place(ids_ref[replica, j], owned)
                found = where[across] == mine[across]

                @pl.when(found)
                def _():
                    distance = lax.rem(where[1 - across] - mine[1 - across] + SIDE, SIDE)
                    row = distance * owned + where[2]
                    take_ref[across, k * most + count] = row
                    add_ref[across, row * SIDE + k] = count

                return count + found.astype(jnp.int32)

            lax.fori_loop(0, distinct, step, jnp.int32(0))


def tables(ids, owned, most):
    return pl.pallas_call(
        functools.partial(tables_body, owned, most),
        out_shape=(
            jax.ShapeDtypeStruct((2, SIDE * most), jnp.int32),
            jax.ShapeDtypeStruct((2, SIDE * owned * SIDE), jnp.int32),
        ),
        in_specs=[SMEM],
        out_specs=(SMEM, SMEM),
    )(ids)


def select_body(take_ref, *refs):
    lines, kept, sems = refs[16:18], refs[18:20], refs[20]
    copies = []
    for across in range(2):
        parts = refs[4 * across : 4 * across + 4]
        line = lines[across]
        owned = parts[0].shape[0]
        for k, part in enumerate(parts):
            for n in range(owned):
                line[k * owned + n] = part[n]
        own, *sent = refs[8 + 4 * across : 12 + 4 * across]
        most = own.shape[0]

        def pick(n, carry):
            kept[across][n] = line[take_ref[across, n]]
            for k, out in enumerate(sent):
                out[n] = line[take_ref[across, (k + 1) * most + n]]
            return carry

        lax.fori_loop(0, most, pick, 0, unroll=2)
        copies.append(pltpu.make_async_copy(kept[across], own, sems.at[across]))
        copies[-1].start()
    for copy in copies:
        copy.wait()


def select(take, keys, values, most):
    owned, nbr, width = keys[0].shape
    line = pltpu.VMEM((SIDE * owned, nbr, width), BF16)
    kept = pltpu.VMEM((most, nbr, width), BF16)
    shapes = chunk_shapes(most, nbr, width)
    out = pl.pallas_call(
        select_body,
        out_shape=((pltpu.HBM(shapes[0].shape, BF16),) + shapes[1:]) * 2,
        in_specs=[SMEM] + [VMEM] * 8,
        out_specs=((HBM,) + (VMEM,) * 3) * 2,
        scratch_shapes=[line, line, kept, kept, pltpu.SemaphoreType.DMA((2,))],
        compiler_params=pltpu.CompilerParams(vmem_limit_bytes=SELECT_VMEM),
    )(take, *keys, *values)
    return (out[:4], out[4:])


def spread_body(add_ref, *refs):
    for across in range(2):
        chunks = refs[4 * across : 4 * across + 4]
        outs = refs[8 + 4 * across : 12 + 4 * across]
        most, owned = chunks[0].shape[0], outs[0].shape[0]

        def add(n, carry):
            for distance, out in enumerate(outs):
                value = jnp.zeros(out.shape[1:], F32)
                for k, chunk in enumerate(chunks):
                    index = add_ref[across, (distance * owned + n) * SIDE + k]
                    term = chunk[jnp.clip(index, 0, most - 1)].astype(F32)
                    value += jnp.where(index >= 0, term, 0.0)
                out[n] = value.astype(out.dtype)
            return carry

        lax.fori_loop(0, owned, add, 0)


def spread(add, keys, values, owned):
    _, nbr, width = keys[0].shape
    out = pl.pallas_call(
        spread_body,
        out_shape=chunk_shapes(owned, nbr, width, F32) * 2,
        in_specs=[SMEM] + [VMEM] * 8,
        out_specs=(VMEM,) * 8,
        compiler_params=pltpu.CompilerParams(vmem_limit_bytes=SPREAD_VMEM),
    )(add, *keys, *values)
    return (out[:4], out[4:])


def attend_body(
    groups, distinct, owned, most, unroll, ids_ref, refs_ref, tokens_ref, *refs
):
    key_parts, value_parts = refs[:4], refs[4:8]
    gq_out, key_out, value_out = refs[8], refs[9:13], refs[13:17]
    (keys, values, key_sum, value_sum, gq_ref, key_send, value_send, query_last, grad_last, held,
     key_rows, value_rows, key_back, value_back, counts, in_sems, out_sems, gq_sem) = refs[17:]
    scale = 1.0 / math.sqrt(DH)
    copies = [
        pltpu.make_async_copy(part, pool.at[pl.ds(k * most, most)], in_sems.at[i, k])
        for i, (parts, pool) in enumerate(((key_parts, keys), (value_parts, values)))
        for k, part in enumerate(parts)
    ]
    for copy in copies:
        copy.start()

    def clear(j, carry):
        key_sum[j] = jnp.zeros(key_sum.shape[1:], F32)
        value_sum[j] = jnp.zeros(value_sum.shape[1:], F32)
        return carry

    lax.fori_loop(0, distinct, clear, 0)
    width = gq_ref.shape[2]
    row = lax.broadcasted_iota(jnp.int32, (GROUP, width), 0)
    me = lax.axis_index("dp")
    mine = (me // SIDE, me % SIDE)
    for i in range(2 * SIDE):
        counts[i] = 0
    for n in range(SIDE * most):
        key_back[n] = -1
        value_back[n] = -1

    def rank(j, carry):
        where = place(ids_ref[me, j], owned)
        for i, (table, back_rows) in enumerate(
            ((key_rows, key_back), (value_rows, value_back))
        ):
            distance = (mine[i] - where[i] + SIDE) % SIDE
            count = counts[i * SIDE + distance]
            table[j] = distance * most + count
            back_rows[distance * most + count] = j
            counts[i * SIDE + distance] = count + 1
        return carry

    lax.fori_loop(0, distinct, rank, 0)

    def rolled(kind, block):
        part = tokens_ref[block // 2, kind, pl.ds((block % 2) * GROUP, GROUP), :]
        return pltpu.roll(part.astype(F32), 1, 0)

    held[...] = jnp.zeros_like(held)
    query_last[...] = rolled(0, 0)
    grad_last[...] = rolled(1, 0)
    for copy in copies:
        copy.wait()

    def shifted(kind, group, last):
        following = rolled(kind, jnp.minimum(group + 1, groups - 1))
        following = jnp.where(group + 1 < groups, following, 0.0)
        block = jnp.where(row == 0, last[...], following)
        last[...] = following
        return block_diagonal(block.astype(BF16))

    def steps(index, carry):
        batch = [index * unroll + u for u in range(unroll)]
        state = []
        for group in batch:
            query = shifted(0, group, query_last)
            grad = shifted(1, group, grad_last)
            pair = (refs_ref[me, 2 * group], refs_ref[me, 2 * group + 1])
            block_keys = [keys[key_rows[j]] for j in pair]
            scores = [matmul(k, query, (1, 1)) for k in block_keys]
            grads = [matmul(values[value_rows[j]], grad, (1, 1)) for j in pair]
            state.append((group, query, grad, pair, block_keys, scores, grads))
        lows = []
        for group, query, grad, pair, block_keys, scores, grads in state:
            top = jnp.maximum(*[jnp.max(s, axis=0, keepdims=True) for s in scores])
            weights = [jnp.exp2((s - top) * (scale * math.log2(math.e))) for s in scores]
            total = sum(jnp.sum(w, axis=0, keepdims=True) for w in weights)
            inverse = 1.0 / total
            weights = [w * inverse for w in weights]
            dots = sum(jnp.sum(w * g, axis=0, keepdims=True) for w, g in zip(weights, grads))
            grad_low = [(w * (g - dots)).astype(BF16) for w, g in zip(weights, grads)]
            lows.append(([w.astype(BF16) for w in weights], grad_low))
        for (group, query, grad, pair, block_keys, _, _), (weights_low, grad_low) in zip(state, lows):
            terms = [(matmul(w, grad, (1, 0)), matmul(g, query, (1, 0))) for w, g in zip(weights_low, grad_low)]
            both = sum(matmul(g, k, (0, 0)) for g, k in zip(grad_low, block_keys)) * scale
            back = jnp.concatenate([both[:GROUP, :DH], both[GROUP:, DH:]], axis=1)
            back = pltpu.roll(back, GROUP - 1, 0)
            for j, (value_term, key_term) in zip(pair, terms):
                value_sum[j] += value_term
                key_sum[j] += key_term
            gq_ref[group // 2, pl.ds((group % 2) * GROUP, GROUP), :] = jnp.where(
                row == GROUP - 1, back, held[...]
            ).astype(BF16)
            held[...] = back
        return carry

    lax.fori_loop(0, groups // unroll, steps, 0)
    copies = [pltpu.make_async_copy(gq_ref, gq_out, gq_sem)]
    copies[0].start()
    for k in (2, 1, 3, 0):
        for i, (send, total, back_rows, out, factor) in enumerate(
            ((key_send, key_sum, key_back, key_out, scale),
             (value_send, value_sum, value_back, value_out, 1.0))
        ):

            def give(n, carry):
                slot = k * most + n
                j = back_rows[slot]

                @pl.when(j >= 0)
                def _():
                    send[slot] = (total[jnp.maximum(j, 0)] * factor).astype(BF16)

                return carry

            lax.fori_loop(0, most, give, 0)
            copy = pltpu.make_async_copy(
                send.at[pl.ds(k * most, most)], out[k], out_sems.at[i, k]
            )
            copy.start()
            copies.append(copy)
    for copy in copies:
        copy.wait()


def attend(ids, refs, tokens, keys, values, owned, most):
    parts, _, part_tokens, width = tokens.shape
    nbr = keys[0].shape[1]
    distinct = ids.shape[1]
    groups = refs.shape[1]
    flat = refs.reshape(refs.shape[0], -1)
    pool = pltpu.VMEM((SIDE * most, nbr, width), BF16)
    total = pltpu.VMEM((distinct, nbr, width), F32)
    rows = pltpu.VMEM((GROUP, width), F32)
    table = pltpu.SMEM((distinct,), jnp.int32)
    reverse = pltpu.SMEM((SIDE * most,), jnp.int32)
    shapes = (jax.ShapeDtypeStruct((parts, part_tokens, width), BF16),) + chunk_shapes(
        most, nbr, width
    ) * 2
    constrain = lambda value: pltpu.with_memory_space_constraint(value, pltpu.MemorySpace.HBM)
    keys, values = jax.tree.map(constrain, (list(keys), list(values)))
    out = pl.pallas_call(
        functools.partial(attend_body, groups, distinct, owned, most, 8),
        out_shape=tuple(pltpu.HBM(shape.shape, shape.dtype) for shape in shapes),
        in_specs=[SMEM, SMEM, VMEM] + [HBM] * 8,
        out_specs=(HBM,) * 9,
        scratch_shapes=[pool, pool, total, total, pltpu.VMEM((parts, part_tokens, width), BF16),
                        pool, pool, rows, rows, rows, table, table, reverse, reverse,
                        pltpu.SMEM((2 * SIDE,), jnp.int32),
                        pltpu.SemaphoreType.DMA((2, SIDE)), pltpu.SemaphoreType.DMA((2, SIDE)),
                        pltpu.SemaphoreType.DMA],
        compiler_params=pltpu.CompilerParams(vmem_limit_bytes=ATTEND_VMEM),
    )(ids, flat, tokens, *keys, *values)
    return (out[0], out[1:5], out[5:])


def collect_body(*refs):
    for i, out in enumerate(refs[8:]):
        own, *others = refs[4 * i : 4 * i + 4]
        for n in range(own.shape[0]):
            value = own[n]
            for other in others:
                value += other[n].astype(F32)
            out[n] = value.astype(BF16)


def collect(keys, values):
    out = jax.ShapeDtypeStruct(keys[0].shape, BF16)
    return pl.pallas_call(
        collect_body,
        out_shape=(out, out),
        in_specs=[VMEM] * 8,
        out_specs=(VMEM, VMEM),
        compiler_params=pltpu.CompilerParams(vmem_limit_bytes=COLLECT_VMEM),
    )(*keys, *values)


def on_device(queries, grad_out, neighbour_keys, neighbour_values, distinct_ids, group_refs):
    parts = lax.axis_size("ctx")
    owned = neighbour_keys.shape[0]
    most = SIDE * (owned // 2)
    take, add = tables(distinct_ids, owned, most)
    lines = gather_lines(((neighbour_keys, "x"), (neighbour_values, "y")))
    packed = pack_heads(queries[0], grad_out[0], parts)
    tokens = lax.all_to_all(packed, "ctx", split_axis=0, concat_axis=0, tiled=True)
    keys, values = select(take, *lines, most)
    keys, values = exchange_lines(((keys, "y", 1), (values, "x", 1)))
    back, keys, values = attend(distinct_ids, group_refs, tokens, keys, values, owned, most)
    keys, values = exchange_lines(((keys, "y", -1), (values, "x", -1)))
    back = lax.all_to_all(back, "ctx", split_axis=0, concat_axis=0, tiled=True)
    keys, values = spread(add, keys, values, owned)
    keys, values = exchange_lines(((keys, "x", 1), (values, "y", 1)))
    grad_queries = join_heads(back)[None]
    grad_queries, keys, values = lax.optimization_barrier((grad_queries, keys, values))
    grad_keys, grad_values = collect(keys, values)
    return (grad_queries, grad_keys, grad_values)


def solution(mesh):
    return jax.shard_map(
        on_device,
        mesh=mesh,
        in_specs=(
            P("dp", "ctx", None),
            P("dp", "ctx", None),
            P("dp", None, "ctx"),
            P("dp", None, "ctx"),
            P(),
            P(),
        ),
        out_specs=(P("dp", "ctx", None), P("dp", None, "ctx"), P("dp", None, "ctx")),
        check_vma=False,
    )
```

```python
import functools
import math

import jax
import jax.numpy as jnp
from jax import lax
from jax.experimental import pallas as pl
from jax.experimental.pallas import tpu as pltpu
from jax.sharding import PartitionSpec as P

DH = 128
GROUP = 64
BF16 = jnp.bfloat16
F32 = jnp.float32
HBM = pl.BlockSpec(memory_space=pltpu.MemorySpace.HBM)
VMEM = pl.BlockSpec(memory_space=pltpu.VMEM)
SMEM = pl.BlockSpec(memory_space=pltpu.SMEM)
SELECT_VMEM = 10 * 1024 * 1024
SPREAD_VMEM = 8 * 1024 * 1024
ATTEND_VMEM = 20 * 1024 * 1024
COLLECT_VMEM = 8 * 1024 * 1024


SIDE = 4


def place(n, owned):
    owner = lax.div(n, owned)
    return (lax.div(owner, SIDE), lax.rem(owner, SIDE), lax.rem(n, owned))


def shift(value, axis, amount):
    pairs = []
    for y in range(SIDE):
        for x in range(SIDE):
            to = (y, (x + amount) % SIDE) if axis == "x" else ((y + amount) % SIDE, x)
            pairs.append((y * SIDE + x, to[0] * SIDE + to[1]))
    return lax.ppermute(value, "dp", pairs)


def exchange_lines(lines):
    parts = [list(chunks) for chunks, _, _ in lines]
    for n, distances in ((0, (2, 1, 3)), (1, (1, 3, 2))):
        chunks, axis, sign = lines[n]
        for distance in distances:
            value = chunks[distance]
            if n == 1 and distance == 2:
                value, parts[n][1] = lax.optimization_barrier((value, parts[n][1]))
            parts[n][distance] = shift(value, axis, sign * distance)
    return parts


def gather_lines(keys, values):
    return exchange_lines((((keys,) * SIDE, "x", -1), ((values,) * SIDE, "y", -1)))


def chunk_shapes(most, nbr, width, own_type=BF16):
    return tuple(
        jax.ShapeDtypeStruct((most, nbr, width), own_type if k == 0 else BF16) for k in range(SIDE)
    )


def pack_heads_body(parts, width, q_ref, g_ref, out_ref, sems):
    copies = []
    for i, ref in enumerate((q_ref, g_ref)):
        for j in range(parts):
            copies.append(
                pltpu.make_async_copy(
                    ref.at[:, pl.ds(j * width, width)], out_ref.at[j, i], sems.at[i, j]
                )
            )
    for copy in copies:
        copy.start()
    for copy in copies:
        copy.wait()


def pack_heads(queries, grad_out, parts):
    tokens, features = queries.shape
    width = features // parts
    return pl.pallas_call(
        functools.partial(pack_heads_body, parts, width),
        out_shape=jax.ShapeDtypeStruct((parts, 2, tokens, width), BF16),
        in_specs=[HBM, HBM],
        out_specs=VMEM,
        scratch_shapes=[pltpu.SemaphoreType.DMA((2, parts))],
    )(queries, grad_out)


def join_heads_body(parts, width, in_ref, out_ref, sems):
    copies = [
        pltpu.make_async_copy(in_ref.at[j], out_ref.at[:, pl.ds(j * width, width)], sems.at[j])
        for j in range(parts)
    ]
    for copy in copies:
        copy.start()
    for copy in copies:
        copy.wait()


def join_heads(blocks):
    parts, tokens, width = blocks.shape
    return pl.pallas_call(
        functools.partial(join_heads_body, parts, width),
        out_shape=jax.ShapeDtypeStruct((tokens, parts * width), BF16),
        in_specs=[VMEM],
        out_specs=HBM,
        scratch_shapes=[pltpu.SemaphoreType.DMA((parts,))],
    )(blocks)


def matmul(a, b, contract):
    return lax.dot_general(a, b, ((contract[:1], contract[1:]), ((), ())), preferred_element_type=F32)


def block_diagonal(rows):
    zero = jnp.zeros((rows.shape[0], DH), BF16)
    return jnp.concatenate(
        [
            jnp.concatenate([rows[:, :DH], zero], axis=1),
            jnp.concatenate([zero, rows[:, DH:]], axis=1),
        ],
        axis=0,
    )


def tables_body(owned, most, ids_ref, take_ref, add_ref):
    me = lax.axis_index("dp")
    mine = (lax.div(me, SIDE), lax.rem(me, SIDE))
    distinct = ids_ref.shape[1]
    for across in range(2):
        for n in range(SIDE * most):
            take_ref[across, n] = 0
        for n in range(SIDE * owned * SIDE):
            add_ref[across, n] = -1
        for k in range(SIDE):
            other = lax.rem(mine[across] + k, SIDE)
            replica = other * SIDE + mine[1] if across == 0 else mine[0] * SIDE + other

            def step(j, count):
                where = place(ids_ref[replica, j], owned)
                found = where[across] == mine[across]

                @pl.when(found)
                def _():
                    distance = lax.rem(where[1 - across] - mine[1 - across] + SIDE, SIDE)
                    row = distance * owned + where[2]
                    take_ref[across, k * most + count] = row
                    add_ref[across, row * SIDE + k] = count

                return count + found.astype(jnp.int32)

            lax.fori_loop(0, distinct, step, jnp.int32(0))


def tables(ids, owned, most):
    return pl.pallas_call(
        functools.partial(tables_body, owned, most),
        out_shape=(
            jax.ShapeDtypeStruct((2, SIDE * most), jnp.int32),
            jax.ShapeDtypeStruct((2, SIDE * owned * SIDE), jnp.int32),
        ),
        in_specs=[SMEM],
        out_specs=(SMEM, SMEM),
    )(ids)


def select_body(take_ref, *refs):
    lines, kept, sems = refs[16:18], refs[18:20], refs[20]
    copies = []
    for across in range(2):
        parts = refs[4 * across : 4 * across + 4]
        line = lines[across]
        owned = parts[0].shape[0]
        for k, part in enumerate(parts):
            for n in range(owned):
                line[k * owned + n] = part[n]
        own, *sent = refs[8 + 4 * across : 12 + 4 * across]
        most = own.shape[0]

        def pick(n, carry):
            kept[across][n] = line[take_ref[across, n]]
            for k, out in enumerate(sent):
                out[n] = line[take_ref[across, (k + 1) * most + n]]
            return carry

        lax.fori_loop(0, most, pick, 0, unroll=2)
        copies.append(pltpu.make_async_copy(kept[across], own, sems.at[across]))
        copies[-1].start()
    for copy in copies:
        copy.wait()


def select(take, keys, values, most):
    owned, nbr, width = keys[0].shape
    line = pltpu.VMEM((SIDE * owned, nbr, width), BF16)
    kept = pltpu.VMEM((most, nbr, width), BF16)
    shapes = chunk_shapes(most, nbr, width)
    out = pl.pallas_call(
        select_body,
        out_shape=((pltpu.HBM(shapes[0].shape, BF16),) + shapes[1:]) * 2,
        in_specs=[SMEM] + [VMEM] * 8,
        out_specs=((HBM,) + (VMEM,) * 3) * 2,
        scratch_shapes=[line, line, kept, kept, pltpu.SemaphoreType.DMA((2,))],
        compiler_params=pltpu.CompilerParams(vmem_limit_bytes=SELECT_VMEM),
    )(take, *keys, *values)
    return (out[:4], out[4:])


def spread_body(add_ref, *refs):
    for across in range(2):
        chunks = refs[4 * across : 4 * across + 4]
        outs = refs[8 + 4 * across : 12 + 4 * across]
        most, owned = chunks[0].shape[0], outs[0].shape[0]

        def add(n, carry):
            for distance, out in enumerate(outs):
                value = jnp.zeros(out.shape[1:], F32)
                for k, chunk in enumerate(chunks):
                    index = add_ref[across, (distance * owned + n) * SIDE + k]
                    term = chunk[jnp.clip(index, 0, most - 1)].astype(F32)
                    value += jnp.where(index >= 0, term, 0.0)
                out[n] = value.astype(out.dtype)
            return carry

        lax.fori_loop(0, owned, add, 0)


def spread(add, keys, values, owned):
    _, nbr, width = keys[0].shape
    out = pl.pallas_call(
        spread_body,
        out_shape=chunk_shapes(owned, nbr, width, F32) * 2,
        in_specs=[SMEM] + [VMEM] * 8,
        out_specs=(VMEM,) * 8,
        compiler_params=pltpu.CompilerParams(vmem_limit_bytes=SPREAD_VMEM),
    )(add, *keys, *values)
    return (out[:4], out[4:])


def attend_body(
    groups, distinct, owned, most, unroll, ids_ref, refs_ref, tokens_ref, *refs
):
    key_parts, value_parts = refs[:4], refs[4:8]
    gq_out, key_out, value_out = refs[8], refs[9:13], refs[13:17]
    (keys, values, key_sum, value_sum, gq_ref, key_send, value_send, query_last, grad_last, held,
     key_rows, value_rows, key_back, value_back, counts, in_sems, out_sems, gq_sem) = refs[17:]
    scale = 1.0 / math.sqrt(DH)
    copies = [
        pltpu.make_async_copy(part, pool.at[pl.ds(k * most, most)], in_sems.at[i, k])
        for i, (parts, pool) in enumerate(((key_parts, keys), (value_parts, values)))
        for k, part in enumerate(parts)
    ]
    for copy in copies:
        copy.start()

    def clear(j, carry):
        key_sum[j] = jnp.zeros(key_sum.shape[1:], F32)
        value_sum[j] = jnp.zeros(value_sum.shape[1:], F32)
        return carry

    lax.fori_loop(0, distinct, clear, 0)
    width = gq_ref.shape[2]
    row = lax.broadcasted_iota(jnp.int32, (GROUP, width), 0)
    me = lax.axis_index("dp")
    mine = (me // SIDE, me % SIDE)
    for i in range(2 * SIDE):
        counts[i] = 0
    for n in range(SIDE * most):
        key_back[n] = -1
        value_back[n] = -1

    def rank(j, carry):
        where = place(ids_ref[me, j], owned)
        for i, (table, back_rows) in enumerate(
            ((key_rows, key_back), (value_rows, value_back))
        ):
            distance = (mine[i] - where[i] + SIDE) % SIDE
            count = counts[i * SIDE + distance]
            table[j] = distance * most + count
            back_rows[distance * most + count] = j
            counts[i * SIDE + distance] = count + 1
        return carry

    lax.fori_loop(0, distinct, rank, 0)

    def rolled(kind, block):
        part = tokens_ref[block // 2, kind, pl.ds((block % 2) * GROUP, GROUP), :]
        return pltpu.roll(part.astype(F32), 1, 0)

    held[...] = jnp.zeros_like(held)
    query_last[...] = rolled(0, 0)
    grad_last[...] = rolled(1, 0)
    for copy in copies:
        copy.wait()

    def shifted(kind, group, last):
        following = rolled(kind, jnp.minimum(group + 1, groups - 1))
        following = jnp.where(group + 1 < groups, following, 0.0)
        block = jnp.where(row == 0, last[...], following)
        last[...] = following
        return block_diagonal(block.astype(BF16))

    def steps(index, carry):
        batch = [index * unroll + u for u in range(unroll)]
        state = []
        for group in batch:
            query = shifted(0, group, query_last)
            grad = shifted(1, group, grad_last)
            pair = (refs_ref[me, 2 * group], refs_ref[me, 2 * group + 1])
            block_keys = [keys[key_rows[j]] for j in pair]
            scores = [matmul(k, query, (1, 1)) for k in block_keys]
            grads = [matmul(values[value_rows[j]], grad, (1, 1)) for j in pair]
            state.append((group, query, grad, pair, block_keys, scores, grads))
        lows = []
        for group, query, grad, pair, block_keys, scores, grads in state:
            top = jnp.maximum(*[jnp.max(s, axis=0, keepdims=True) for s in scores])
            weights = [jnp.exp2((s - top) * (scale * math.log2(math.e))) for s in scores]
            total = sum(jnp.sum(w, axis=0, keepdims=True) for w in weights)
            inverse = 1.0 / total
            weights = [w * inverse for w in weights]
            dots = sum(jnp.sum(w * g, axis=0, keepdims=True) for w, g in zip(weights, grads))
            grad_low = [(w * (g - dots)).astype(BF16) for w, g in zip(weights, grads)]
            lows.append(([w.astype(BF16) for w in weights], grad_low))
        for (group, query, grad, pair, block_keys, _, _), (weights_low, grad_low) in zip(state, lows):
            terms = [(matmul(w, grad, (1, 0)), matmul(g, query, (1, 0))) for w, g in zip(weights_low, grad_low)]
            both = sum(matmul(g, k, (0, 0)) for g, k in zip(grad_low, block_keys)) * scale
            back = jnp.concatenate([both[:GROUP, :DH], both[GROUP:, DH:]], axis=1)
            back = pltpu.roll(back, GROUP - 1, 0)
            for j, (value_term, key_term) in zip(pair, terms):
                value_sum[j] += value_term
                key_sum[j] += key_term
            gq_ref[group // 2, pl.ds((group % 2) * GROUP, GROUP), :] = jnp.where(
                row == GROUP - 1, back, held[...]
            ).astype(BF16)
            held[...] = back
        return carry

    lax.fori_loop(0, groups // unroll, steps, 0)
    copies = [pltpu.make_async_copy(gq_ref, gq_out, gq_sem)]
    copies[0].start()
    for k in (2, 1, 3, 0):
        for i, (send, total, back_rows, out, factor) in enumerate(
            ((key_send, key_sum, key_back, key_out, scale),
             (value_send, value_sum, value_back, value_out, 1.0))
        ):

            def give(n, carry):
                slot = k * most + n
                j = back_rows[slot]

                @pl.when(j >= 0)
                def _():
                    send[slot] = (total[jnp.maximum(j, 0)] * factor).astype(BF16)

                return carry

            lax.fori_loop(0, most, give, 0)
            copy = pltpu.make_async_copy(
                send.at[pl.ds(k * most, most)], out[k], out_sems.at[i, k]
            )
            copy.start()
            copies.append(copy)
    for copy in copies:
        copy.wait()


def attend(ids, refs, tokens, keys, values, owned, most):
    parts, _, part_tokens, width = tokens.shape
    nbr = keys[0].shape[1]
    distinct = ids.shape[1]
    groups = refs.shape[1]
    flat = refs.reshape(refs.shape[0], -1)
    pool = pltpu.VMEM((SIDE * most, nbr, width), BF16)
    total = pltpu.VMEM((distinct, nbr, width), F32)
    rows = pltpu.VMEM((GROUP, width), F32)
    table = pltpu.SMEM((distinct,), jnp.int32)
    reverse = pltpu.SMEM((SIDE * most,), jnp.int32)
    shapes = (jax.ShapeDtypeStruct((parts, part_tokens, width), BF16),) + chunk_shapes(
        most, nbr, width
    ) * 2
    constrain = lambda value: pltpu.with_memory_space_constraint(value, pltpu.MemorySpace.HBM)
    keys, values = jax.tree.map(constrain, (list(keys), list(values)))
    out = pl.pallas_call(
        functools.partial(attend_body, groups, distinct, owned, most, 8),
        out_shape=tuple(pltpu.HBM(shape.shape, shape.dtype) for shape in shapes),
        in_specs=[SMEM, SMEM, VMEM] + [HBM] * 8,
        out_specs=(HBM,) * 9,
        scratch_shapes=[pool, pool, total, total, pltpu.VMEM((parts, part_tokens, width), BF16),
                        pool, pool, rows, rows, rows, table, table, reverse, reverse,
                        pltpu.SMEM((2 * SIDE,), jnp.int32),
                        pltpu.SemaphoreType.DMA((2, SIDE)), pltpu.SemaphoreType.DMA((2, SIDE)),
                        pltpu.SemaphoreType.DMA],
        compiler_params=pltpu.CompilerParams(vmem_limit_bytes=ATTEND_VMEM),
    )(ids, flat, tokens, *keys, *values)
    return (out[0], out[1:5], out[5:])


def collect_body(*refs):
    for i, out in enumerate(refs[8:]):
        own, *others = refs[4 * i : 4 * i + 4]
        for n in range(own.shape[0]):
            value = own[n]
            for other in others:
                value += other[n].astype(F32)
            out[n] = value.astype(BF16)


def collect(keys, values):
    out = jax.ShapeDtypeStruct(keys[0].shape, BF16)
    return pl.pallas_call(
        collect_body,
        out_shape=(out, out),
        in_specs=[VMEM] * 8,
        out_specs=(VMEM, VMEM),
        compiler_params=pltpu.CompilerParams(vmem_limit_bytes=COLLECT_VMEM),
    )(*keys, *values)


def on_device(queries, grad_out, neighbour_keys, neighbour_values, distinct_ids, group_refs):
    parts = lax.axis_size("ctx")
    owned = neighbour_keys.shape[0]
    most = SIDE * (owned // 2)
    take, add = tables(distinct_ids, owned, most)
    lines = gather_lines(neighbour_keys, neighbour_values)
    packed = pack_heads(queries[0], grad_out[0], parts)
    tokens = lax.all_to_all(packed, "ctx", split_axis=0, concat_axis=0, tiled=True)
    keys, values = select(take, *lines, most)
    keys, values = exchange_lines(((keys, "y", 1), (values, "x", 1)))
    back, keys, values = attend(distinct_ids, group_refs, tokens, keys, values, owned, most)
    keys, values = exchange_lines(((keys, "y", -1), (values, "x", -1)))
    back = lax.all_to_all(back, "ctx", split_axis=0, concat_axis=0, tiled=True)
    keys, values = spread(add, keys, values, owned)
    keys, values = exchange_lines(((keys, "x", 1), (values, "y", 1)))
    grad_queries = join_heads(back)[None]
    grad_queries, keys, values = lax.optimization_barrier((grad_queries, keys, values))
    grad_keys, grad_values = collect(keys, values)
    return (grad_queries, grad_keys, grad_values)


def solution(mesh):
    return jax.shard_map(
        on_device,
        mesh=mesh,
        in_specs=(
            P("dp", "ctx", None),
            P("dp", "ctx", None),
            P("dp", None, "ctx"),
            P("dp", None, "ctx"),
            P(),
            P(),
        ),
        out_specs=(P("dp", "ctx", None), P("dp", None, "ctx"), P("dp", None, "ctx")),
        check_vma=False,
    )
```

```python
import functools
import math

import jax
import jax.numpy as jnp
from jax import lax
from jax.experimental import pallas as pl
from jax.experimental.pallas import tpu as pltpu
from jax.sharding import PartitionSpec as P

DH = 128
GROUP = 64
BF16 = jnp.bfloat16
F32 = jnp.float32
HBM = pl.BlockSpec(memory_space=pltpu.MemorySpace.HBM)
VMEM = pl.BlockSpec(memory_space=pltpu.VMEM)
SMEM = pl.BlockSpec(memory_space=pltpu.SMEM)
SELECT_VMEM = 10 * 1024 * 1024
SPREAD_VMEM = 8 * 1024 * 1024
ATTEND_VMEM = 20 * 1024 * 1024
COLLECT_VMEM = 8 * 1024 * 1024


SIDE = 4


def place(n, owned):
    owner = lax.div(n, owned)
    return (lax.div(owner, SIDE), lax.rem(owner, SIDE), lax.rem(n, owned))


def shift(value, axis, amount):
    pairs = []
    for y in range(SIDE):
        for x in range(SIDE):
            to = (y, (x + amount) % SIDE) if axis == "x" else ((y + amount) % SIDE, x)
            pairs.append((y * SIDE + x, to[0] * SIDE + to[1]))
    return lax.ppermute(value, "dp", pairs)


def exchange_lines(lines):
    parts = [list(chunks) for chunks, _, _ in lines]
    for n, distances in ((0, (2, 1, 3)), (1, (1, 3, 2))):
        chunks, axis, sign = lines[n]
        for distance in distances:
            value = chunks[distance]
            if n == 1 and distance == 2:
                value, parts[n][1] = lax.optimization_barrier((value, parts[n][1]))
            parts[n][distance] = shift(value, axis, sign * distance)
    return parts


def gather_lines(keys, values):
    return exchange_lines((((keys,) * SIDE, "x", -1), ((values,) * SIDE, "y", -1)))


def chunk_shapes(most, nbr, width, own_type=BF16):
    return tuple(
        jax.ShapeDtypeStruct((most, nbr, width), own_type if k == 0 else BF16) for k in range(SIDE)
    )


def pack_heads_body(parts, width, q_ref, g_ref, out_ref, held, in_sems, out_sems):
    arrivals = []
    for j in range(parts):
        for i, ref in enumerate((q_ref, g_ref)):
            copy = pltpu.make_async_copy(
                ref.at[:, pl.ds(j * width, width)], held.at[j, i], in_sems.at[j, i]
            )
            copy.start()
            arrivals.append(copy)
    departures = []
    for j in range(parts):
        for copy in arrivals[2 * j : 2 * j + 2]:
            copy.wait()
        departures.append(pltpu.make_async_copy(held.at[j], out_ref.at[j], out_sems.at[j]))
        departures[-1].start()
    for copy in departures:
        copy.wait()


def pack_heads(queries, grad_out, parts):
    tokens, features = queries.shape
    width = features // parts
    shape = (parts, 2, tokens, width)
    return pl.pallas_call(
        functools.partial(pack_heads_body, parts, width),
        out_shape=pltpu.HBM(shape, BF16),
        in_specs=[HBM, HBM],
        out_specs=HBM,
        scratch_shapes=[
            pltpu.VMEM(shape, BF16),
            pltpu.SemaphoreType.DMA((parts, 2)),
            pltpu.SemaphoreType.DMA((parts,)),
        ],
    )(queries, grad_out)


def join_heads_body(parts, width, in_ref, out_ref, sems):
    copies = [
        pltpu.make_async_copy(in_ref.at[j], out_ref.at[:, pl.ds(j * width, width)], sems.at[j])
        for j in range(parts)
    ]
    for copy in copies:
        copy.start()
    for copy in copies:
        copy.wait()


def join_heads(blocks):
    parts, tokens, width = blocks.shape
    return pl.pallas_call(
        functools.partial(join_heads_body, parts, width),
        out_shape=jax.ShapeDtypeStruct((tokens, parts * width), BF16),
        in_specs=[VMEM],
        out_specs=HBM,
        scratch_shapes=[pltpu.SemaphoreType.DMA((parts,))],
    )(blocks)


def matmul(a, b, contract):
    return lax.dot_general(a, b, ((contract[:1], contract[1:]), ((), ())), preferred_element_type=F32)


def block_diagonal(rows):
    zero = jnp.zeros((rows.shape[0], DH), BF16)
    return jnp.concatenate(
        [
            jnp.concatenate([rows[:, :DH], zero], axis=1),
            jnp.concatenate([zero, rows[:, DH:]], axis=1),
        ],
        axis=0,
    )


def tables_body(owned, most, ids_ref, take_ref, add_ref):
    me = lax.axis_index("dp")
    mine = (lax.div(me, SIDE), lax.rem(me, SIDE))
    distinct = ids_ref.shape[1]
    for across in range(2):
        for n in range(SIDE * most):
            take_ref[across, n] = 0
        for n in range(SIDE * owned * SIDE):
            add_ref[across, n] = -1
        for k in range(SIDE):
            other = lax.rem(mine[across] + k, SIDE)
            replica = other * SIDE + mine[1] if across == 0 else mine[0] * SIDE + other

            def step(j, count):
                where = place(ids_ref[replica, j], owned)
                found = where[across] == mine[across]

                @pl.when(found)
                def _():
                    distance = lax.rem(where[1 - across] - mine[1 - across] + SIDE, SIDE)
                    row = distance * owned + where[2]
                    take_ref[across, k * most + count] = row
                    add_ref[across, row * SIDE + k] = count + (other if across == 0 else k) * most

                return count + found.astype(jnp.int32)

            lax.fori_loop(0, distinct, step, jnp.int32(0))


def tables(ids, owned, most):
    return pl.pallas_call(
        functools.partial(tables_body, owned, most),
        out_shape=(
            jax.ShapeDtypeStruct((2, SIDE * most), jnp.int32),
            jax.ShapeDtypeStruct((2, SIDE * owned * SIDE), jnp.int32),
        ),
        in_specs=[SMEM],
        out_specs=(SMEM, SMEM),
    )(ids)


def select_body(take_ref, *refs):
    lines, kept, sems = refs[16:18], refs[18:20], refs[20]
    copies = []
    for across in range(2):
        parts = refs[4 * across : 4 * across + 4]
        line = lines[across]
        owned = parts[0].shape[0]
        for k, part in enumerate(parts):
            for n in range(owned):
                line[k * owned + n] = part[n]
        own, *sent = refs[8 + 4 * across : 12 + 4 * across]
        most = own.shape[0]

        def pick(n, carry):
            kept[across][n] = line[take_ref[across, n]]
            for k, out in enumerate(sent):
                out[n] = line[take_ref[across, (k + 1) * most + n]]
            return carry

        lax.fori_loop(0, most, pick, 0, unroll=2)
        copies.append(pltpu.make_async_copy(kept[across], own, sems.at[across]))
        copies[-1].start()
    for copy in copies:
        copy.wait()


def select(take, keys, values, most):
    owned, nbr, width = keys[0].shape
    line = pltpu.VMEM((SIDE * owned, nbr, width), BF16)
    kept = pltpu.VMEM((most, nbr, width), BF16)
    shapes = chunk_shapes(most, nbr, width)
    out = pl.pallas_call(
        select_body,
        out_shape=((pltpu.HBM(shapes[0].shape, BF16),) + shapes[1:]) * 2,
        in_specs=[SMEM] + [VMEM] * 8,
        out_specs=((HBM,) + (VMEM,) * 3) * 2,
        scratch_shapes=[line, line, kept, kept, pltpu.SemaphoreType.DMA((2,))],
        compiler_params=pltpu.CompilerParams(vmem_limit_bytes=SELECT_VMEM),
    )(take, *keys, *values)
    return (out[:4], out[4:])


def spread_body(add_ref, key_ref, *refs):
    value_refs, key_outs, value_outs, (pool, sems) = refs[:4], refs[4:8], refs[8:12], refs[12:]
    most = value_refs[0].shape[0]
    copies = [
        pltpu.make_async_copy(ref, pool.at[pl.ds(k * most, most)], sems.at[k])
        for k, ref in enumerate(value_refs)
    ]
    for copy in copies:
        copy.start()
    for across, terms, outs in ((0, key_ref, key_outs), (1, pool, value_outs)):
        owned = outs[0].shape[0]
        if across == 1:
            for copy in copies:
                copy.wait()

        def add(n, carry):
            for distance, out in enumerate(outs):
                value = jnp.zeros(out.shape[1:], F32)
                for k in range(SIDE):
                    index = add_ref[across, (distance * owned + n) * SIDE + k]
                    term = terms[jnp.maximum(index, 0)].astype(F32)
                    value += jnp.where(index >= 0, term, 0.0)
                out[n] = value.astype(out.dtype)
            return carry

        lax.fori_loop(0, owned, add, 0)


def in_hbm(values):
    return [pltpu.with_memory_space_constraint(v, pltpu.MemorySpace.HBM) for v in values]


def spread(add, keys, values, owned):
    rows, nbr, width = keys.shape
    out = pl.pallas_call(
        spread_body,
        out_shape=chunk_shapes(owned, nbr, width, F32) * 2,
        in_specs=[SMEM, VMEM] + [HBM] * 4,
        out_specs=(VMEM,) * 8,
        scratch_shapes=[pltpu.VMEM((rows, nbr, width), BF16), pltpu.SemaphoreType.DMA((SIDE,))],
        compiler_params=pltpu.CompilerParams(vmem_limit_bytes=SPREAD_VMEM),
    )(add, keys, *in_hbm(values))
    return (out[:4], out[4:])


def attend_body(
    groups, distinct, owned, most, unroll, ids_ref, refs_ref, tokens_ref, *refs
):
    key_parts, value_parts = refs[:4], refs[4:8]
    gq_out, key_all, value_out = refs[8], refs[9], refs[10:14]
    key_out = [key_all.at[pl.ds(k * most, most)] for k in range(SIDE)]
    (keys, values, key_sum, value_sum, gq_ref, key_send, value_send, query_last, grad_last, held,
     key_rows, value_rows, key_back, value_back, counts, in_sems, out_sems, gq_sem) = refs[14:]
    scale = 1.0 / math.sqrt(DH)
    copies = [
        pltpu.make_async_copy(part, pool.at[pl.ds(k * most, most)], in_sems.at[i, k])
        for i, (parts, pool) in enumerate(((key_parts, keys), (value_parts, values)))
        for k, part in enumerate(parts)
    ]
    for copy in copies:
        copy.start()

    def clear(j, carry):
        key_sum[j] = jnp.zeros(key_sum.shape[1:], F32)
        value_sum[j] = jnp.zeros(value_sum.shape[1:], F32)
        return carry

    lax.fori_loop(0, distinct, clear, 0)
    width = gq_ref.shape[2]
    row = lax.broadcasted_iota(jnp.int32, (GROUP, width), 0)
    me = lax.axis_index("dp")
    mine = (me // SIDE, me % SIDE)
    for i in range(2 * SIDE):
        counts[i] = 0
    for n in range(SIDE * most):
        key_back[n] = -1
        value_back[n] = -1

    def rank(j, carry):
        where = place(ids_ref[me, j], owned)
        for i, (table, back_rows) in enumerate(
            ((key_rows, key_back), (value_rows, value_back))
        ):
            distance = (mine[i] - where[i] + SIDE) % SIDE
            count = counts[i * SIDE + distance]
            table[j] = distance * most + count
            back_rows[(where[0] if i == 0 else distance) * most + count] = j
            counts[i * SIDE + distance] = count + 1
        return carry

    lax.fori_loop(0, distinct, rank, 0)

    def rolled(kind, block):
        part = tokens_ref[block // 2, kind, pl.ds((block % 2) * GROUP, GROUP), :]
        return pltpu.roll(part.astype(F32), 1, 0)

    held[...] = jnp.zeros_like(held)
    query_last[...] = rolled(0, 0)
    grad_last[...] = rolled(1, 0)
    for copy in copies:
        copy.wait()

    def shifted(kind, group, last):
        following = rolled(kind, jnp.minimum(group + 1, groups - 1))
        following = jnp.where(group + 1 < groups, following, 0.0)
        block = jnp.where(row == 0, last[...], following)
        last[...] = following
        return block_diagonal(block.astype(BF16))

    def steps(index, carry):
        batch = [index * unroll + u for u in range(unroll)]
        state = []
        for group in batch:
            query = shifted(0, group, query_last)
            grad = shifted(1, group, grad_last)
            pair = (refs_ref[me, 2 * group], refs_ref[me, 2 * group + 1])
            block_keys = [keys[key_rows[j]] for j in pair]
            scores = [matmul(k, query, (1, 1)) for k in block_keys]
            grads = [matmul(values[value_rows[j]], grad, (1, 1)) for j in pair]
            state.append((group, query, grad, pair, block_keys, scores, grads))
        lows = []
        for group, query, grad, pair, block_keys, scores, grads in state:
            top = jnp.maximum(*[jnp.max(s, axis=0, keepdims=True) for s in scores])
            weights = [jnp.exp2((s - top) * (scale * math.log2(math.e))) for s in scores]
            total = sum(jnp.sum(w, axis=0, keepdims=True) for w in weights)
            inverse = 1.0 / total
            weights = [w * inverse for w in weights]
            dots = sum(jnp.sum(w * g, axis=0, keepdims=True) for w, g in zip(weights, grads))
            grad_low = [(w * (g - dots)).astype(BF16) for w, g in zip(weights, grads)]
            lows.append(([w.astype(BF16) for w in weights], grad_low))
        for (group, query, grad, pair, block_keys, _, _), (weights_low, grad_low) in zip(state, lows):
            terms = [(matmul(w, grad, (1, 0)), matmul(g, query, (1, 0))) for w, g in zip(weights_low, grad_low)]
            both = sum(matmul(g, k, (0, 0)) for g, k in zip(grad_low, block_keys)) * scale
            back = jnp.concatenate([both[:GROUP, :DH], both[GROUP:, DH:]], axis=1)
            back = pltpu.roll(back, GROUP - 1, 0)
            for j, (value_term, key_term) in zip(pair, terms):
                value_sum[j] += value_term
                key_sum[j] += key_term
            gq_ref[group // 2, pl.ds((group % 2) * GROUP, GROUP), :] = jnp.where(
                row == GROUP - 1, back, held[...]
            ).astype(BF16)
            held[...] = back
        return carry

    lax.fori_loop(0, groups // unroll, steps, 0)
    copies = [pltpu.make_async_copy(gq_ref, gq_out, gq_sem)]
    copies[0].start()
    for k in (2, 1, 3, 0):
        for i, (send, total, back_rows, out, factor) in enumerate(
            ((key_send, key_sum, key_back, key_out, scale),
             (value_send, value_sum, value_back, value_out, 1.0))
        ):

            def give(n, carry):
                slot = k * most + n
                j = back_rows[slot]

                @pl.when(j >= 0)
                def _():
                    send[slot] = (total[jnp.maximum(j, 0)] * factor).astype(BF16)

                return carry

            lax.fori_loop(0, most, give, 0)
            copy = pltpu.make_async_copy(
                send.at[pl.ds(k * most, most)], out[k], out_sems.at[i, k]
            )
            copy.start()
            copies.append(copy)
    for copy in copies:
        copy.wait()


def attend(ids, refs, tokens, keys, values, owned, most):
    parts, _, part_tokens, width = tokens.shape
    nbr = keys[0].shape[1]
    distinct = ids.shape[1]
    groups = refs.shape[1]
    flat = refs.reshape(refs.shape[0], -1)
    pool = pltpu.VMEM((SIDE * most, nbr, width), BF16)
    total = pltpu.VMEM((distinct, nbr, width), F32)
    rows = pltpu.VMEM((GROUP, width), F32)
    table = pltpu.SMEM((distinct,), jnp.int32)
    reverse = pltpu.SMEM((SIDE * most,), jnp.int32)
    shapes = (
        jax.ShapeDtypeStruct((parts, part_tokens, width), BF16),
        jax.ShapeDtypeStruct((SIDE * most, nbr, width), BF16),
    ) + chunk_shapes(most, nbr, width)
    out = pl.pallas_call(
        functools.partial(attend_body, groups, distinct, owned, most, 8),
        out_shape=tuple(pltpu.HBM(shape.shape, shape.dtype) for shape in shapes),
        in_specs=[SMEM, SMEM, VMEM] + [HBM] * 8,
        out_specs=(HBM,) * 6,
        scratch_shapes=[pool, pool, total, total, pltpu.VMEM((parts, part_tokens, width), BF16),
                        pool, pool, rows, rows, rows, table, table, reverse, reverse,
                        pltpu.SMEM((2 * SIDE,), jnp.int32),
                        pltpu.SemaphoreType.DMA((2, SIDE)), pltpu.SemaphoreType.DMA((2, SIDE)),
                        pltpu.SemaphoreType.DMA],
        compiler_params=pltpu.CompilerParams(vmem_limit_bytes=ATTEND_VMEM),
    )(ids, flat, tokens, *in_hbm(keys), *in_hbm(values))
    return (out[0], out[1], out[2:])


def collect_body(*refs):
    for i, out in enumerate(refs[8:]):
        own, *others = refs[4 * i : 4 * i + 4]
        for n in range(own.shape[0]):
            value = own[n]
            for other in others:
                value += other[n].astype(F32)
            out[n] = value.astype(BF16)


def collect(keys, values):
    out = jax.ShapeDtypeStruct(keys[0].shape, BF16)
    return pl.pallas_call(
        collect_body,
        out_shape=(out, out),
        in_specs=[VMEM] * 8,
        out_specs=(VMEM, VMEM),
        compiler_params=pltpu.CompilerParams(vmem_limit_bytes=COLLECT_VMEM),
    )(*keys, *values)


def on_device(queries, grad_out, neighbour_keys, neighbour_values, distinct_ids, group_refs):
    parts = lax.axis_size("ctx")
    owned = neighbour_keys.shape[0]
    most = SIDE * (owned // 2)
    take, add = tables(distinct_ids, owned, most)
    lines = gather_lines(neighbour_keys, neighbour_values)
    packed = pack_heads(queries[0], grad_out[0], parts)
    tokens = lax.all_to_all(packed, "ctx", split_axis=0, concat_axis=0, tiled=True)
    keys, values = select(take, *lines, most)
    keys, values = exchange_lines(((keys, "y", 1), (values, "x", 1)))
    back, keys, values = attend(distinct_ids, group_refs, tokens, keys, values, owned, most)
    keys = lax.all_to_all(
        keys, "dp", split_axis=0, concat_axis=0, tiled=True,
        axis_index_groups=[[y * SIDE + x for y in range(SIDE)] for x in range(SIDE)],
    )
    values = (values[0],) + tuple(shift(values[k], "x", -k) for k in range(1, SIDE))
    back, keys, values = lax.optimization_barrier((back, keys, values))
    back = lax.all_to_all(back, "ctx", split_axis=0, concat_axis=0, tiled=True)
    keys, values = spread(add, keys, values, owned)
    keys, values = exchange_lines(((keys, "x", 1), (values, "y", 1)))
    grad_queries = join_heads(back)[None]
    grad_queries, keys, values = lax.optimization_barrier((grad_queries, keys, values))
    grad_keys, grad_values = collect(keys, values)
    return (grad_queries, grad_keys, grad_values)


def solution(mesh):
    return jax.shard_map(
        on_device,
        mesh=mesh,
        in_specs=(
            P("dp", "ctx", None),
            P("dp", "ctx", None),
            P("dp", None, "ctx"),
            P("dp", None, "ctx"),
            P(),
            P(),
        ),
        out_specs=(P("dp", "ctx", None), P("dp", None, "ctx"), P("dp", None, "ctx")),
        check_vma=False,
    )
```

```python
import functools
import math

import jax
import jax.numpy as jnp
from jax import lax
from jax.experimental import pallas as pl
from jax.experimental.pallas import tpu as pltpu
from jax.sharding import PartitionSpec as P

DH = 128
GROUP = 64
BF16 = jnp.bfloat16
F32 = jnp.float32
HBM = pl.BlockSpec(memory_space=pltpu.MemorySpace.HBM)
VMEM = pl.BlockSpec(memory_space=pltpu.VMEM)
SMEM = pl.BlockSpec(memory_space=pltpu.SMEM)
SELECT_VMEM = 10 * 1024 * 1024
SPREAD_VMEM = 12 * 1024 * 1024
SPREAD_FLOPS = 200_000_000_000
ATTEND_VMEM = 20 * 1024 * 1024
COLLECT_VMEM = 8 * 1024 * 1024


SIDE = 4


def place(n, owned):
    owner = lax.div(n, owned)
    return (lax.div(owner, SIDE), lax.rem(owner, SIDE), lax.rem(n, owned))


def shift(value, axis, amount):
    pairs = []
    for y in range(SIDE):
        for x in range(SIDE):
            to = (y, (x + amount) % SIDE) if axis == "x" else ((y + amount) % SIDE, x)
            pairs.append((y * SIDE + x, to[0] * SIDE + to[1]))
    return lax.ppermute(value, "dp", pairs)


def exchange_lines(lines):
    parts = [list(chunks) for chunks, _, _ in lines]
    for n, distances in ((0, (2, 1, 3)), (1, (1, 3, 2))):
        chunks, axis, sign = lines[n]
        for distance in distances:
            value = chunks[distance]
            if n == 1 and distance == 2:
                value, parts[n][1] = lax.optimization_barrier((value, parts[n][1]))
            parts[n][distance] = shift(value, axis, sign * distance)
    return parts


def gather_lines(keys, values):
    return exchange_lines((((keys,) * SIDE, "x", -1), ((values,) * SIDE, "y", -1)))


def chunk_shapes(most, nbr, width, own_type=BF16):
    return tuple(
        jax.ShapeDtypeStruct((most, nbr, width), own_type if k == 0 else BF16) for k in range(SIDE)
    )


def pack_heads_body(parts, width, q_ref, g_ref, out_ref, held, in_sems, out_sems):
    arrivals = []
    for j in range(parts):
        for i, ref in enumerate((q_ref, g_ref)):
            copy = pltpu.make_async_copy(
                ref.at[:, pl.ds(j * width, width)], held.at[j, i], in_sems.at[j, i]
            )
            copy.start()
            arrivals.append(copy)
    departures = []
    for j in range(parts):
        for copy in arrivals[2 * j : 2 * j + 2]:
            copy.wait()
        departures.append(pltpu.make_async_copy(held.at[j], out_ref.at[j], out_sems.at[j]))
        departures[-1].start()
    for copy in departures:
        copy.wait()


def pack_heads(queries, grad_out, parts):
    tokens, features = queries.shape
    width = features // parts
    shape = (parts, 2, tokens, width)
    return pl.pallas_call(
        functools.partial(pack_heads_body, parts, width),
        out_shape=pltpu.HBM(shape, BF16),
        in_specs=[HBM, HBM],
        out_specs=HBM,
        scratch_shapes=[
            pltpu.VMEM(shape, BF16),
            pltpu.SemaphoreType.DMA((parts, 2)),
            pltpu.SemaphoreType.DMA((parts,)),
        ],
    )(queries, grad_out)


def join_heads_body(parts, width, in_ref, out_ref, sems):
    copies = [
        pltpu.make_async_copy(in_ref.at[j], out_ref.at[:, pl.ds(j * width, width)], sems.at[j])
        for j in range(parts)
    ]
    for copy in copies:
        copy.start()
    for copy in copies:
        copy.wait()


def join_heads(blocks):
    parts, tokens, width = blocks.shape
    return pl.pallas_call(
        functools.partial(join_heads_body, parts, width),
        out_shape=jax.ShapeDtypeStruct((tokens, parts * width), BF16),
        in_specs=[VMEM],
        out_specs=HBM,
        scratch_shapes=[pltpu.SemaphoreType.DMA((parts,))],
    )(blocks)


def matmul(a, b, contract):
    return lax.dot_general(a, b, ((contract[:1], contract[1:]), ((), ())), preferred_element_type=F32)


def block_diagonal(rows):
    zero = jnp.zeros((rows.shape[0], DH), BF16)
    return jnp.concatenate(
        [
            jnp.concatenate([rows[:, :DH], zero], axis=1),
            jnp.concatenate([zero, rows[:, DH:]], axis=1),
        ],
        axis=0,
    )


def tables_body(owned, most, ids_ref, take_ref, add_ref):
    me = lax.axis_index("dp")
    mine = (lax.div(me, SIDE), lax.rem(me, SIDE))
    distinct = ids_ref.shape[1]
    for across in range(2):
        for n in range(SIDE * most):
            take_ref[across, n] = 0
        for n in range(SIDE * owned * SIDE):
            add_ref[across, n] = -1
        for k in range(SIDE):
            other = lax.rem(mine[across] + k, SIDE)
            replica = other * SIDE + mine[1] if across == 0 else mine[0] * SIDE + other

            def step(j, count):
                where = place(ids_ref[replica, j], owned)
                found = where[across] == mine[across]

                @pl.when(found)
                def _():
                    distance = lax.rem(where[1 - across] - mine[1 - across] + SIDE, SIDE)
                    row = distance * owned + where[2]
                    take_ref[across, k * most + count] = row
                    add_ref[across, row * SIDE + k] = count

                return count + found.astype(jnp.int32)

            lax.fori_loop(0, distinct, step, jnp.int32(0))


def tables(ids, owned, most):
    return pl.pallas_call(
        functools.partial(tables_body, owned, most),
        out_shape=(
            jax.ShapeDtypeStruct((2, SIDE * most), jnp.int32),
            jax.ShapeDtypeStruct((2, SIDE * owned * SIDE), jnp.int32),
        ),
        in_specs=[SMEM],
        out_specs=(SMEM, SMEM),
    )(ids)


def select_body(take_ref, *refs):
    lines, kept, sems = refs[16:18], refs[18:20], refs[20]
    copies = []
    for across in range(2):
        parts = refs[4 * across : 4 * across + 4]
        line = lines[across]
        owned = parts[0].shape[0]
        for k, part in enumerate(parts):
            for n in range(owned):
                line[k * owned + n] = part[n]
        own, *sent = refs[8 + 4 * across : 12 + 4 * across]
        most = own.shape[0]

        def pick(n, carry):
            kept[across][n] = line[take_ref[across, n]]
            for k, out in enumerate(sent):
                out[n] = line[take_ref[across, (k + 1) * most + n]]
            return carry

        lax.fori_loop(0, most, pick, 0, unroll=2)
        copies.append(pltpu.make_async_copy(kept[across], own, sems.at[across]))
        copies[-1].start()
    for copy in copies:
        copy.wait()


def select(take, keys, values, most):
    owned, nbr, width = keys[0].shape
    line = pltpu.VMEM((SIDE * owned, nbr, width), BF16)
    kept = pltpu.VMEM((most, nbr, width), BF16)
    shapes = chunk_shapes(most, nbr, width)
    out = pl.pallas_call(
        select_body,
        out_shape=((pltpu.HBM(shapes[0].shape, BF16),) + shapes[1:]) * 2,
        in_specs=[SMEM] + [VMEM] * 8,
        out_specs=((HBM,) + (VMEM,) * 3) * 2,
        scratch_shapes=[line, line, kept, kept, pltpu.SemaphoreType.DMA((2,))],
        compiler_params=pltpu.CompilerParams(vmem_limit_bytes=SELECT_VMEM),
    )(take, *keys, *values)
    return (out[:4], out[4:])


def spread_body(add_ref, *refs):
    outs, (pool, sems) = (refs[8:12], refs[12:16]), refs[16:]
    most = refs[0].shape[0]
    copies = [
        pltpu.make_async_copy(ref, pool.at[pl.ds(n * most, most)], sems.at[n])
        for n, ref in enumerate(refs[:8])
    ]
    for copy in copies:
        copy.start()
    for across in range(2):
        owned = outs[across][0].shape[0]
        for copy in copies[SIDE * across : SIDE * (across + 1)]:
            copy.wait()

        def add(n, carry):
            for distance, out in enumerate(outs[across]):
                value = jnp.zeros(out.shape[1:], F32)
                for k in range(SIDE):
                    index = add_ref[across, (distance * owned + n) * SIDE + k]
                    slot = (SIDE * across + k) * most + jnp.maximum(index, 0)
                    value += jnp.where(index >= 0, pool[slot].astype(F32), 0.0)
                out[n] = value.astype(out.dtype)
            return carry

        lax.fori_loop(0, owned, add, 0)


def in_hbm(values):
    return [pltpu.with_memory_space_constraint(v, pltpu.MemorySpace.HBM) for v in values]


def spread(add, keys, values, owned):
    most, nbr, width = keys[0].shape
    return_shapes = chunk_shapes(owned, nbr, width, F32) * 2
    out = pl.pallas_call(
        spread_body,
        out_shape=return_shapes,
        in_specs=[SMEM] + [HBM] * 8,
        out_specs=(VMEM,) * 8,
        scratch_shapes=[
            pltpu.VMEM((2 * SIDE * most, nbr, width), BF16),
            pltpu.SemaphoreType.DMA((2 * SIDE,)),
        ],
        compiler_params=pltpu.CompilerParams(vmem_limit_bytes=SPREAD_VMEM),
        cost_estimate=pl.CostEstimate(
            flops=SPREAD_FLOPS, bytes_accessed=4 * 1024 * 1024, transcendentals=0
        ),
    )(add, *in_hbm(keys), *in_hbm(values))
    return (out[:4], out[4:])


def attend_body(
    groups, distinct, owned, most, unroll, ids_ref, refs_ref, tokens_ref, *refs
):
    key_parts, value_parts = refs[:4], refs[4:8]
    gq_out, key_out, value_out = refs[8], refs[9:13], refs[13:17]
    (keys, values, key_sum, value_sum, gq_ref, key_send, value_send, query_last, grad_last, held,
     key_rows, value_rows, key_back, value_back, counts, in_sems, out_sems, gq_sem) = refs[17:]
    scale = 1.0 / math.sqrt(DH)
    copies = [
        pltpu.make_async_copy(part, pool.at[pl.ds(k * most, most)], in_sems.at[i, k])
        for i, (parts, pool) in enumerate(((key_parts, keys), (value_parts, values)))
        for k, part in enumerate(parts)
    ]
    for copy in copies:
        copy.start()

    def clear(j, carry):
        key_sum[j] = jnp.zeros(key_sum.shape[1:], F32)
        value_sum[j] = jnp.zeros(value_sum.shape[1:], F32)
        return carry

    lax.fori_loop(0, distinct, clear, 0)
    width = gq_ref.shape[2]
    row = lax.broadcasted_iota(jnp.int32, (GROUP, width), 0)
    me = lax.axis_index("dp")
    mine = (me // SIDE, me % SIDE)
    for i in range(2 * SIDE):
        counts[i] = 0
    for n in range(SIDE * most):
        key_back[n] = -1
        value_back[n] = -1

    def rank(j, carry):
        where = place(ids_ref[me, j], owned)
        for i, (table, back_rows) in enumerate(
            ((key_rows, key_back), (value_rows, value_back))
        ):
            distance = (mine[i] - where[i] + SIDE) % SIDE
            count = counts[i * SIDE + distance]
            table[j] = distance * most + count
            back_rows[distance * most + count] = j
            counts[i * SIDE + distance] = count + 1
        return carry

    lax.fori_loop(0, distinct, rank, 0)

    def rolled(kind, block):
        part = tokens_ref[block // 2, kind, pl.ds((block % 2) * GROUP, GROUP), :]
        return pltpu.roll(part.astype(F32), 1, 0)

    held[...] = jnp.zeros_like(held)
    query_last[...] = rolled(0, 0)
    grad_last[...] = rolled(1, 0)
    for copy in copies:
        copy.wait()

    def shifted(kind, group, last):
        following = rolled(kind, jnp.minimum(group + 1, groups - 1))
        following = jnp.where(group + 1 < groups, following, 0.0)
        block = jnp.where(row == 0, last[...], following)
        last[...] = following
        return block_diagonal(block.astype(BF16))

    def steps(index, carry):
        batch = [index * unroll + u for u in range(unroll)]
        state = []
        for group in batch:
            query = shifted(0, group, query_last)
            grad = shifted(1, group, grad_last)
            pair = (refs_ref[me, 2 * group], refs_ref[me, 2 * group + 1])
            block_keys = [keys[key_rows[j]] for j in pair]
            scores = [matmul(k, query, (1, 1)) for k in block_keys]
            grads = [matmul(values[value_rows[j]], grad, (1, 1)) for j in pair]
            state.append((group, query, grad, pair, block_keys, scores, grads))
        lows = []
        for group, query, grad, pair, block_keys, scores, grads in state:
            top = jnp.maximum(*[jnp.max(s, axis=0, keepdims=True) for s in scores])
            weights = [jnp.exp2((s - top) * (scale * math.log2(math.e))) for s in scores]
            total = sum(jnp.sum(w, axis=0, keepdims=True) for w in weights)
            inverse = 1.0 / total
            weights = [w * inverse for w in weights]
            dots = sum(jnp.sum(w * g, axis=0, keepdims=True) for w, g in zip(weights, grads))
            grad_low = [(w * (g - dots)).astype(BF16) for w, g in zip(weights, grads)]
            lows.append(([w.astype(BF16) for w in weights], grad_low))
        for (group, query, grad, pair, block_keys, _, _), (weights_low, grad_low) in zip(state, lows):
            terms = [(matmul(w, grad, (1, 0)), matmul(g, query, (1, 0))) for w, g in zip(weights_low, grad_low)]
            both = sum(matmul(g, k, (0, 0)) for g, k in zip(grad_low, block_keys)) * scale
            back = jnp.concatenate([both[:GROUP, :DH], both[GROUP:, DH:]], axis=1)
            back = pltpu.roll(back, GROUP - 1, 0)
            for j, (value_term, key_term) in zip(pair, terms):
                value_sum[j] += value_term
                key_sum[j] += key_term
            gq_ref[group // 2, pl.ds((group % 2) * GROUP, GROUP), :] = jnp.where(
                row == GROUP - 1, back, held[...]
            ).astype(BF16)
            held[...] = back
        return carry

    lax.fori_loop(0, groups // unroll, steps, 0)
    copies = [pltpu.make_async_copy(gq_ref, gq_out, gq_sem)]
    copies[0].start()
    for k in (2, 1, 3, 0):
        for i, (send, total, back_rows, out, factor) in enumerate(
            ((key_send, key_sum, key_back, key_out, scale),
             (value_send, value_sum, value_back, value_out, 1.0))
        ):

            def give(n, carry):
                slot = k * most + n
                j = back_rows[slot]

                @pl.when(j >= 0)
                def _():
                    send[slot] = (total[jnp.maximum(j, 0)] * factor).astype(BF16)

                return carry

            lax.fori_loop(0, most, give, 0)
            copy = pltpu.make_async_copy(
                send.at[pl.ds(k * most, most)], out[k], out_sems.at[i, k]
            )
            copy.start()
            copies.append(copy)
    for copy in copies:
        copy.wait()


def attend(ids, refs, tokens, keys, values, owned, most):
    parts, _, part_tokens, width = tokens.shape
    nbr = keys[0].shape[1]
    distinct = ids.shape[1]
    groups = refs.shape[1]
    flat = refs.reshape(refs.shape[0], -1)
    pool = pltpu.VMEM((SIDE * most, nbr, width), BF16)
    total = pltpu.VMEM((distinct, nbr, width), F32)
    rows = pltpu.VMEM((GROUP, width), F32)
    table = pltpu.SMEM((distinct,), jnp.int32)
    reverse = pltpu.SMEM((SIDE * most,), jnp.int32)
    shapes = (jax.ShapeDtypeStruct((parts, part_tokens, width), BF16),) + chunk_shapes(
        most, nbr, width
    ) * 2
    out = pl.pallas_call(
        functools.partial(attend_body, groups, distinct, owned, most, 8),
        out_shape=tuple(pltpu.HBM(shape.shape, shape.dtype) for shape in shapes),
        in_specs=[SMEM, SMEM, VMEM] + [HBM] * 8,
        out_specs=(HBM,) * 9,
        scratch_shapes=[pool, pool, total, total, pltpu.VMEM((parts, part_tokens, width), BF16),
                        pool, pool, rows, rows, rows, table, table, reverse, reverse,
                        pltpu.SMEM((2 * SIDE,), jnp.int32),
                        pltpu.SemaphoreType.DMA((2, SIDE)), pltpu.SemaphoreType.DMA((2, SIDE)),
                        pltpu.SemaphoreType.DMA],
        compiler_params=pltpu.CompilerParams(vmem_limit_bytes=ATTEND_VMEM),
    )(ids, flat, tokens, *in_hbm(keys), *in_hbm(values))
    return (out[0], out[1:5], out[5:])


def collect_body(*refs):
    for i, out in enumerate(refs[8:]):
        own, *others = refs[4 * i : 4 * i + 4]
        for n in range(own.shape[0]):
            value = own[n]
            for other in others:
                value += other[n].astype(F32)
            out[n] = value.astype(BF16)


def collect(keys, values):
    out = jax.ShapeDtypeStruct(keys[0].shape, BF16)
    return pl.pallas_call(
        collect_body,
        out_shape=(out, out),
        in_specs=[VMEM] * 8,
        out_specs=(VMEM, VMEM),
        compiler_params=pltpu.CompilerParams(vmem_limit_bytes=COLLECT_VMEM),
    )(*keys, *values)


def on_device(queries, grad_out, neighbour_keys, neighbour_values, distinct_ids, group_refs):
    parts = lax.axis_size("ctx")
    owned = neighbour_keys.shape[0]
    most = SIDE * (owned // 2)
    take, add = tables(distinct_ids, owned, most)
    lines = gather_lines(neighbour_keys, neighbour_values)
    packed = pack_heads(queries[0], grad_out[0], parts)
    tokens = lax.all_to_all(packed, "ctx", split_axis=0, concat_axis=0, tiled=True)
    keys, values = select(take, *lines, most)
    keys, values = exchange_lines(((keys, "y", 1), (values, "x", 1)))
    back, keys, values = attend(distinct_ids, group_refs, tokens, keys, values, owned, most)
    keys, values = exchange_lines(((keys, "y", -1), (values, "x", -1)))
    back = lax.all_to_all(back, "ctx", split_axis=0, concat_axis=0, tiled=True)
    keys, values = spread(add, keys, values, owned)
    keys, values = exchange_lines(((keys, "x", 1), (values, "y", 1)))
    grad_queries = join_heads(back)[None]
    grad_queries, keys, values = lax.optimization_barrier((grad_queries, keys, values))
    grad_keys, grad_values = collect(keys, values)
    return (grad_queries, grad_keys, grad_values)


def solution(mesh):
    return jax.shard_map(
        on_device,
        mesh=mesh,
        in_specs=(
            P("dp", "ctx", None),
            P("dp", "ctx", None),
            P("dp", None, "ctx"),
            P("dp", None, "ctx"),
            P(),
            P(),
        ),
        out_specs=(P("dp", "ctx", None), P("dp", None, "ctx"), P("dp", None, "ctx")),
        check_vma=False,
    )
```

```python
import functools
import math

import jax
import jax.numpy as jnp
from jax import lax
from jax.experimental import pallas as pl
from jax.experimental.pallas import tpu as pltpu
from jax.sharding import PartitionSpec as P

DH = 128
GROUP = 64
BF16 = jnp.bfloat16
F32 = jnp.float32
HBM = pl.BlockSpec(memory_space=pltpu.MemorySpace.HBM)
VMEM = pl.BlockSpec(memory_space=pltpu.VMEM)
SMEM = pl.BlockSpec(memory_space=pltpu.SMEM)
SELECT_VMEM = 10 * 1024 * 1024
SPREAD_VMEM = 12 * 1024 * 1024
SPREAD_FLOPS = 200_000_000_000
ATTEND_VMEM = 20 * 1024 * 1024
COLLECT_VMEM = 8 * 1024 * 1024


SIDE = 4


def place(n, owned):
    owner = lax.div(n, owned)
    return (lax.div(owner, SIDE), lax.rem(owner, SIDE), lax.rem(n, owned))


def shift(value, axis, amount):
    pairs = []
    for y in range(SIDE):
        for x in range(SIDE):
            to = (y, (x + amount) % SIDE) if axis == "x" else ((y + amount) % SIDE, x)
            pairs.append((y * SIDE + x, to[0] * SIDE + to[1]))
    return lax.ppermute(value, "dp", pairs)


def exchange_lines(lines):
    parts = [list(chunks) for chunks, _, _ in lines]
    for n, distances in ((0, (2, 1, 3)), (1, (1, 3, 2))):
        chunks, axis, sign = lines[n]
        for distance in distances:
            value = chunks[distance]
            if n == 1 and distance == 2:
                value, parts[n][1] = lax.optimization_barrier((value, parts[n][1]))
            parts[n][distance] = shift(value, axis, sign * distance)
    return parts


def gather_lines(keys, values):
    lines = [[keys, None, None, None], [values, None, None, None]]
    for distance in (1, 3):
        for line, axis in zip(lines, "xy"):
            line[distance] = shift(line[0], axis, -distance)
    for line, axis in zip(lines, "xy"):
        line[2] = shift(line[1], axis, -1)
    return lines


def chunk_shapes(most, nbr, width, own_type=BF16):
    return tuple(
        jax.ShapeDtypeStruct((most, nbr, width), own_type if k == 0 else BF16) for k in range(SIDE)
    )


def pack_heads_body(parts, width, q_ref, g_ref, out_ref, held, in_sems, out_sems):
    arrivals = []
    for j in range(parts):
        for i, ref in enumerate((q_ref, g_ref)):
            copy = pltpu.make_async_copy(
                ref.at[:, pl.ds(j * width, width)], held.at[j, i], in_sems.at[j, i]
            )
            copy.start()
            arrivals.append(copy)
    departures = []
    for j in range(parts):
        for copy in arrivals[2 * j : 2 * j + 2]:
            copy.wait()
        departures.append(pltpu.make_async_copy(held.at[j], out_ref.at[j], out_sems.at[j]))
        departures[-1].start()
    for copy in departures:
        copy.wait()


def pack_heads(queries, grad_out, parts):
    tokens, features = queries.shape
    width = features // parts
    shape = (parts, 2, tokens, width)
    return pl.pallas_call(
        functools.partial(pack_heads_body, parts, width),
        out_shape=pltpu.HBM(shape, BF16),
        in_specs=[HBM, HBM],
        out_specs=HBM,
        scratch_shapes=[
            pltpu.VMEM(shape, BF16),
            pltpu.SemaphoreType.DMA((parts, 2)),
            pltpu.SemaphoreType.DMA((parts,)),
        ],
    )(queries, grad_out)


def join_heads_body(parts, width, in_ref, out_ref, sems):
    copies = [
        pltpu.make_async_copy(in_ref.at[j], out_ref.at[:, pl.ds(j * width, width)], sems.at[j])
        for j in range(parts)
    ]
    for copy in copies:
        copy.start()
    for copy in copies:
        copy.wait()


def join_heads(blocks):
    parts, tokens, width = blocks.shape
    return pl.pallas_call(
        functools.partial(join_heads_body, parts, width),
        out_shape=jax.ShapeDtypeStruct((tokens, parts * width), BF16),
        in_specs=[VMEM],
        out_specs=HBM,
        scratch_shapes=[pltpu.SemaphoreType.DMA((parts,))],
    )(blocks)


def matmul(a, b, contract):
    return lax.dot_general(a, b, ((contract[:1], contract[1:]), ((), ())), preferred_element_type=F32)


def block_diagonal(rows):
    zero = jnp.zeros((rows.shape[0], DH), BF16)
    return jnp.concatenate(
        [
            jnp.concatenate([rows[:, :DH], zero], axis=1),
            jnp.concatenate([zero, rows[:, DH:]], axis=1),
        ],
        axis=0,
    )


def tables_body(owned, most, ids_ref, take_ref, add_ref):
    me = lax.axis_index("dp")
    mine = (lax.div(me, SIDE), lax.rem(me, SIDE))
    distinct = ids_ref.shape[1]
    for across in range(2):
        for n in range(SIDE * most):
            take_ref[across, n] = 0
        for n in range(SIDE * owned * SIDE):
            add_ref[across, n] = -1
        for k in range(SIDE):
            other = lax.rem(mine[across] + k, SIDE)
            replica = other * SIDE + mine[1] if across == 0 else mine[0] * SIDE + other

            def step(j, count):
                where = place(ids_ref[replica, j], owned)
                found = where[across] == mine[across]

                @pl.when(found)
                def _():
                    distance = lax.rem(where[1 - across] - mine[1 - across] + SIDE, SIDE)
                    row = distance * owned + where[2]
                    take_ref[across, k * most + count] = row
                    add_ref[across, row * SIDE + k] = count

                return count + found.astype(jnp.int32)

            lax.fori_loop(0, distinct, step, jnp.int32(0))


def tables(ids, owned, most):
    return pl.pallas_call(
        functools.partial(tables_body, owned, most),
        out_shape=(
            jax.ShapeDtypeStruct((2, SIDE * most), jnp.int32),
            jax.ShapeDtypeStruct((2, SIDE * owned * SIDE), jnp.int32),
        ),
        in_specs=[SMEM],
        out_specs=(SMEM, SMEM),
    )(ids)


def select_body(take_ref, *refs):
    outs = (refs[8:12], refs[12:16])
    line, picked, in_sems, out_sems = refs[16:]
    owned = refs[0].shape[0]
    most = outs[0][0].shape[0]
    arrivals = [
        pltpu.make_async_copy(ref, line.at[pl.ds(n * owned, owned)], in_sems.at[n])
        for n, ref in enumerate(refs[:8])
    ]
    for copy in arrivals:
        copy.start()
    departures = []
    for across in range(2):
        for copy in arrivals[SIDE * across : SIDE * (across + 1)]:
            copy.wait()
        for k in (2, 1, 3, 0) if across == 0 else (1, 3, 2, 0):
            base = (SIDE * across + k) * most

            def pick(n, carry):
                picked[base + n] = line[SIDE * owned * across + take_ref[across, k * most + n]]
                return carry

            lax.fori_loop(0, most, pick, 0, unroll=4)
            copy = pltpu.make_async_copy(
                picked.at[pl.ds(base, most)], outs[across][k], out_sems.at[SIDE * across + k]
            )
            copy.start()
            departures.append(copy)
    for copy in departures:
        copy.wait()


def select(take, keys, values, most):
    owned, nbr, width = keys[0].shape
    out = pl.pallas_call(
        select_body,
        out_shape=tuple(
            pltpu.HBM(shape.shape, shape.dtype) for shape in chunk_shapes(most, nbr, width) * 2
        ),
        in_specs=[SMEM] + [HBM] * 8,
        out_specs=(HBM,) * 8,
        scratch_shapes=[
            pltpu.VMEM((2 * SIDE * owned, nbr, width), BF16),
            pltpu.VMEM((2 * SIDE * most, nbr, width), BF16),
            pltpu.SemaphoreType.DMA((2 * SIDE,)),
            pltpu.SemaphoreType.DMA((2 * SIDE,)),
        ],
        compiler_params=pltpu.CompilerParams(vmem_limit_bytes=SELECT_VMEM),
    )(take, *keys, *values)
    return (out[:4], out[4:])


def spread_body(add_ref, *refs):
    outs, (pool, sems) = (refs[8:12], refs[12:16]), refs[16:]
    most = refs[0].shape[0]
    copies = [
        pltpu.make_async_copy(ref, pool.at[pl.ds(n * most, most)], sems.at[n])
        for n, ref in enumerate(refs[:8])
    ]
    for copy in copies:
        copy.start()
    for across in range(2):
        owned = outs[across][0].shape[0]
        for copy in copies[SIDE * across : SIDE * (across + 1)]:
            copy.wait()

        def add(n, carry):
            for distance, out in enumerate(outs[across]):
                value = jnp.zeros(out.shape[1:], F32)
                for k in range(SIDE):
                    index = add_ref[across, (distance * owned + n) * SIDE + k]
                    slot = (SIDE * across + k) * most + jnp.maximum(index, 0)
                    value += jnp.where(index >= 0, pool[slot].astype(F32), 0.0)
                out[n] = value.astype(out.dtype)
            return carry

        lax.fori_loop(0, owned, add, 0)


def in_hbm(values):
    return [pltpu.with_memory_space_constraint(v, pltpu.MemorySpace.HBM) for v in values]


def spread(add, keys, values, owned):
    most, nbr, width = keys[0].shape
    return_shapes = chunk_shapes(owned, nbr, width, F32) * 2
    out = pl.pallas_call(
        spread_body,
        out_shape=return_shapes,
        in_specs=[SMEM] + [HBM] * 8,
        out_specs=(VMEM,) * 8,
        scratch_shapes=[
            pltpu.VMEM((2 * SIDE * most, nbr, width), BF16),
            pltpu.SemaphoreType.DMA((2 * SIDE,)),
        ],
        compiler_params=pltpu.CompilerParams(vmem_limit_bytes=SPREAD_VMEM),
        cost_estimate=pl.CostEstimate(
            flops=SPREAD_FLOPS, bytes_accessed=4 * 1024 * 1024, transcendentals=0
        ),
    )(add, *in_hbm(keys), *in_hbm(values))
    return (out[:4], out[4:])


def attend_body(
    groups, distinct, owned, most, unroll, ids_ref, refs_ref, tokens_ref, *refs
):
    key_parts, value_parts = refs[:4], refs[4:8]
    gq_out, key_out, value_out = refs[8], refs[9:13], refs[13:17]
    (keys, values, key_sum, value_sum, gq_ref, key_send, value_send, query_last, grad_last, held,
     key_rows, value_rows, key_back, value_back, counts, in_sems, out_sems, gq_sem) = refs[17:]
    scale = 1.0 / math.sqrt(DH)
    copies = [
        pltpu.make_async_copy(part, pool.at[pl.ds(k * most, most)], in_sems.at[i, k])
        for i, (parts, pool) in enumerate(((key_parts, keys), (value_parts, values)))
        for k, part in enumerate(parts)
    ]
    for copy in copies:
        copy.start()

    def clear(j, carry):
        key_sum[j] = jnp.zeros(key_sum.shape[1:], F32)
        value_sum[j] = jnp.zeros(value_sum.shape[1:], F32)
        return carry

    lax.fori_loop(0, distinct, clear, 0)
    width = gq_ref.shape[2]
    row = lax.broadcasted_iota(jnp.int32, (GROUP, width), 0)
    me = lax.axis_index("dp")
    mine = (me // SIDE, me % SIDE)
    for i in range(2 * SIDE):
        counts[i] = 0
    for n in range(SIDE * most):
        key_back[n] = -1
        value_back[n] = -1

    def rank(j, carry):
        where = place(ids_ref[me, j], owned)
        for i, (table, back_rows) in enumerate(
            ((key_rows, key_back), (value_rows, value_back))
        ):
            distance = (mine[i] - where[i] + SIDE) % SIDE
            count = counts[i * SIDE + distance]
            table[j] = distance * most + count
            back_rows[distance * most + count] = j
            counts[i * SIDE + distance] = count + 1
        return carry

    lax.fori_loop(0, distinct, rank, 0)

    def rolled(kind, block):
        part = tokens_ref[block // 2, kind, pl.ds((block % 2) * GROUP, GROUP), :]
        return pltpu.roll(part.astype(F32), 1, 0)

    held[...] = jnp.zeros_like(held)
    query_last[...] = rolled(0, 0)
    grad_last[...] = rolled(1, 0)
    for copy in copies:
        copy.wait()

    def shifted(kind, group, last):
        following = rolled(kind, jnp.minimum(group + 1, groups - 1))
        following = jnp.where(group + 1 < groups, following, 0.0)
        block = jnp.where(row == 0, last[...], following)
        last[...] = following
        return block_diagonal(block.astype(BF16))

    def steps(index, carry):
        batch = [index * unroll + u for u in range(unroll)]
        state = []
        for group in batch:
            query = shifted(0, group, query_last)
            grad = shifted(1, group, grad_last)
            pair = (refs_ref[me, 2 * group], refs_ref[me, 2 * group + 1])
            block_keys = [keys[key_rows[j]] for j in pair]
            scores = [matmul(k, query, (1, 1)) for k in block_keys]
            grads = [matmul(values[value_rows[j]], grad, (1, 1)) for j in pair]
            state.append((group, query, grad, pair, block_keys, scores, grads))
        lows = []
        for group, query, grad, pair, block_keys, scores, grads in state:
            top = jnp.maximum(*[jnp.max(s, axis=0, keepdims=True) for s in scores])
            weights = [jnp.exp2((s - top) * (scale * math.log2(math.e))) for s in scores]
            total = sum(jnp.sum(w, axis=0, keepdims=True) for w in weights)
            inverse = 1.0 / total
            weights = [w * inverse for w in weights]
            dots = sum(jnp.sum(w * g, axis=0, keepdims=True) for w, g in zip(weights, grads))
            grad_low = [(w * (g - dots)).astype(BF16) for w, g in zip(weights, grads)]
            lows.append(([w.astype(BF16) for w in weights], grad_low))
        for (group, query, grad, pair, block_keys, _, _), (weights_low, grad_low) in zip(state, lows):
            terms = [(matmul(w, grad, (1, 0)), matmul(g, query, (1, 0))) for w, g in zip(weights_low, grad_low)]
            both = sum(matmul(g, k, (0, 0)) for g, k in zip(grad_low, block_keys)) * scale
            back = jnp.concatenate([both[:GROUP, :DH], both[GROUP:, DH:]], axis=1)
            back = pltpu.roll(back, GROUP - 1, 0)
            for j, (value_term, key_term) in zip(pair, terms):
                value_sum[j] += value_term
                key_sum[j] += key_term
            gq_ref[group // 2, pl.ds((group % 2) * GROUP, GROUP), :] = jnp.where(
                row == GROUP - 1, back, held[...]
            ).astype(BF16)
            held[...] = back
        return carry

    lax.fori_loop(0, groups // unroll, steps, 0)
    copies = [pltpu.make_async_copy(gq_ref, gq_out, gq_sem)]
    copies[0].start()
    for k in (2, 1, 3, 0):
        for i, (send, total, back_rows, out, factor) in enumerate(
            ((key_send, key_sum, key_back, key_out, scale),
             (value_send, value_sum, value_back, value_out, 1.0))
        ):

            def give(n, carry):
                slot = k * most + n
                j = back_rows[slot]

                @pl.when(j >= 0)
                def _():
                    send[slot] = (total[jnp.maximum(j, 0)] * factor).astype(BF16)

                return carry

            lax.fori_loop(0, most, give, 0)
            copy = pltpu.make_async_copy(
                send.at[pl.ds(k * most, most)], out[k], out_sems.at[i, k]
            )
            copy.start()
            copies.append(copy)
    for copy in copies:
        copy.wait()


def attend(ids, refs, tokens, keys, values, owned, most):
    parts, _, part_tokens, width = tokens.shape
    nbr = keys[0].shape[1]
    distinct = ids.shape[1]
    groups = refs.shape[1]
    flat = refs.reshape(refs.shape[0], -1)
    pool = pltpu.VMEM((SIDE * most, nbr, width), BF16)
    total = pltpu.VMEM((distinct, nbr, width), F32)
    rows = pltpu.VMEM((GROUP, width), F32)
    table = pltpu.SMEM((distinct,), jnp.int32)
    reverse = pltpu.SMEM((SIDE * most,), jnp.int32)
    shapes = (jax.ShapeDtypeStruct((parts, part_tokens, width), BF16),) + chunk_shapes(
        most, nbr, width
    ) * 2
    out = pl.pallas_call(
        functools.partial(attend_body, groups, distinct, owned, most, 8),
        out_shape=tuple(pltpu.HBM(shape.shape, shape.dtype) for shape in shapes),
        in_specs=[SMEM, SMEM, VMEM] + [HBM] * 8,
        out_specs=(HBM,) * 9,
        scratch_shapes=[pool, pool, total, total, pltpu.VMEM((parts, part_tokens, width), BF16),
                        pool, pool, rows, rows, rows, table, table, reverse, reverse,
                        pltpu.SMEM((2 * SIDE,), jnp.int32),
                        pltpu.SemaphoreType.DMA((2, SIDE)), pltpu.SemaphoreType.DMA((2, SIDE)),
                        pltpu.SemaphoreType.DMA],
        compiler_params=pltpu.CompilerParams(vmem_limit_bytes=ATTEND_VMEM),
    )(ids, flat, tokens, *in_hbm(keys), *in_hbm(values))
    return (out[0], out[1:5], out[5:])


def collect_body(*refs):
    for i, out in enumerate(refs[8:]):
        own, *others = refs[4 * i : 4 * i + 4]
        for n in range(own.shape[0]):
            value = own[n]
            for other in others:
                value += other[n].astype(F32)
            out[n] = value.astype(BF16)


def collect(keys, values):
    out = jax.ShapeDtypeStruct(keys[0].shape, BF16)
    return pl.pallas_call(
        collect_body,
        out_shape=(out, out),
        in_specs=[VMEM] * 8,
        out_specs=(VMEM, VMEM),
        compiler_params=pltpu.CompilerParams(vmem_limit_bytes=COLLECT_VMEM),
    )(*keys, *values)


def on_device(queries, grad_out, neighbour_keys, neighbour_values, distinct_ids, group_refs):
    parts = lax.axis_size("ctx")
    owned = neighbour_keys.shape[0]
    most = SIDE * (owned // 2)
    take, add = tables(distinct_ids, owned, most)
    lines = gather_lines(neighbour_keys, neighbour_values)
    packed = pack_heads(queries[0], grad_out[0], parts)
    tokens = lax.all_to_all(packed, "ctx", split_axis=0, concat_axis=0, tiled=True)
    keys, values = select(take, *lines, most)
    keys, values = exchange_lines(((keys, "y", 1), (values, "x", 1)))
    back, keys, values = attend(distinct_ids, group_refs, tokens, keys, values, owned, most)
    keys, values = exchange_lines(((keys, "y", -1), (values, "x", -1)))
    back = lax.all_to_all(back, "ctx", split_axis=0, concat_axis=0, tiled=True)
    keys, values = spread(add, keys, values, owned)
    keys, values = exchange_lines(((keys, "x", 1), (values, "y", 1)))
    grad_queries = join_heads(back)[None]
    grad_queries, keys, values = lax.optimization_barrier((grad_queries, keys, values))
    grad_keys, grad_values = collect(keys, values)
    return (grad_queries, grad_keys, grad_values)


def solution(mesh):
    return jax.shard_map(
        on_device,
        mesh=mesh,
        in_specs=(
            P("dp", "ctx", None),
            P("dp", "ctx", None),
            P("dp", None, "ctx"),
            P("dp", None, "ctx"),
            P(),
            P(),
        ),
        out_specs=(P("dp", "ctx", None), P("dp", None, "ctx"), P("dp", None, "ctx")),
        check_vma=False,
    )
```

```python
import functools
import math

import jax
import jax.numpy as jnp
from jax import lax
from jax.experimental import pallas as pl
from jax.experimental.pallas import tpu as pltpu
from jax.sharding import PartitionSpec as P

DH = 128
GROUP = 64
BF16 = jnp.bfloat16
F32 = jnp.float32
HBM = pl.BlockSpec(memory_space=pltpu.MemorySpace.HBM)
VMEM = pl.BlockSpec(memory_space=pltpu.VMEM)
SMEM = pl.BlockSpec(memory_space=pltpu.SMEM)
SELECT_VMEM = 10 * 1024 * 1024
SPREAD_VMEM = 12 * 1024 * 1024
SPREAD_FLOPS = 200_000_000_000
ATTEND_VMEM = 20 * 1024 * 1024
COLLECT_VMEM = 8 * 1024 * 1024


SIDE = 4


def place(n, owned):
    owner = lax.div(n, owned)
    return (lax.div(owner, SIDE), lax.rem(owner, SIDE), lax.rem(n, owned))


def shift(value, axis, amount):
    pairs = []
    for y in range(SIDE):
        for x in range(SIDE):
            to = (y, (x + amount) % SIDE) if axis == "x" else ((y + amount) % SIDE, x)
            pairs.append((y * SIDE + x, to[0] * SIDE + to[1]))
    return lax.ppermute(value, "dp", pairs)


def exchange_lines(lines):
    parts = [list(chunks) for chunks, _, _ in lines]
    for n, distances in ((0, (2, 1, 3)), (1, (1, 3, 2))):
        chunks, axis, sign = lines[n]
        for distance in distances:
            value = chunks[distance]
            if n == 1 and distance == 2:
                value, parts[n][1] = lax.optimization_barrier((value, parts[n][1]))
            parts[n][distance] = shift(value, axis, sign * distance)
    return parts


def gather_lines(keys, values):
    return exchange_lines((((keys,) * SIDE, "x", -1), ((values,) * SIDE, "y", -1)))


def chunk_shapes(most, nbr, width, own_type=BF16):
    return tuple(
        jax.ShapeDtypeStruct((most, nbr, width), own_type if k == 0 else BF16) for k in range(SIDE)
    )


def pack_heads_body(parts, width, q_ref, g_ref, out_ref, held, in_sems, out_sems):
    arrivals = []
    for j in range(parts):
        for i, ref in enumerate((q_ref, g_ref)):
            copy = pltpu.make_async_copy(
                ref.at[:, pl.ds(j * width, width)], held.at[j, i], in_sems.at[j, i]
            )
            copy.start()
            arrivals.append(copy)
    departures = []
    for j in range(parts):
        for copy in arrivals[2 * j : 2 * j + 2]:
            copy.wait()
        departures.append(pltpu.make_async_copy(held.at[j], out_ref.at[j], out_sems.at[j]))
        departures[-1].start()
    for copy in departures:
        copy.wait()


def pack_heads(queries, grad_out, parts):
    tokens, features = queries.shape
    width = features // parts
    shape = (parts, 2, tokens, width)
    return pl.pallas_call(
        functools.partial(pack_heads_body, parts, width),
        out_shape=pltpu.HBM(shape, BF16),
        in_specs=[HBM, HBM],
        out_specs=HBM,
        scratch_shapes=[
            pltpu.VMEM(shape, BF16),
            pltpu.SemaphoreType.DMA((parts, 2)),
            pltpu.SemaphoreType.DMA((parts,)),
        ],
    )(queries, grad_out)


def join_heads_body(parts, width, in_ref, out_ref, sems):
    copies = [
        pltpu.make_async_copy(in_ref.at[j], out_ref.at[:, pl.ds(j * width, width)], sems.at[j])
        for j in range(parts)
    ]
    for copy in copies:
        copy.start()
    for copy in copies:
        copy.wait()


def join_heads(blocks):
    parts, tokens, width = blocks.shape
    return pl.pallas_call(
        functools.partial(join_heads_body, parts, width),
        out_shape=jax.ShapeDtypeStruct((tokens, parts * width), BF16),
        in_specs=[VMEM],
        out_specs=HBM,
        scratch_shapes=[pltpu.SemaphoreType.DMA((parts,))],
    )(blocks)


def matmul(a, b, contract):
    return lax.dot_general(a, b, ((contract[:1], contract[1:]), ((), ())), preferred_element_type=F32)


def block_diagonal(rows):
    zero = jnp.zeros((rows.shape[0], DH), BF16)
    return jnp.concatenate(
        [
            jnp.concatenate([rows[:, :DH], zero], axis=1),
            jnp.concatenate([zero, rows[:, DH:]], axis=1),
        ],
        axis=0,
    )


def tables_body(owned, most, ids_ref, take_ref, add_ref):
    me = lax.axis_index("dp")
    mine = (lax.div(me, SIDE), lax.rem(me, SIDE))
    distinct = ids_ref.shape[1]
    for across in range(2):
        for n in range(SIDE * most):
            take_ref[across, n] = 0
        for n in range(SIDE * owned * SIDE):
            add_ref[across, n] = -1
        for k in range(SIDE):
            other = lax.rem(mine[across] + k, SIDE)
            replica = other * SIDE + mine[1] if across == 0 else mine[0] * SIDE + other

            def step(j, count):
                where = place(ids_ref[replica, j], owned)
                found = where[across] == mine[across]

                @pl.when(found)
                def _():
                    distance = lax.rem(where[1 - across] - mine[1 - across] + SIDE, SIDE)
                    row = distance * owned + where[2]
                    take_ref[across, k * most + count] = row
                    add_ref[across, row * SIDE + k] = count

                return count + found.astype(jnp.int32)

            lax.fori_loop(0, distinct, step, jnp.int32(0))


def tables(ids, owned, most):
    return pl.pallas_call(
        functools.partial(tables_body, owned, most),
        out_shape=(
            jax.ShapeDtypeStruct((2, SIDE * most), jnp.int32),
            jax.ShapeDtypeStruct((2, SIDE * owned * SIDE), jnp.int32),
        ),
        in_specs=[SMEM],
        out_specs=(SMEM, SMEM),
    )(ids)


def select_body(take_ref, *refs):
    outs = (refs[8:12], refs[12:16])
    line, picked, in_sems, out_sems = refs[16:]
    owned = refs[0].shape[0]
    most = outs[0][0].shape[0]
    arrivals = [
        pltpu.make_async_copy(ref, line.at[pl.ds(n * owned, owned)], in_sems.at[n])
        for n, ref in enumerate(refs[:8])
    ]
    for copy in arrivals:
        copy.start()
    departures = []
    for across in range(2):
        for copy in arrivals[SIDE * across : SIDE * (across + 1)]:
            copy.wait()
        for k in (2, 1, 3, 0) if across == 0 else (1, 3, 2, 0):
            base = (SIDE * across + k) * most

            def pick(n, carry):
                picked[base + n] = line[SIDE * owned * across + take_ref[across, k * most + n]]
                return carry

            lax.fori_loop(0, most, pick, 0, unroll=4)
            copy = pltpu.make_async_copy(
                picked.at[pl.ds(base, most)], outs[across][k], out_sems.at[SIDE * across + k]
            )
            copy.start()
            departures.append(copy)
    for copy in departures:
        copy.wait()


def select(take, keys, values, most):
    owned, nbr, width = keys[0].shape
    out = pl.pallas_call(
        select_body,
        out_shape=tuple(
            pltpu.HBM(shape.shape, shape.dtype) for shape in chunk_shapes(most, nbr, width) * 2
        ),
        in_specs=[SMEM] + [HBM] * 8,
        out_specs=(HBM,) * 8,
        scratch_shapes=[
            pltpu.VMEM((2 * SIDE * owned, nbr, width), BF16),
            pltpu.VMEM((2 * SIDE * most, nbr, width), BF16),
            pltpu.SemaphoreType.DMA((2 * SIDE,)),
            pltpu.SemaphoreType.DMA((2 * SIDE,)),
        ],
        compiler_params=pltpu.CompilerParams(vmem_limit_bytes=SELECT_VMEM),
    )(take, *keys, *values)
    return (out[:4], out[4:])


def spread_body(across, add_ref, *refs):
    outs, (pool, sems) = refs[4:8], refs[8:]
    most, owned = refs[0].shape[0], outs[0].shape[0]
    copies = [
        pltpu.make_async_copy(ref, pool.at[pl.ds(k * most, most)], sems.at[k])
        for k, ref in enumerate(refs[:4])
    ]
    for copy in copies:
        copy.start()
    for copy in copies:
        copy.wait()

    def add(n, carry):
        for distance, out in enumerate(outs):
            value = jnp.zeros(out.shape[1:], F32)
            for k in range(SIDE):
                index = add_ref[across, (distance * owned + n) * SIDE + k]
                term = pool[k * most + jnp.maximum(index, 0)].astype(F32)
                value += jnp.where(index >= 0, term, 0.0)
            out[n] = value.astype(out.dtype)
        return carry

    lax.fori_loop(0, owned, add, 0)


def in_hbm(values):
    return [pltpu.with_memory_space_constraint(v, pltpu.MemorySpace.HBM) for v in values]


def spread(add, chunks, across, owned):
    most, nbr, width = chunks[0].shape
    return pl.pallas_call(
        functools.partial(spread_body, across),
        out_shape=chunk_shapes(owned, nbr, width, F32),
        in_specs=[SMEM] + [HBM] * 4,
        out_specs=(VMEM,) * 4,
        scratch_shapes=[
            pltpu.VMEM((SIDE * most, nbr, width), BF16),
            pltpu.SemaphoreType.DMA((SIDE,)),
        ],
        compiler_params=pltpu.CompilerParams(vmem_limit_bytes=SPREAD_VMEM),
        cost_estimate=pl.CostEstimate(
            flops=SPREAD_FLOPS, bytes_accessed=2 * 1024 * 1024, transcendentals=0
        ),
    )(add, *in_hbm(chunks))


def attend_body(
    groups, distinct, owned, most, unroll, ids_ref, refs_ref, tokens_ref, *refs
):
    key_parts, value_parts = refs[:4], refs[4:8]
    gq_out, key_out, value_out = refs[8], refs[9:13], refs[13:17]
    (keys, values, key_sum, value_sum, gq_ref, key_send, value_send, query_last, grad_last, held,
     key_rows, value_rows, key_back, value_back, counts, in_sems, out_sems, gq_sem) = refs[17:]
    scale = 1.0 / math.sqrt(DH)
    copies = [
        pltpu.make_async_copy(part, pool.at[pl.ds(k * most, most)], in_sems.at[i, k])
        for i, (parts, pool) in enumerate(((key_parts, keys), (value_parts, values)))
        for k, part in enumerate(parts)
    ]
    for copy in copies:
        copy.start()

    def clear(j, carry):
        key_sum[j] = jnp.zeros(key_sum.shape[1:], F32)
        value_sum[j] = jnp.zeros(value_sum.shape[1:], F32)
        return carry

    lax.fori_loop(0, distinct, clear, 0)
    width = gq_ref.shape[2]
    row = lax.broadcasted_iota(jnp.int32, (GROUP, width), 0)
    me = lax.axis_index("dp")
    mine = (me // SIDE, me % SIDE)
    for i in range(2 * SIDE):
        counts[i] = 0
    for n in range(SIDE * most):
        key_back[n] = -1
        value_back[n] = -1

    def rank(j, carry):
        where = place(ids_ref[me, j], owned)
        for i, (table, back_rows) in enumerate(
            ((key_rows, key_back), (value_rows, value_back))
        ):
            distance = (mine[i] - where[i] + SIDE) % SIDE
            count = counts[i * SIDE + distance]
            table[j] = distance * most + count
            back_rows[distance * most + count] = j
            counts[i * SIDE + distance] = count + 1
        return carry

    lax.fori_loop(0, distinct, rank, 0)

    def rolled(kind, block):
        part = tokens_ref[block // 2, kind, pl.ds((block % 2) * GROUP, GROUP), :]
        return pltpu.roll(part.astype(F32), 1, 0)

    held[...] = jnp.zeros_like(held)
    query_last[...] = rolled(0, 0)
    grad_last[...] = rolled(1, 0)
    for copy in copies:
        copy.wait()

    def shifted(kind, group, last):
        following = rolled(kind, jnp.minimum(group + 1, groups - 1))
        following = jnp.where(group + 1 < groups, following, 0.0)
        block = jnp.where(row == 0, last[...], following)
        last[...] = following
        return block_diagonal(block.astype(BF16))

    def steps(index, carry):
        batch = [index * unroll + u for u in range(unroll)]
        state = []
        for group in batch:
            query = shifted(0, group, query_last)
            grad = shifted(1, group, grad_last)
            pair = (refs_ref[me, 2 * group], refs_ref[me, 2 * group + 1])
            block_keys = [keys[key_rows[j]] for j in pair]
            scores = [matmul(k, query, (1, 1)) for k in block_keys]
            grads = [matmul(values[value_rows[j]], grad, (1, 1)) for j in pair]
            state.append((group, query, grad, pair, block_keys, scores, grads))
        lows = []
        for group, query, grad, pair, block_keys, scores, grads in state:
            top = jnp.maximum(*[jnp.max(s, axis=0, keepdims=True) for s in scores])
            weights = [jnp.exp2((s - top) * (scale * math.log2(math.e))) for s in scores]
            total = sum(jnp.sum(w, axis=0, keepdims=True) for w in weights)
            inverse = 1.0 / total
            weights = [w * inverse for w in weights]
            dots = sum(jnp.sum(w * g, axis=0, keepdims=True) for w, g in zip(weights, grads))
            grad_low = [(w * (g - dots)).astype(BF16) for w, g in zip(weights, grads)]
            lows.append(([w.astype(BF16) for w in weights], grad_low))
        for (group, query, grad, pair, block_keys, _, _), (weights_low, grad_low) in zip(state, lows):
            terms = [(matmul(w, grad, (1, 0)), matmul(g, query, (1, 0))) for w, g in zip(weights_low, grad_low)]
            both = sum(matmul(g, k, (0, 0)) for g, k in zip(grad_low, block_keys)) * scale
            back = jnp.concatenate([both[:GROUP, :DH], both[GROUP:, DH:]], axis=1)
            back = pltpu.roll(back, GROUP - 1, 0)
            for j, (value_term, key_term) in zip(pair, terms):
                value_sum[j] += value_term
                key_sum[j] += key_term
            gq_ref[group // 2, pl.ds((group % 2) * GROUP, GROUP), :] = jnp.where(
                row == GROUP - 1, back, held[...]
            ).astype(BF16)
            held[...] = back
        return carry

    lax.fori_loop(0, groups // unroll, steps, 0)
    copies = [pltpu.make_async_copy(gq_ref, gq_out, gq_sem)]
    copies[0].start()
    for k in (2, 1, 3, 0):
        for i, (send, total, back_rows, out, factor) in enumerate(
            ((key_send, key_sum, key_back, key_out, scale),
             (value_send, value_sum, value_back, value_out, 1.0))
        ):

            def give(n, carry):
                slot = k * most + n
                j = back_rows[slot]

                @pl.when(j >= 0)
                def _():
                    send[slot] = (total[jnp.maximum(j, 0)] * factor).astype(BF16)

                return carry

            lax.fori_loop(0, most, give, 0)
            copy = pltpu.make_async_copy(
                send.at[pl.ds(k * most, most)], out[k], out_sems.at[i, k]
            )
            copy.start()
            copies.append(copy)
    for copy in copies:
        copy.wait()


def attend(ids, refs, tokens, keys, values, owned, most):
    parts, _, part_tokens, width = tokens.shape
    nbr = keys[0].shape[1]
    distinct = ids.shape[1]
    groups = refs.shape[1]
    flat = refs.reshape(refs.shape[0], -1)
    pool = pltpu.VMEM((SIDE * most, nbr, width), BF16)
    total = pltpu.VMEM((distinct, nbr, width), F32)
    rows = pltpu.VMEM((GROUP, width), F32)
    table = pltpu.SMEM((distinct,), jnp.int32)
    reverse = pltpu.SMEM((SIDE * most,), jnp.int32)
    shapes = (jax.ShapeDtypeStruct((parts, part_tokens, width), BF16),) + chunk_shapes(
        most, nbr, width
    ) * 2
    out = pl.pallas_call(
        functools.partial(attend_body, groups, distinct, owned, most, 8),
        out_shape=tuple(pltpu.HBM(shape.shape, shape.dtype) for shape in shapes),
        in_specs=[SMEM, SMEM, VMEM] + [HBM] * 8,
        out_specs=(HBM,) * 9,
        scratch_shapes=[pool, pool, total, total, pltpu.VMEM((parts, part_tokens, width), BF16),
                        pool, pool, rows, rows, rows, table, table, reverse, reverse,
                        pltpu.SMEM((2 * SIDE,), jnp.int32),
                        pltpu.SemaphoreType.DMA((2, SIDE)), pltpu.SemaphoreType.DMA((2, SIDE)),
                        pltpu.SemaphoreType.DMA],
        compiler_params=pltpu.CompilerParams(vmem_limit_bytes=ATTEND_VMEM),
    )(ids, flat, tokens, *in_hbm(keys), *in_hbm(values))
    return (out[0], out[1:5], out[5:])


def collect_body(*refs):
    for i, out in enumerate(refs[8:]):
        own, *others = refs[4 * i : 4 * i + 4]
        for n in range(own.shape[0]):
            value = own[n]
            for other in others:
                value += other[n].astype(F32)
            out[n] = value.astype(BF16)


def collect(keys, values):
    out = jax.ShapeDtypeStruct(keys[0].shape, BF16)
    return pl.pallas_call(
        collect_body,
        out_shape=(out, out),
        in_specs=[VMEM] * 8,
        out_specs=(VMEM, VMEM),
        compiler_params=pltpu.CompilerParams(vmem_limit_bytes=COLLECT_VMEM),
    )(*keys, *values)


def on_device(queries, grad_out, neighbour_keys, neighbour_values, distinct_ids, group_refs):
    parts = lax.axis_size("ctx")
    owned = neighbour_keys.shape[0]
    most = SIDE * (owned // 2)
    take, add = tables(distinct_ids, owned, most)
    lines = gather_lines(neighbour_keys, neighbour_values)
    packed = pack_heads(queries[0], grad_out[0], parts)
    tokens = lax.all_to_all(packed, "ctx", split_axis=0, concat_axis=0, tiled=True)
    keys, values = select(take, *lines, most)
    keys, values = exchange_lines(((keys, "y", 1), (values, "x", 1)))
    back, keys, values = attend(distinct_ids, group_refs, tokens, keys, values, owned, most)
    keys, values = exchange_lines(((keys, "y", -1), (values, "x", -1)))
    back = lax.all_to_all(back, "ctx", split_axis=0, concat_axis=0, tiled=True)
    keys = list(spread(add, keys, 0, owned))
    keys[0], values[0] = lax.optimization_barrier((keys[0], values[0]))
    values = spread(add, values, 1, owned)
    keys, values = exchange_lines(((keys, "x", 1), (values, "y", 1)))
    grad_queries = join_heads(back)[None]
    grad_queries, keys, values = lax.optimization_barrier((grad_queries, keys, values))
    grad_keys, grad_values = collect(keys, values)
    return (grad_queries, grad_keys, grad_values)


def solution(mesh):
    return jax.shard_map(
        on_device,
        mesh=mesh,
        in_specs=(
            P("dp", "ctx", None),
            P("dp", "ctx", None),
            P("dp", None, "ctx"),
            P("dp", None, "ctx"),
            P(),
            P(),
        ),
        out_specs=(P("dp", "ctx", None), P("dp", None, "ctx"), P("dp", None, "ctx")),
        check_vma=False,
    )
```

```python
import functools
import math

import jax
import jax.numpy as jnp
from jax import lax
from jax.experimental import pallas as pl
from jax.experimental.pallas import tpu as pltpu
from jax.sharding import PartitionSpec as P

DH = 128
GROUP = 64
BF16 = jnp.bfloat16
F32 = jnp.float32
HBM = pl.BlockSpec(memory_space=pltpu.MemorySpace.HBM)
VMEM = pl.BlockSpec(memory_space=pltpu.VMEM)
SMEM = pl.BlockSpec(memory_space=pltpu.SMEM)
SELECT_VMEM = 10 * 1024 * 1024
SPREAD_VMEM = 12 * 1024 * 1024
SPREAD_FLOPS = 200_000_000_000
ATTEND_VMEM = 20 * 1024 * 1024
COLLECT_VMEM = 8 * 1024 * 1024


SIDE = 4


def place(n, owned):
    owner = lax.div(n, owned)
    return (lax.div(owner, SIDE), lax.rem(owner, SIDE), lax.rem(n, owned))


def shift(value, axis, amount):
    pairs = []
    for y in range(SIDE):
        for x in range(SIDE):
            to = (y, (x + amount) % SIDE) if axis == "x" else ((y + amount) % SIDE, x)
            pairs.append((y * SIDE + x, to[0] * SIDE + to[1]))
    return lax.ppermute(value, "dp", pairs)


def exchange_lines(lines):
    parts = [list(chunks) for chunks, _, _ in lines]
    for n, distances in ((0, (2, 1, 3)), (1, (1, 3, 2))):
        chunks, axis, sign = lines[n]
        for distance in distances:
            value = chunks[distance]
            if n == 1 and distance == 2:
                value, parts[n][1] = lax.optimization_barrier((value, parts[n][1]))
            parts[n][distance] = shift(value, axis, sign * distance)
    return parts


def gather_lines(keys, values):
    return exchange_lines((((keys,) * SIDE, "x", -1), ((values,) * SIDE, "y", -1)))


def chunk_shapes(most, nbr, width, own_type=BF16):
    return tuple(
        jax.ShapeDtypeStruct((most, nbr, width), own_type if k == 0 else BF16) for k in range(SIDE)
    )


def pack_heads_body(parts, width, q_ref, g_ref, out_ref, held, in_sems, out_sems):
    arrivals = []
    for j in range(parts):
        for i, ref in enumerate((q_ref, g_ref)):
            copy = pltpu.make_async_copy(
                ref.at[:, pl.ds(j * width, width)], held.at[j, i], in_sems.at[j, i]
            )
            copy.start()
            arrivals.append(copy)
    departures = []
    for j in range(parts):
        for copy in arrivals[2 * j : 2 * j + 2]:
            copy.wait()
        departures.append(pltpu.make_async_copy(held.at[j], out_ref.at[j], out_sems.at[j]))
        departures[-1].start()
    for copy in departures:
        copy.wait()


def pack_heads(queries, grad_out, parts):
    tokens, features = queries.shape
    width = features // parts
    shape = (parts, 2, tokens, width)
    return pl.pallas_call(
        functools.partial(pack_heads_body, parts, width),
        out_shape=pltpu.HBM(shape, BF16),
        in_specs=[HBM, HBM],
        out_specs=HBM,
        scratch_shapes=[
            pltpu.VMEM(shape, BF16),
            pltpu.SemaphoreType.DMA((parts, 2)),
            pltpu.SemaphoreType.DMA((parts,)),
        ],
    )(queries, grad_out)


def join_heads_body(parts, width, in_ref, out_ref, sems):
    copies = [
        pltpu.make_async_copy(in_ref.at[j], out_ref.at[:, pl.ds(j * width, width)], sems.at[j])
        for j in range(parts)
    ]
    for copy in copies:
        copy.start()
    for copy in copies:
        copy.wait()


def join_heads(blocks):
    parts, tokens, width = blocks.shape
    return pl.pallas_call(
        functools.partial(join_heads_body, parts, width),
        out_shape=jax.ShapeDtypeStruct((tokens, parts * width), BF16),
        in_specs=[VMEM],
        out_specs=HBM,
        scratch_shapes=[pltpu.SemaphoreType.DMA((parts,))],
    )(blocks)


def matmul(a, b, contract):
    return lax.dot_general(a, b, ((contract[:1], contract[1:]), ((), ())), preferred_element_type=F32)


def block_diagonal(rows):
    zero = jnp.zeros((rows.shape[0], DH), BF16)
    return jnp.concatenate(
        [
            jnp.concatenate([rows[:, :DH], zero], axis=1),
            jnp.concatenate([zero, rows[:, DH:]], axis=1),
        ],
        axis=0,
    )


def tables_body(owned, most, ids_ref, take_ref, add_ref):
    me = lax.axis_index("dp")
    mine = (lax.div(me, SIDE), lax.rem(me, SIDE))
    distinct = ids_ref.shape[1]
    for across in range(2):
        for n in range(SIDE * most):
            take_ref[across, n] = 0
        for n in range(SIDE * owned * SIDE):
            add_ref[across, n] = -1
        for k in range(SIDE):
            other = lax.rem(mine[across] + k, SIDE)
            replica = other * SIDE + mine[1] if across == 0 else mine[0] * SIDE + other

            def step(j, count):
                where = place(ids_ref[replica, j], owned)
                found = where[across] == mine[across]

                @pl.when(found)
                def _():
                    distance = lax.rem(where[1 - across] - mine[1 - across] + SIDE, SIDE)
                    row = distance * owned + where[2]
                    take_ref[across, k * most + count] = row
                    add_ref[across, row * SIDE + k] = count

                return count + found.astype(jnp.int32)

            lax.fori_loop(0, distinct, step, jnp.int32(0))


def tables(ids, owned, most):
    return pl.pallas_call(
        functools.partial(tables_body, owned, most),
        out_shape=(
            jax.ShapeDtypeStruct((2, SIDE * most), jnp.int32),
            jax.ShapeDtypeStruct((2, SIDE * owned * SIDE), jnp.int32),
        ),
        in_specs=[SMEM],
        out_specs=(SMEM, SMEM),
    )(ids)


def select_body(take_ref, *refs):
    outs = (refs[8:12], refs[12:16])
    line, picked, in_sems, out_sems = refs[16:]
    owned = refs[0].shape[0]
    most = outs[0][0].shape[0]
    arrivals = [
        pltpu.make_async_copy(ref, line.at[pl.ds(n * owned, owned)], in_sems.at[n])
        for n, ref in enumerate(refs[:8])
    ]
    for copy in arrivals:
        copy.start()
    departures = []
    for across in range(2):
        for copy in arrivals[SIDE * across : SIDE * (across + 1)]:
            copy.wait()
        for k in (2, 1, 3, 0) if across == 0 else (1, 3, 2, 0):
            base = (SIDE * across + k) * most

            def pick(n, carry):
                picked[base + n] = line[SIDE * owned * across + take_ref[across, k * most + n]]
                return carry

            lax.fori_loop(0, most, pick, 0, unroll=4)
            copy = pltpu.make_async_copy(
                picked.at[pl.ds(base, most)], outs[across][k], out_sems.at[SIDE * across + k]
            )
            copy.start()
            departures.append(copy)
    for copy in departures:
        copy.wait()


def select(take, keys, values, most):
    owned, nbr, width = keys[0].shape
    out = pl.pallas_call(
        select_body,
        out_shape=tuple(
            pltpu.HBM(shape.shape, shape.dtype) for shape in chunk_shapes(most, nbr, width) * 2
        ),
        in_specs=[SMEM] + [HBM] * 8,
        out_specs=(HBM,) * 8,
        scratch_shapes=[
            pltpu.VMEM((2 * SIDE * owned, nbr, width), BF16),
            pltpu.VMEM((2 * SIDE * most, nbr, width), BF16),
            pltpu.SemaphoreType.DMA((2 * SIDE,)),
            pltpu.SemaphoreType.DMA((2 * SIDE,)),
        ],
        compiler_params=pltpu.CompilerParams(vmem_limit_bytes=SELECT_VMEM),
    )(take, *keys, *values)
    return (out[:4], out[4:])


def spread_body(across, add_ref, *refs):
    outs, (pool, sems) = refs[4:8], refs[8:]
    most, owned = refs[0].shape[0], outs[0].shape[0]
    copies = [
        pltpu.make_async_copy(ref, pool.at[pl.ds(k * most, most)], sems.at[k])
        for k, ref in enumerate(refs[:4])
    ]
    for copy in copies:
        copy.start()
    for copy in copies:
        copy.wait()

    def add(n, carry):
        for distance, out in enumerate(outs):
            value = jnp.zeros(out.shape[1:], F32)
            for k in range(SIDE):
                index = add_ref[across, (distance * owned + n) * SIDE + k]
                term = pool[k * most + jnp.maximum(index, 0)].astype(F32)
                value += jnp.where(index >= 0, term, 0.0)
            out[n] = value.astype(out.dtype)
        return carry

    lax.fori_loop(0, owned, add, 0)


def in_hbm(values):
    return [pltpu.with_memory_space_constraint(v, pltpu.MemorySpace.HBM) for v in values]


def spread(add, chunks, across, owned):
    most, nbr, width = chunks[0].shape
    return pl.pallas_call(
        functools.partial(spread_body, across),
        out_shape=chunk_shapes(owned, nbr, width, F32),
        in_specs=[SMEM] + [HBM] * 4,
        out_specs=(VMEM,) * 4,
        scratch_shapes=[
            pltpu.VMEM((SIDE * most, nbr, width), BF16),
            pltpu.SemaphoreType.DMA((SIDE,)),
        ],
        compiler_params=pltpu.CompilerParams(vmem_limit_bytes=SPREAD_VMEM),
        cost_estimate=pl.CostEstimate(
            flops=SPREAD_FLOPS, bytes_accessed=2 * 1024 * 1024, transcendentals=0
        ),
    )(add, *in_hbm(chunks))


def attend_body(
    groups, distinct, owned, most, unroll, ids_ref, refs_ref, tokens_ref, *refs
):
    key_parts, value_parts = refs[:4], refs[4:8]
    gq_out, key_out, value_out = refs[8], refs[9:13], refs[13:17]
    (keys, values, key_sum, value_sum, gq_ref, key_send, value_send, query_last, grad_last, held,
     key_rows, value_rows, key_back, value_back, counts, in_sems, out_sems, gq_sem) = refs[17:]
    scale = 1.0 / math.sqrt(DH)
    copies = [
        pltpu.make_async_copy(part, pool.at[pl.ds(k * most, most)], in_sems.at[i, k])
        for i, (parts, pool) in enumerate(((key_parts, keys), (value_parts, values)))
        for k, part in enumerate(parts)
    ]
    for copy in copies:
        copy.start()

    def clear(j, carry):
        key_sum[j] = jnp.zeros(key_sum.shape[1:], F32)
        value_sum[j] = jnp.zeros(value_sum.shape[1:], F32)
        return carry

    lax.fori_loop(0, distinct, clear, 0)
    width = gq_ref.shape[2]
    row = lax.broadcasted_iota(jnp.int32, (GROUP, width), 0)
    me = lax.axis_index("dp")
    mine = (me // SIDE, me % SIDE)
    for i in range(2 * SIDE):
        counts[i] = 0
    for n in range(SIDE * most):
        key_back[n] = -1
        value_back[n] = -1

    def rank(j, carry):
        where = place(ids_ref[me, j], owned)
        for i, (table, back_rows) in enumerate(
            ((key_rows, key_back), (value_rows, value_back))
        ):
            distance = (mine[i] - where[i] + SIDE) % SIDE
            count = counts[i * SIDE + distance]
            table[j] = distance * most + count
            back_rows[distance * most + count] = j
            counts[i * SIDE + distance] = count + 1
        return carry

    lax.fori_loop(0, distinct, rank, 0)

    def rolled(kind, block):
        part = tokens_ref[block // 2, kind, pl.ds((block % 2) * GROUP, GROUP), :]
        return pltpu.roll(part.astype(F32), 1, 0)

    held[...] = jnp.zeros_like(held)
    query_last[...] = rolled(0, 0)
    grad_last[...] = rolled(1, 0)
    for copy in copies:
        copy.wait()

    def shifted(kind, group, last):
        following = rolled(kind, jnp.minimum(group + 1, groups - 1))
        following = jnp.where(group + 1 < groups, following, 0.0)
        block = jnp.where(row == 0, last[...], following)
        last[...] = following
        return block_diagonal(block.astype(BF16))

    def steps(index, carry):
        batch = [index * unroll + u for u in range(unroll)]
        state = []
        for group in batch:
            query = shifted(0, group, query_last)
            grad = shifted(1, group, grad_last)
            pair = (refs_ref[me, 2 * group], refs_ref[me, 2 * group + 1])
            block_keys = [keys[key_rows[j]] for j in pair]
            scores = [matmul(k, query, (1, 1)) for k in block_keys]
            grads = [matmul(values[value_rows[j]], grad, (1, 1)) for j in pair]
            state.append((group, query, grad, pair, block_keys, scores, grads))
        lows = []
        for group, query, grad, pair, block_keys, scores, grads in state:
            top = jnp.maximum(*[jnp.max(s, axis=0, keepdims=True) for s in scores])
            weights = [jnp.exp2((s - top) * (scale * math.log2(math.e))) for s in scores]
            total = sum(jnp.sum(w, axis=0, keepdims=True) for w in weights)
            inverse = 1.0 / total
            weights = [w * inverse for w in weights]
            dots = sum(jnp.sum(w * g, axis=0, keepdims=True) for w, g in zip(weights, grads))
            grad_low = [(w * (g - dots)).astype(BF16) for w, g in zip(weights, grads)]
            lows.append(([w.astype(BF16) for w in weights], grad_low))
        for (group, query, grad, pair, block_keys, _, _), (weights_low, grad_low) in zip(state, lows):
            terms = [(matmul(w, grad, (1, 0)), matmul(g, query, (1, 0))) for w, g in zip(weights_low, grad_low)]
            both = sum(matmul(g, k, (0, 0)) for g, k in zip(grad_low, block_keys)) * scale
            back = jnp.concatenate([both[:GROUP, :DH], both[GROUP:, DH:]], axis=1)
            back = pltpu.roll(back, GROUP - 1, 0)
            for j, (value_term, key_term) in zip(pair, terms):
                value_sum[j] += value_term
                key_sum[j] += key_term
            gq_ref[group // 2, pl.ds((group % 2) * GROUP, GROUP), :] = jnp.where(
                row == GROUP - 1, back, held[...]
            ).astype(BF16)
            held[...] = back
        return carry

    lax.fori_loop(0, groups // unroll, steps, 0)
    copies = [pltpu.make_async_copy(gq_ref, gq_out, gq_sem)]
    copies[0].start()
    for k in (2, 1, 3, 0):
        for i, (send, total, back_rows, out, factor) in enumerate(
            ((key_send, key_sum, key_back, key_out, scale),
             (value_send, value_sum, value_back, value_out, 1.0))
        ):

            def give(n, carry):
                slot = k * most + n
                j = back_rows[slot]

                @pl.when(j >= 0)
                def _():
                    send[slot] = (total[jnp.maximum(j, 0)] * factor).astype(BF16)

                return carry

            lax.fori_loop(0, most, give, 0)
            copy = pltpu.make_async_copy(
                send.at[pl.ds(k * most, most)], out[k], out_sems.at[i, k]
            )
            copy.start()
            copies.append(copy)
    for copy in copies:
        copy.wait()


def attend(ids, refs, tokens, keys, values, owned, most):
    parts, _, part_tokens, width = tokens.shape
    nbr = keys[0].shape[1]
    distinct = ids.shape[1]
    groups = refs.shape[1]
    flat = refs.reshape(refs.shape[0], -1)
    pool = pltpu.VMEM((SIDE * most, nbr, width), BF16)
    total = pltpu.VMEM((distinct, nbr, width), F32)
    rows = pltpu.VMEM((GROUP, width), F32)
    table = pltpu.SMEM((distinct,), jnp.int32)
    reverse = pltpu.SMEM((SIDE * most,), jnp.int32)
    shapes = (jax.ShapeDtypeStruct((parts, part_tokens, width), BF16),) + chunk_shapes(
        most, nbr, width
    ) * 2
    out = pl.pallas_call(
        functools.partial(attend_body, groups, distinct, owned, most, 8),
        out_shape=tuple(pltpu.HBM(shape.shape, shape.dtype) for shape in shapes),
        in_specs=[SMEM, SMEM, VMEM] + [HBM] * 8,
        out_specs=(HBM,) * 9,
        scratch_shapes=[pool, pool, total, total, pltpu.VMEM((parts, part_tokens, width), BF16),
                        pool, pool, rows, rows, rows, table, table, reverse, reverse,
                        pltpu.SMEM((2 * SIDE,), jnp.int32),
                        pltpu.SemaphoreType.DMA((2, SIDE)), pltpu.SemaphoreType.DMA((2, SIDE)),
                        pltpu.SemaphoreType.DMA],
        compiler_params=pltpu.CompilerParams(vmem_limit_bytes=ATTEND_VMEM),
    )(ids, flat, tokens, *in_hbm(keys), *in_hbm(values))
    return (out[0], out[1:5], out[5:])


def collect_body(*refs):
    for i, out in enumerate(refs[8:]):
        own, *others = refs[4 * i : 4 * i + 4]
        for n in range(own.shape[0]):
            value = own[n]
            for other in others:
                value += other[n].astype(F32)
            out[n] = value.astype(BF16)


def collect(keys, values):
    out = jax.ShapeDtypeStruct(keys[0].shape, BF16)
    return pl.pallas_call(
        collect_body,
        out_shape=(out, out),
        in_specs=[VMEM] * 8,
        out_specs=(VMEM, VMEM),
        compiler_params=pltpu.CompilerParams(vmem_limit_bytes=COLLECT_VMEM),
    )(*keys, *values)


def on_device(queries, grad_out, neighbour_keys, neighbour_values, distinct_ids, group_refs):
    parts = lax.axis_size("ctx")
    owned = neighbour_keys.shape[0]
    most = SIDE * (owned // 2)
    take, add = tables(distinct_ids, owned, most)
    lines = gather_lines(neighbour_keys, neighbour_values)
    packed = pack_heads(queries[0], grad_out[0], parts)
    tokens = lax.all_to_all(packed, "ctx", split_axis=0, concat_axis=0, tiled=True)
    keys, values = select(take, *lines, most)
    keys, values = exchange_lines(((keys, "y", 1), (values, "x", 1)))
    back, keys, values = attend(distinct_ids, group_refs, tokens, keys, values, owned, most)
    keys, values = exchange_lines(((keys, "y", -1), (values, "x", -1)))
    back = lax.all_to_all(back, "ctx", split_axis=0, concat_axis=0, tiled=True)
    keys, values = list(keys), list(values)
    keys[0], values[3] = lax.optimization_barrier((keys[0], values[3]))
    keys = list(spread(add, keys, 0, owned))
    keys[0], values[0] = lax.optimization_barrier((keys[0], values[0]))
    values = spread(add, values, 1, owned)
    keys, values = exchange_lines(((keys, "x", 1), (values, "y", 1)))
    grad_queries = join_heads(back)[None]
    grad_queries, keys, values = lax.optimization_barrier((grad_queries, keys, values))
    grad_keys, grad_values = collect(keys, values)
    return (grad_queries, grad_keys, grad_values)


def solution(mesh):
    return jax.shard_map(
        on_device,
        mesh=mesh,
        in_specs=(
            P("dp", "ctx", None),
            P("dp", "ctx", None),
            P("dp", None, "ctx"),
            P("dp", None, "ctx"),
            P(),
            P(),
        ),
        out_specs=(P("dp", "ctx", None), P("dp", None, "ctx"), P("dp", None, "ctx")),
        check_vma=False,
    )
```

```python
import functools
import math

import jax
import jax.numpy as jnp
from jax import lax
from jax.experimental import pallas as pl
from jax.experimental.pallas import tpu as pltpu
from jax.sharding import PartitionSpec as P

DH = 128
GROUP = 64
BF16 = jnp.bfloat16
F32 = jnp.float32
HBM = pl.BlockSpec(memory_space=pltpu.MemorySpace.HBM)
VMEM = pl.BlockSpec(memory_space=pltpu.VMEM)
SMEM = pl.BlockSpec(memory_space=pltpu.SMEM)
SELECT_VMEM = 10 * 1024 * 1024
SPREAD_VMEM = 12 * 1024 * 1024
SPREAD_FLOPS = 200_000_000_000
ATTEND_VMEM = 20 * 1024 * 1024
COLLECT_VMEM = 8 * 1024 * 1024


SIDE = 4


def place(n, owned):
    owner = lax.div(n, owned)
    return (lax.div(owner, SIDE), lax.rem(owner, SIDE), lax.rem(n, owned))


def shift(value, axis, amount):
    pairs = []
    for y in range(SIDE):
        for x in range(SIDE):
            to = (y, (x + amount) % SIDE) if axis == "x" else ((y + amount) % SIDE, x)
            pairs.append((y * SIDE + x, to[0] * SIDE + to[1]))
    return lax.ppermute(value, "dp", pairs)


def exchange_lines(lines):
    parts = [list(chunks) for chunks, _, _ in lines]
    for n, distances in ((0, (2, 1, 3)), (1, (1, 3, 2))):
        chunks, axis, sign = lines[n]
        for distance in distances:
            value = chunks[distance]
            if n == 1 and distance == 2:
                value, parts[n][1] = lax.optimization_barrier((value, parts[n][1]))
            parts[n][distance] = shift(value, axis, sign * distance)
    return parts


def gather_lines(keys, values):
    return exchange_lines((((keys,) * SIDE, "x", -1), ((values,) * SIDE, "y", -1)))


def chunk_shapes(most, nbr, width, own_type=BF16):
    return tuple(
        jax.ShapeDtypeStruct((most, nbr, width), own_type if k == 0 else BF16) for k in range(SIDE)
    )


def pack_heads_body(parts, width, q_ref, g_ref, out_ref, held, in_sems, out_sems):
    arrivals = []
    for j in range(parts):
        for i, ref in enumerate((q_ref, g_ref)):
            copy = pltpu.make_async_copy(
                ref.at[:, pl.ds(j * width, width)], held.at[j, i], in_sems.at[j, i]
            )
            copy.start()
            arrivals.append(copy)
    departures = []
    for j in range(parts):
        for copy in arrivals[2 * j : 2 * j + 2]:
            copy.wait()
        departures.append(pltpu.make_async_copy(held.at[j], out_ref.at[j], out_sems.at[j]))
        departures[-1].start()
    for copy in departures:
        copy.wait()


def pack_heads(queries, grad_out, parts):
    tokens, features = queries.shape
    width = features // parts
    shape = (parts, 2, tokens, width)
    return pl.pallas_call(
        functools.partial(pack_heads_body, parts, width),
        out_shape=pltpu.HBM(shape, BF16),
        in_specs=[HBM, HBM],
        out_specs=HBM,
        scratch_shapes=[
            pltpu.VMEM(shape, BF16),
            pltpu.SemaphoreType.DMA((parts, 2)),
            pltpu.SemaphoreType.DMA((parts,)),
        ],
    )(queries, grad_out)


def join_heads_body(parts, width, in_ref, out_ref, sems):
    copies = [
        pltpu.make_async_copy(in_ref.at[j], out_ref.at[:, pl.ds(j * width, width)], sems.at[j])
        for j in range(parts)
    ]
    for copy in copies:
        copy.start()
    for copy in copies:
        copy.wait()


def join_heads(blocks):
    parts, tokens, width = blocks.shape
    return pl.pallas_call(
        functools.partial(join_heads_body, parts, width),
        out_shape=jax.ShapeDtypeStruct((tokens, parts * width), BF16),
        in_specs=[VMEM],
        out_specs=HBM,
        scratch_shapes=[pltpu.SemaphoreType.DMA((parts,))],
    )(blocks)


def matmul(a, b, contract):
    return lax.dot_general(a, b, ((contract[:1], contract[1:]), ((), ())), preferred_element_type=F32)


def block_diagonal(rows):
    zero = jnp.zeros((rows.shape[0], DH), BF16)
    return jnp.concatenate(
        [
            jnp.concatenate([rows[:, :DH], zero], axis=1),
            jnp.concatenate([zero, rows[:, DH:]], axis=1),
        ],
        axis=0,
    )


def tables_body(owned, most, ids_ref, take_ref, add_ref):
    me = lax.axis_index("dp")
    mine = (lax.div(me, SIDE), lax.rem(me, SIDE))
    distinct = ids_ref.shape[1]
    for across in range(2):
        for n in range(SIDE * most):
            take_ref[across, n] = 0
        for n in range(SIDE * owned * SIDE):
            add_ref[across, n] = -1
        for k in range(SIDE):
            other = lax.rem(mine[across] + k, SIDE)
            replica = other * SIDE + mine[1] if across == 0 else mine[0] * SIDE + other

            def step(j, count):
                where = place(ids_ref[replica, j], owned)
                found = where[across] == mine[across]

                @pl.when(found)
                def _():
                    distance = lax.rem(where[1 - across] - mine[1 - across] + SIDE, SIDE)
                    row = distance * owned + where[2]
                    take_ref[across, k * most + count] = row
                    add_ref[across, row * SIDE + k] = count

                return count + found.astype(jnp.int32)

            lax.fori_loop(0, distinct, step, jnp.int32(0))


def tables(ids, owned, most):
    return pl.pallas_call(
        functools.partial(tables_body, owned, most),
        out_shape=(
            jax.ShapeDtypeStruct((2, SIDE * most), jnp.int32),
            jax.ShapeDtypeStruct((2, SIDE * owned * SIDE), jnp.int32),
        ),
        in_specs=[SMEM],
        out_specs=(SMEM, SMEM),
    )(ids)


def select_body(take_ref, *refs):
    outs = (refs[8:12], refs[12:16])
    line, picked, in_sems, out_sems = refs[16:]
    owned = refs[0].shape[0]
    most = outs[0][0].shape[0]
    arrivals = [
        pltpu.make_async_copy(ref, line.at[pl.ds(n * owned, owned)], in_sems.at[n])
        for n, ref in enumerate(refs[:8])
    ]
    for copy in arrivals:
        copy.start()
    departures = []
    for across in range(2):
        for copy in arrivals[SIDE * across : SIDE * (across + 1)]:
            copy.wait()
        for k in (2, 1, 3, 0) if across == 0 else (1, 3, 2, 0):
            base = (SIDE * across + k) * most

            def pick(n, carry):
                picked[base + n] = line[SIDE * owned * across + take_ref[across, k * most + n]]
                return carry

            lax.fori_loop(0, most, pick, 0, unroll=4)
            copy = pltpu.make_async_copy(
                picked.at[pl.ds(base, most)], outs[across][k], out_sems.at[SIDE * across + k]
            )
            copy.start()
            departures.append(copy)
    for copy in departures:
        copy.wait()


def select(take, keys, values, most):
    owned, nbr, width = keys[0].shape
    out = pl.pallas_call(
        select_body,
        out_shape=tuple(
            pltpu.HBM(shape.shape, shape.dtype) for shape in chunk_shapes(most, nbr, width) * 2
        ),
        in_specs=[SMEM] + [HBM] * 8,
        out_specs=(HBM,) * 8,
        scratch_shapes=[
            pltpu.VMEM((2 * SIDE * owned, nbr, width), BF16),
            pltpu.VMEM((2 * SIDE * most, nbr, width), BF16),
            pltpu.SemaphoreType.DMA((2 * SIDE,)),
            pltpu.SemaphoreType.DMA((2 * SIDE,)),
        ],
        compiler_params=pltpu.CompilerParams(vmem_limit_bytes=SELECT_VMEM),
    )(take, *keys, *values)
    return (out[:4], out[4:])


def spread_body(across, add_ref, *refs):
    chunks, outs = refs[:4], refs[4:8]
    owned = outs[0].shape[0]

    def add(n, carry):
        for distance, out in enumerate(outs):
            value = jnp.zeros(out.shape[1:], F32)
            for k, chunk in enumerate(chunks):
                index = add_ref[across, (distance * owned + n) * SIDE + k]
                term = chunk[jnp.maximum(index, 0)].astype(F32)
                value += jnp.where(index >= 0, term, 0.0)
            out[n] = value.astype(out.dtype)
        return carry

    lax.fori_loop(0, owned, add, 0)


def in_hbm(values):
    return [pltpu.with_memory_space_constraint(v, pltpu.MemorySpace.HBM) for v in values]


def spread(add, chunks, across, owned):
    most, nbr, width = chunks[0].shape
    return pl.pallas_call(
        functools.partial(spread_body, across),
        out_shape=chunk_shapes(owned, nbr, width, F32),
        in_specs=[SMEM] + [VMEM] * 4,
        out_specs=(VMEM,) * 4,
        compiler_params=pltpu.CompilerParams(vmem_limit_bytes=SPREAD_VMEM),
        cost_estimate=pl.CostEstimate(
            flops=SPREAD_FLOPS, bytes_accessed=2 * 1024 * 1024, transcendentals=0
        ),
    )(add, *chunks)


def attend_body(
    groups, distinct, owned, most, unroll, ids_ref, refs_ref, tokens_ref, *refs
):
    key_parts, value_parts = refs[:4], refs[4:8]
    gq_out, key_out, value_out = refs[8], refs[9:13], refs[13:17]
    (keys, values, key_sum, value_sum, gq_ref, key_send, value_send, query_last, grad_last, held,
     key_rows, value_rows, key_back, value_back, counts, in_sems, out_sems, gq_sem) = refs[17:]
    scale = 1.0 / math.sqrt(DH)
    copies = [
        pltpu.make_async_copy(part, pool.at[pl.ds(k * most, most)], in_sems.at[i, k])
        for i, (parts, pool) in enumerate(((key_parts, keys), (value_parts, values)))
        for k, part in enumerate(parts)
    ]
    for copy in copies:
        copy.start()

    def clear(j, carry):
        key_sum[j] = jnp.zeros(key_sum.shape[1:], F32)
        value_sum[j] = jnp.zeros(value_sum.shape[1:], F32)
        return carry

    lax.fori_loop(0, distinct, clear, 0)
    width = gq_ref.shape[2]
    row = lax.broadcasted_iota(jnp.int32, (GROUP, width), 0)
    me = lax.axis_index("dp")
    mine = (me // SIDE, me % SIDE)
    for i in range(2 * SIDE):
        counts[i] = 0
    for n in range(SIDE * most):
        key_back[n] = -1
        value_back[n] = -1

    def rank(j, carry):
        where = place(ids_ref[me, j], owned)
        for i, (table, back_rows) in enumerate(
            ((key_rows, key_back), (value_rows, value_back))
        ):
            distance = (mine[i] - where[i] + SIDE) % SIDE
            count = counts[i * SIDE + distance]
            table[j] = distance * most + count
            back_rows[distance * most + count] = j
            counts[i * SIDE + distance] = count + 1
        return carry

    lax.fori_loop(0, distinct, rank, 0)

    def rolled(kind, block):
        part = tokens_ref[block // 2, kind, pl.ds((block % 2) * GROUP, GROUP), :]
        return pltpu.roll(part.astype(F32), 1, 0)

    held[...] = jnp.zeros_like(held)
    query_last[...] = rolled(0, 0)
    grad_last[...] = rolled(1, 0)
    for copy in copies:
        copy.wait()

    def shifted(kind, group, last):
        following = rolled(kind, jnp.minimum(group + 1, groups - 1))
        following = jnp.where(group + 1 < groups, following, 0.0)
        block = jnp.where(row == 0, last[...], following)
        last[...] = following
        return block_diagonal(block.astype(BF16))

    def steps(index, carry):
        batch = [index * unroll + u for u in range(unroll)]
        state = []
        for group in batch:
            query = shifted(0, group, query_last)
            grad = shifted(1, group, grad_last)
            pair = (refs_ref[me, 2 * group], refs_ref[me, 2 * group + 1])
            block_keys = [keys[key_rows[j]] for j in pair]
            scores = [matmul(k, query, (1, 1)) for k in block_keys]
            grads = [matmul(values[value_rows[j]], grad, (1, 1)) for j in pair]
            state.append((group, query, grad, pair, block_keys, scores, grads))
        lows = []
        for group, query, grad, pair, block_keys, scores, grads in state:
            top = jnp.maximum(*[jnp.max(s, axis=0, keepdims=True) for s in scores])
            weights = [jnp.exp2((s - top) * (scale * math.log2(math.e))) for s in scores]
            total = sum(jnp.sum(w, axis=0, keepdims=True) for w in weights)
            inverse = 1.0 / total
            weights = [w * inverse for w in weights]
            dots = sum(jnp.sum(w * g, axis=0, keepdims=True) for w, g in zip(weights, grads))
            grad_low = [(w * (g - dots)).astype(BF16) for w, g in zip(weights, grads)]
            lows.append(([w.astype(BF16) for w in weights], grad_low))
        for (group, query, grad, pair, block_keys, _, _), (weights_low, grad_low) in zip(state, lows):
            terms = [(matmul(w, grad, (1, 0)), matmul(g, query, (1, 0))) for w, g in zip(weights_low, grad_low)]
            both = sum(matmul(g, k, (0, 0)) for g, k in zip(grad_low, block_keys)) * scale
            back = jnp.concatenate([both[:GROUP, :DH], both[GROUP:, DH:]], axis=1)
            back = pltpu.roll(back, GROUP - 1, 0)
            for j, (value_term, key_term) in zip(pair, terms):
                value_sum[j] += value_term
                key_sum[j] += key_term
            gq_ref[group // 2, pl.ds((group % 2) * GROUP, GROUP), :] = jnp.where(
                row == GROUP - 1, back, held[...]
            ).astype(BF16)
            held[...] = back
        return carry

    lax.fori_loop(0, groups // unroll, steps, 0)
    copies = [pltpu.make_async_copy(gq_ref, gq_out, gq_sem)]
    copies[0].start()
    for k in (2, 1, 3, 0):
        for i, (send, total, back_rows, out, factor) in enumerate(
            ((key_send, key_sum, key_back, key_out, scale),
             (value_send, value_sum, value_back, value_out, 1.0))
        ):

            def give(n, carry):
                slot = k * most + n
                j = back_rows[slot]

                @pl.when(j >= 0)
                def _():
                    send[slot] = (total[jnp.maximum(j, 0)] * factor).astype(BF16)

                return carry

            lax.fori_loop(0, most, give, 0)
            copy = pltpu.make_async_copy(
                send.at[pl.ds(k * most, most)], out[k], out_sems.at[i, k]
            )
            copy.start()
            copies.append(copy)
    for copy in copies:
        copy.wait()


def attend(ids, refs, tokens, keys, values, owned, most):
    parts, _, part_tokens, width = tokens.shape
    nbr = keys[0].shape[1]
    distinct = ids.shape[1]
    groups = refs.shape[1]
    flat = refs.reshape(refs.shape[0], -1)
    pool = pltpu.VMEM((SIDE * most, nbr, width), BF16)
    total = pltpu.VMEM((distinct, nbr, width), F32)
    rows = pltpu.VMEM((GROUP, width), F32)
    table = pltpu.SMEM((distinct,), jnp.int32)
    reverse = pltpu.SMEM((SIDE * most,), jnp.int32)
    shapes = (jax.ShapeDtypeStruct((parts, part_tokens, width), BF16),) + chunk_shapes(
        most, nbr, width
    ) * 2
    out = pl.pallas_call(
        functools.partial(attend_body, groups, distinct, owned, most, 8),
        out_shape=tuple(pltpu.HBM(shape.shape, shape.dtype) for shape in shapes),
        in_specs=[SMEM, SMEM, VMEM] + [HBM] * 8,
        out_specs=(HBM,) * 9,
        scratch_shapes=[pool, pool, total, total, pltpu.VMEM((parts, part_tokens, width), BF16),
                        pool, pool, rows, rows, rows, table, table, reverse, reverse,
                        pltpu.SMEM((2 * SIDE,), jnp.int32),
                        pltpu.SemaphoreType.DMA((2, SIDE)), pltpu.SemaphoreType.DMA((2, SIDE)),
                        pltpu.SemaphoreType.DMA],
        compiler_params=pltpu.CompilerParams(vmem_limit_bytes=ATTEND_VMEM),
    )(ids, flat, tokens, *in_hbm(keys), *in_hbm(values))
    return (out[0], out[1:5], out[5:])


def collect_body(*refs):
    for i, out in enumerate(refs[8:]):
        own, *others = refs[4 * i : 4 * i + 4]
        for n in range(own.shape[0]):
            value = own[n]
            for other in others:
                value += other[n].astype(F32)
            out[n] = value.astype(BF16)


def collect(keys, values):
    out = jax.ShapeDtypeStruct(keys[0].shape, BF16)
    return pl.pallas_call(
        collect_body,
        out_shape=(out, out),
        in_specs=[VMEM] * 8,
        out_specs=(VMEM, VMEM),
        compiler_params=pltpu.CompilerParams(vmem_limit_bytes=COLLECT_VMEM),
    )(*keys, *values)


def on_device(queries, grad_out, neighbour_keys, neighbour_values, distinct_ids, group_refs):
    parts = lax.axis_size("ctx")
    owned = neighbour_keys.shape[0]
    most = SIDE * (owned // 2)
    take, add = tables(distinct_ids, owned, most)
    lines = gather_lines(neighbour_keys, neighbour_values)
    packed = pack_heads(queries[0], grad_out[0], parts)
    tokens = lax.all_to_all(packed, "ctx", split_axis=0, concat_axis=0, tiled=True)
    keys, values = select(take, *lines, most)
    keys, values = exchange_lines(((keys, "y", 1), (values, "x", 1)))
    back, keys, values = attend(distinct_ids, group_refs, tokens, keys, values, owned, most)
    keys, values = exchange_lines(((keys, "y", -1), (values, "x", -1)))
    back = lax.all_to_all(back, "ctx", split_axis=0, concat_axis=0, tiled=True)
    keys, values = list(keys), list(values)
    keys[0], values[3] = lax.optimization_barrier((keys[0], values[3]))
    keys = list(spread(add, keys, 0, owned))
    keys[0], values[0] = lax.optimization_barrier((keys[0], values[0]))
    values = spread(add, values, 1, owned)
    keys, values = exchange_lines(((keys, "x", 1), (values, "y", 1)))
    grad_queries = join_heads(back)[None]
    grad_queries, keys, values = lax.optimization_barrier((grad_queries, keys, values))
    grad_keys, grad_values = collect(keys, values)
    return (grad_queries, grad_keys, grad_values)


def solution(mesh):
    return jax.shard_map(
        on_device,
        mesh=mesh,
        in_specs=(
            P("dp", "ctx", None),
            P("dp", "ctx", None),
            P("dp", None, "ctx"),
            P("dp", None, "ctx"),
            P(),
            P(),
        ),
        out_specs=(P("dp", "ctx", None), P("dp", None, "ctx"), P("dp", None, "ctx")),
        check_vma=False,
    )
```

```python
import functools
import math

import jax
import jax.numpy as jnp
from jax import lax
from jax.experimental import pallas as pl
from jax.experimental.pallas import tpu as pltpu
from jax.sharding import PartitionSpec as P

DH = 128
GROUP = 64
BF16 = jnp.bfloat16
F32 = jnp.float32
HBM = pl.BlockSpec(memory_space=pltpu.MemorySpace.HBM)
VMEM = pl.BlockSpec(memory_space=pltpu.VMEM)
SMEM = pl.BlockSpec(memory_space=pltpu.SMEM)
SELECT_VMEM = 10 * 1024 * 1024
SPREAD_VMEM = 12 * 1024 * 1024
SPREAD_FLOPS = 200_000_000_000
ATTEND_VMEM = 20 * 1024 * 1024
COLLECT_VMEM = 8 * 1024 * 1024


SIDE = 4


def place(n, owned):
    owner = lax.div(n, owned)
    return (lax.div(owner, SIDE), lax.rem(owner, SIDE), lax.rem(n, owned))


def shift(value, axis, amount):
    pairs = []
    for y in range(SIDE):
        for x in range(SIDE):
            to = (y, (x + amount) % SIDE) if axis == "x" else ((y + amount) % SIDE, x)
            pairs.append((y * SIDE + x, to[0] * SIDE + to[1]))
    return lax.ppermute(value, "dp", pairs)


def exchange_lines(lines):
    parts = [list(chunks) for chunks, _, _ in lines]
    for n, distances in ((0, (2, 1, 3)), (1, (1, 3, 2))):
        chunks, axis, sign = lines[n]
        for distance in distances:
            value = chunks[distance]
            if n == 1 and distance == 2:
                value, parts[n][1] = lax.optimization_barrier((value, parts[n][1]))
            parts[n][distance] = shift(value, axis, sign * distance)
    return parts


def gather_lines(keys, values):
    return exchange_lines((((keys,) * SIDE, "x", -1), ((values,) * SIDE, "y", -1)))


def chunk_shapes(most, nbr, width, own_type=BF16):
    return tuple(
        jax.ShapeDtypeStruct((most, nbr, width), own_type if k == 0 else BF16) for k in range(SIDE)
    )


def pack_heads_body(parts, width, q_ref, g_ref, out_ref, held, in_sems, out_sems):
    arrivals = []
    for j in range(parts):
        for i, ref in enumerate((q_ref, g_ref)):
            copy = pltpu.make_async_copy(
                ref.at[:, pl.ds(j * width, width)], held.at[j, i], in_sems.at[j, i]
            )
            copy.start()
            arrivals.append(copy)
    departures = []
    for j in range(parts):
        for copy in arrivals[2 * j : 2 * j + 2]:
            copy.wait()
        departures.append(pltpu.make_async_copy(held.at[j], out_ref.at[j], out_sems.at[j]))
        departures[-1].start()
    for copy in departures:
        copy.wait()


def pack_heads(queries, grad_out, parts):
    tokens, features = queries.shape
    width = features // parts
    shape = (parts, 2, tokens, width)
    return pl.pallas_call(
        functools.partial(pack_heads_body, parts, width),
        out_shape=pltpu.HBM(shape, BF16),
        in_specs=[HBM, HBM],
        out_specs=HBM,
        scratch_shapes=[
            pltpu.VMEM(shape, BF16),
            pltpu.SemaphoreType.DMA((parts, 2)),
            pltpu.SemaphoreType.DMA((parts,)),
        ],
    )(queries, grad_out)


def join_heads_body(parts, width, in_ref, out_ref, sems):
    copies = [
        pltpu.make_async_copy(in_ref.at[j], out_ref.at[:, pl.ds(j * width, width)], sems.at[j])
        for j in range(parts)
    ]
    for copy in copies:
        copy.start()
    for copy in copies:
        copy.wait()


def join_heads(blocks):
    parts, tokens, width = blocks.shape
    return pl.pallas_call(
        functools.partial(join_heads_body, parts, width),
        out_shape=jax.ShapeDtypeStruct((tokens, parts * width), BF16),
        in_specs=[VMEM],
        out_specs=HBM,
        scratch_shapes=[pltpu.SemaphoreType.DMA((parts,))],
    )(blocks)


def matmul(a, b, contract):
    return lax.dot_general(a, b, ((contract[:1], contract[1:]), ((), ())), preferred_element_type=F32)


def block_diagonal(rows):
    zero = jnp.zeros((rows.shape[0], DH), BF16)
    return jnp.concatenate(
        [
            jnp.concatenate([rows[:, :DH], zero], axis=1),
            jnp.concatenate([zero, rows[:, DH:]], axis=1),
        ],
        axis=0,
    )


def tables_body(owned, most, ids_ref, take_ref, add_ref):
    me = lax.axis_index("dp")
    mine = (lax.div(me, SIDE), lax.rem(me, SIDE))
    distinct = ids_ref.shape[1]
    for across in range(2):
        for n in range(SIDE * most):
            take_ref[across, n] = 0
        for n in range(SIDE * owned * SIDE):
            add_ref[across, n] = -1
        for k in range(SIDE):
            other = lax.rem(mine[across] + k, SIDE)
            replica = other * SIDE + mine[1] if across == 0 else mine[0] * SIDE + other

            def step(j, count):
                where = place(ids_ref[replica, j], owned)
                found = where[across] == mine[across]

                @pl.when(found)
                def _():
                    distance = lax.rem(where[1 - across] - mine[1 - across] + SIDE, SIDE)
                    row = distance * owned + where[2]
                    take_ref[across, k * most + count] = row
                    add_ref[across, row * SIDE + k] = count

                return count + found.astype(jnp.int32)

            lax.fori_loop(0, distinct, step, jnp.int32(0))


def tables(ids, owned, most):
    return pl.pallas_call(
        functools.partial(tables_body, owned, most),
        out_shape=(
            jax.ShapeDtypeStruct((2, SIDE * most), jnp.int32),
            jax.ShapeDtypeStruct((2, SIDE * owned * SIDE), jnp.int32),
        ),
        in_specs=[SMEM],
        out_specs=(SMEM, SMEM),
    )(ids)


def select_body(take_ref, *refs):
    outs = (refs[8:12], refs[12:16])
    line, picked, in_sems, out_sems = refs[16:]
    owned = refs[0].shape[0]
    most = outs[0][0].shape[0]
    arrivals = [
        pltpu.make_async_copy(ref, line.at[pl.ds(n * owned, owned)], in_sems.at[n])
        for n, ref in enumerate(refs[:8])
    ]
    for copy in arrivals:
        copy.start()
    departures = []
    for across in range(2):
        for copy in arrivals[SIDE * across : SIDE * (across + 1)]:
            copy.wait()
        for k in (2, 1, 3, 0) if across == 0 else (1, 3, 2, 0):
            base = (SIDE * across + k) * most

            def pick(n, carry):
                picked[base + n] = line[SIDE * owned * across + take_ref[across, k * most + n]]
                return carry

            lax.fori_loop(0, most, pick, 0, unroll=4)
            copy = pltpu.make_async_copy(
                picked.at[pl.ds(base, most)], outs[across][k], out_sems.at[SIDE * across + k]
            )
            copy.start()
            departures.append(copy)
    for copy in departures:
        copy.wait()


def select(take, keys, values, most):
    owned, nbr, width = keys[0].shape
    out = pl.pallas_call(
        select_body,
        out_shape=tuple(
            pltpu.HBM(shape.shape, shape.dtype) for shape in chunk_shapes(most, nbr, width) * 2
        ),
        in_specs=[SMEM] + [HBM] * 8,
        out_specs=(HBM,) * 8,
        scratch_shapes=[
            pltpu.VMEM((2 * SIDE * owned, nbr, width), BF16),
            pltpu.VMEM((2 * SIDE * most, nbr, width), BF16),
            pltpu.SemaphoreType.DMA((2 * SIDE,)),
            pltpu.SemaphoreType.DMA((2 * SIDE,)),
        ],
        compiler_params=pltpu.CompilerParams(vmem_limit_bytes=SELECT_VMEM),
    )(take, *keys, *values)
    return (out[:4], out[4:])


def spread_body(across, add_ref, *refs):
    chunks, outs = refs[:4], refs[4:8]
    owned = outs[0].shape[0]

    def add(n, carry):
        for distance, out in enumerate(outs):
            value = jnp.zeros(out.shape[1:], F32)
            for k, chunk in enumerate(chunks):
                index = add_ref[across, (distance * owned + n) * SIDE + k]
                term = chunk[jnp.maximum(index, 0)].astype(F32)
                value += jnp.where(index >= 0, term, 0.0)
            out[n] = value.astype(out.dtype)
        return carry

    lax.fori_loop(0, owned, add, 0)


def in_hbm(values):
    return [pltpu.with_memory_space_constraint(v, pltpu.MemorySpace.HBM) for v in values]


def spread(add, chunks, across, owned):
    most, nbr, width = chunks[0].shape
    return pl.pallas_call(
        functools.partial(spread_body, across),
        out_shape=chunk_shapes(owned, nbr, width, F32),
        in_specs=[SMEM] + [VMEM] * 4,
        out_specs=(VMEM,) * 4,
        compiler_params=pltpu.CompilerParams(vmem_limit_bytes=SPREAD_VMEM),
        cost_estimate=pl.CostEstimate(
            flops=SPREAD_FLOPS, bytes_accessed=2 * 1024 * 1024, transcendentals=0
        ),
    )(add, *chunks)


def attend_body(
    groups, distinct, owned, most, unroll, ids_ref, refs_ref, tokens_ref, *refs
):
    key_parts, value_parts = refs[:4], refs[4:8]
    gq_out, key_out, value_out = refs[8], refs[9:13], refs[13:17]
    (keys, values, key_sum, value_sum, gq_ref, key_send, value_send, query_last, grad_last, held,
     key_rows, value_rows, key_back, value_back, counts, in_sems, out_sems, gq_sem) = refs[17:]
    scale = 1.0 / math.sqrt(DH)
    copies = [
        pltpu.make_async_copy(part, pool.at[pl.ds(k * most, most)], in_sems.at[i, k])
        for i, (parts, pool) in enumerate(((key_parts, keys), (value_parts, values)))
        for k, part in enumerate(parts)
    ]
    for copy in copies:
        copy.start()

    def clear(j, carry):
        key_sum[j] = jnp.zeros(key_sum.shape[1:], F32)
        value_sum[j] = jnp.zeros(value_sum.shape[1:], F32)
        return carry

    lax.fori_loop(0, distinct, clear, 0)
    width = gq_ref.shape[2]
    row = lax.broadcasted_iota(jnp.int32, (GROUP, width), 0)
    me = lax.axis_index("dp")
    mine = (me // SIDE, me % SIDE)
    for i in range(2 * SIDE):
        counts[i] = 0
    for n in range(SIDE * most):
        key_back[n] = -1
        value_back[n] = -1

    def rank(j, carry):
        where = place(ids_ref[me, j], owned)
        for i, (table, back_rows) in enumerate(
            ((key_rows, key_back), (value_rows, value_back))
        ):
            distance = (mine[i] - where[i] + SIDE) % SIDE
            count = counts[i * SIDE + distance]
            table[j] = distance * most + count
            back_rows[distance * most + count] = j
            counts[i * SIDE + distance] = count + 1
        return carry

    lax.fori_loop(0, distinct, rank, 0)

    def rolled(kind, block):
        part = tokens_ref[block // 2, kind, pl.ds((block % 2) * GROUP, GROUP), :]
        return pltpu.roll(part.astype(F32), 1, 0)

    held[...] = jnp.zeros_like(held)
    query_last[...] = rolled(0, 0)
    grad_last[...] = rolled(1, 0)
    for copy in copies:
        copy.wait()

    def shifted(kind, group, last):
        following = rolled(kind, jnp.minimum(group + 1, groups - 1))
        following = jnp.where(group + 1 < groups, following, 0.0)
        block = jnp.where(row == 0, last[...], following)
        last[...] = following
        return block_diagonal(block.astype(BF16))

    def steps(index, carry):
        batch = [index * unroll + u for u in range(unroll)]
        state = []
        for group in batch:
            query = shifted(0, group, query_last)
            grad = shifted(1, group, grad_last)
            pair = (refs_ref[me, 2 * group], refs_ref[me, 2 * group + 1])
            block_keys = [keys[key_rows[j]] for j in pair]
            scores = [matmul(k, query, (1, 1)) for k in block_keys]
            grads = [matmul(values[value_rows[j]], grad, (1, 1)) for j in pair]
            state.append((group, query, grad, pair, block_keys, scores, grads))
        lows = []
        for group, query, grad, pair, block_keys, scores, grads in state:
            top = jnp.maximum(*[jnp.max(s, axis=0, keepdims=True) for s in scores])
            weights = [jnp.exp2((s - top) * (scale * math.log2(math.e))) for s in scores]
            total = sum(jnp.sum(w, axis=0, keepdims=True) for w in weights)
            inverse = 1.0 / total
            weights = [w * inverse for w in weights]
            dots = sum(jnp.sum(w * g, axis=0, keepdims=True) for w, g in zip(weights, grads))
            grad_low = [(w * (g - dots)).astype(BF16) for w, g in zip(weights, grads)]
            lows.append(([w.astype(BF16) for w in weights], grad_low))
        for (group, query, grad, pair, block_keys, _, _), (weights_low, grad_low) in zip(state, lows):
            terms = [(matmul(w, grad, (1, 0)), matmul(g, query, (1, 0))) for w, g in zip(weights_low, grad_low)]
            both = sum(matmul(g, k, (0, 0)) for g, k in zip(grad_low, block_keys)) * scale
            back = jnp.concatenate([both[:GROUP, :DH], both[GROUP:, DH:]], axis=1)
            back = pltpu.roll(back, GROUP - 1, 0)
            for j, (value_term, key_term) in zip(pair, terms):
                value_sum[j] += value_term
                key_sum[j] += key_term
            gq_ref[group // 2, pl.ds((group % 2) * GROUP, GROUP), :] = jnp.where(
                row == GROUP - 1, back, held[...]
            ).astype(BF16)
            held[...] = back
        return carry

    lax.fori_loop(0, groups // unroll, steps, 0)
    copies = [pltpu.make_async_copy(gq_ref, gq_out, gq_sem)]
    copies[0].start()
    for k in (2, 1, 3, 0):
        for i, (send, total, back_rows, out, factor) in enumerate(
            ((key_send, key_sum, key_back, key_out, scale),
             (value_send, value_sum, value_back, value_out, 1.0))
        ):

            def give(n, carry):
                slot = k * most + n
                j = back_rows[slot]

                @pl.when(j >= 0)
                def _():
                    send[slot] = (total[jnp.maximum(j, 0)] * factor).astype(BF16)

                return carry

            lax.fori_loop(0, most, give, 0)
            copy = pltpu.make_async_copy(
                send.at[pl.ds(k * most, most)], out[k], out_sems.at[i, k]
            )
            copy.start()
            copies.append(copy)
    for copy in copies:
        copy.wait()


def attend(ids, refs, tokens, keys, values, owned, most):
    parts, _, part_tokens, width = tokens.shape
    nbr = keys[0].shape[1]
    distinct = ids.shape[1]
    groups = refs.shape[1]
    flat = refs.reshape(refs.shape[0], -1)
    pool = pltpu.VMEM((SIDE * most, nbr, width), BF16)
    total = pltpu.VMEM((distinct, nbr, width), F32)
    rows = pltpu.VMEM((GROUP, width), F32)
    table = pltpu.SMEM((distinct,), jnp.int32)
    reverse = pltpu.SMEM((SIDE * most,), jnp.int32)
    shapes = (jax.ShapeDtypeStruct((parts, part_tokens, width), BF16),) + chunk_shapes(
        most, nbr, width
    ) * 2
    out = pl.pallas_call(
        functools.partial(attend_body, groups, distinct, owned, most, 16),
        out_shape=tuple(pltpu.HBM(shape.shape, shape.dtype) for shape in shapes),
        in_specs=[SMEM, SMEM, VMEM] + [HBM] * 8,
        out_specs=(HBM,) * 9,
        scratch_shapes=[pool, pool, total, total, pltpu.VMEM((parts, part_tokens, width), BF16),
                        pool, pool, rows, rows, rows, table, table, reverse, reverse,
                        pltpu.SMEM((2 * SIDE,), jnp.int32),
                        pltpu.SemaphoreType.DMA((2, SIDE)), pltpu.SemaphoreType.DMA((2, SIDE)),
                        pltpu.SemaphoreType.DMA],
        compiler_params=pltpu.CompilerParams(vmem_limit_bytes=ATTEND_VMEM),
    )(ids, flat, tokens, *in_hbm(keys), *in_hbm(values))
    return (out[0], out[1:5], out[5:])


def collect_body(*refs):
    for i, out in enumerate(refs[8:]):
        own, *others = refs[4 * i : 4 * i + 4]
        for n in range(own.shape[0]):
            value = own[n]
            for other in others:
                value += other[n].astype(F32)
            out[n] = value.astype(BF16)


def collect(keys, values):
    out = jax.ShapeDtypeStruct(keys[0].shape, BF16)
    return pl.pallas_call(
        collect_body,
        out_shape=(out, out),
        in_specs=[VMEM] * 8,
        out_specs=(VMEM, VMEM),
        compiler_params=pltpu.CompilerParams(vmem_limit_bytes=COLLECT_VMEM),
    )(*keys, *values)


def on_device(queries, grad_out, neighbour_keys, neighbour_values, distinct_ids, group_refs):
    parts = lax.axis_size("ctx")
    owned = neighbour_keys.shape[0]
    most = SIDE * (owned // 2)
    take, add = tables(distinct_ids, owned, most)
    lines = gather_lines(neighbour_keys, neighbour_values)
    packed = pack_heads(queries[0], grad_out[0], parts)
    tokens = lax.all_to_all(packed, "ctx", split_axis=0, concat_axis=0, tiled=True)
    keys, values = select(take, *lines, most)
    keys, values = exchange_lines(((keys, "y", 1), (values, "x", 1)))
    back, keys, values = attend(distinct_ids, group_refs, tokens, keys, values, owned, most)
    keys, values = exchange_lines(((keys, "y", -1), (values, "x", -1)))
    back = lax.all_to_all(back, "ctx", split_axis=0, concat_axis=0, tiled=True)
    keys, values = list(keys), list(values)
    keys[0], values[3] = lax.optimization_barrier((keys[0], values[3]))
    keys = list(spread(add, keys, 0, owned))
    keys[0], values[0] = lax.optimization_barrier((keys[0], values[0]))
    values = spread(add, values, 1, owned)
    keys, values = exchange_lines(((keys, "x", 1), (values, "y", 1)))
    grad_queries = join_heads(back)[None]
    grad_queries, keys, values = lax.optimization_barrier((grad_queries, keys, values))
    grad_keys, grad_values = collect(keys, values)
    return (grad_queries, grad_keys, grad_values)


def solution(mesh):
    return jax.shard_map(
        on_device,
        mesh=mesh,
        in_specs=(
            P("dp", "ctx", None),
            P("dp", "ctx", None),
            P("dp", None, "ctx"),
            P("dp", None, "ctx"),
            P(),
            P(),
        ),
        out_specs=(P("dp", "ctx", None), P("dp", None, "ctx"), P("dp", None, "ctx")),
        check_vma=False,
    )
```
